128 devices in a mesh: dp: 16 (over x_lo, z, core), tensor: 8 (over y, x_hi).
Axes of the slice: x: 4 (x_hi: 2, x_lo: 2; x = x_hi * 2 + x_lo), y: 4, z: 4, core: 2. Of those that a mesh axis runs over, the one named last changes fastest.
Arguments:
- tokens: bfloat16 [16384, 1024], P('dp'), may hold values from -6 to 6
- segment_ids: int32 [16384], P('dp'), may hold values from 0 to 7, as said below
- attn_gain: float32 [1024], replicated, may hold values from 0.25 to 1.75
- w_query: bfloat16 [1024, 1024], P(None, 'tensor'), may hold values from -0.1875 to 0.1875
- w_key: bfloat16 [1024, 512], P(None, 'tensor'), may hold values from -0.1875 to 0.1875
- w_value: bfloat16 [1024, 512], P(None, 'tensor'), may hold values from -0.1875 to 0.1875
- query_gain: float32 [64], replicated, may hold values from 0.25 to 1.75
- key_gain: float32 [64], replicated, may hold values from 0.25 to 1.75
- w_out: bfloat16 [1024, 1024], P('tensor'), may hold values from -1.5 to 1.5
- ffn_gain: float32 [1024], replicated, may hold values from 0.25 to 1.75
- w_gate: bfloat16 [1024, 4608], P(None, 'tensor'), may hold values from -0.1875 to 0.1875
- w_up: bfloat16 [1024, 4608], P(None, 'tensor'), may hold values from -0.1875 to 0.1875
- w_down: bfloat16 [4608, 1024], P('tensor'), may hold values from -0.1875 to 0.1875
- cotangent: bfloat16 [16384, 1024], P('dp'), may hold values from -6 to 6
Outputs:
- output: bfloat16 [16384, 1024], P('dp')
- input_grad: float32 [16384, 1024], P('dp')
- attn_gain_grad: float32 [1024], replicated
- w_query_grad: float32 [1024, 1024], P(None, 'tensor')
- w_key_grad: float32 [1024, 512], P(None, 'tensor')
- w_value_grad: float32 [1024, 512], P(None, 'tensor')
- query_gain_grad: float32 [64], replicated
- key_gain_grad: float32 [64], replicated
- w_out_grad: float32 [1024, 1024], P('tensor')
- ffn_gain_grad: float32 [1024], replicated
- w_gate_grad: float32 [1024, 4608], P(None, 'tensor')
- w_up_grad: float32 [1024, 4608], P(None, 'tensor')
- w_down_grad: float32 [4608, 1024], P('tensor')
The draws below stay inside these ranges and needn't reach their ends.
Inputs may be any that keep to these rules, and one draw needn't show every extreme that they name: `segment_ids`: within each index of dp's 1024 tokens the ids start at 0 and never fall; a sequence is a run of equal ids and never crosses devices.
All inputs are finite; a program needn't handle non-finite values.
Results may differ from the reference program's by a relative error of at most 0.014.
The reference program's roundings to bfloat16 on the way count: a program that leaves them out, or rounds other values in their place, can miss the bound.
Values sent between devices are 32-bit elements; how exact they have to be, the bound alone decides.
No kernel may reach another device: no remote copies, remote signals or barrier semaphores. Data moves between devices by JAX's collectives and lax.ppermute only.
A program may use at most 128 MiB of HBM per device.

```python
import math
import jax
import jax.numpy as jnp
from jax import lax

D = 1024
H = 16
KV = 8
HD = 64
FF = 4608
TOK_DEV = 1024
TOKENS = 16384
N_DP = 16


def draw_segment_ids(key, part):
    subkeys = jax.random.split(key, 4)
    cut_points = jax.random.randint(subkeys[0], (N_DP, 7), 1, TOK_DEV)
    cut_count = jax.random.randint(subkeys[1], (N_DP,), 1, 8)
    whole_row = jax.random.randint(subkeys[2], (), 0, N_DP)
    busy_row = (whole_row + 1 + jax.random.randint(subkeys[3], (), 0, N_DP - 1)) % N_DP
    row_index = jnp.arange(N_DP)
    cut_count = jnp.where(row_index == whole_row, 0, jnp.where(row_index == busy_row, 7, cut_count))
    slot_index = jnp.arange(7)
    kept = slot_index[None, :] < cut_count[:, None]
    places = jnp.arange(TOK_DEV)
    passed = kept[:, :, None] & (cut_points[:, :, None] <= places[None, None, :])
    segment = jnp.sum(passed.astype(jnp.int32), axis=1)
    return segment.reshape(N_DP * TOK_DEV).astype(jnp.int32)


def steps_of(own_key, dims, cuts, smallest, high):
    def one(axis_at, shards_of):
        heights = jax.random.uniform(jax.random.fold_in(jax.random.fold_in(own_key, 6), axis_at), (shards_of,), jnp.float32, smallest / len(cuts), high / len(cuts))
        return jnp.repeat(jnp.exp(heights), dims[axis_at] // shards_of).reshape((-1,) + (1,) * (len(dims) - axis_at - 1))

    factor_of = one(*cuts[0])
    for cut in cuts[1:]:
        factor_of = factor_of * one(*cut)
    return factor_of


def noise(rng, dims, width, most, cuts=(), held_as=jnp.bfloat16):
    result = jax.random.normal(rng, dims, jnp.float32) * width
    if len(cuts) > 0:
        result = steps_of(rng, dims, cuts, -0.22, 0.18) * result
    return jnp.clip(result, min=-most, max=most).astype(held_as)


def setup_inputs(seed: int = 0) -> dict:
    streams_of = jax.random.split(jax.random.key(seed), 15)
    tokens = noise(streams_of[0], (TOKENS, D), 1.0, 6.0, ((0, 16),))
    segment_ids = draw_segment_ids(jax.random.fold_in(streams_of[14], 71), 0)
    attn_gain = jnp.clip(1.0 + 0.15 * jax.random.normal(streams_of[2], (D,), jnp.float32), 0.25, 1.75)
    w_query = noise(streams_of[3], (D, H * HD), D ** -0.5, 0.1875, ((1, 8),))
    w_key = noise(streams_of[4], (D, KV * HD), D ** -0.5, 0.1875, ((1, 8),))
    w_value = noise(streams_of[5], (D, KV * HD), D ** -0.5, 0.1875, ((1, 8),))
    query_gain = jnp.clip(1.0 + 0.15 * jax.random.normal(streams_of[6], (HD,), jnp.float32), 0.25, 1.75)
    key_gain = jnp.clip(1.0 + 0.15 * jax.random.normal(streams_of[7], (HD,), jnp.float32), 0.25, 1.75)
    w_out = noise(streams_of[8], (H * HD, D), (HD // 4) ** -0.5, 1.5, ((0, 8),))
    ffn_gain = jnp.clip(1.0 + 0.15 * jax.random.normal(streams_of[9], (D,), jnp.float32), 0.25, 1.75)
    w_gate = noise(streams_of[10], (D, FF), D ** -0.5, 0.1875, ((1, 8),))
    w_up = noise(streams_of[11], (D, FF), D ** -0.5, 0.1875, ((1, 8),))
    w_down = noise(streams_of[12], (FF, D), (FF // 4) ** -0.5, 0.1875, ((0, 8),))
    cotangent = noise(streams_of[13], (TOKENS, D), 1.0, 6.0, ((0, 16),))
    return dict(tokens=tokens, segment_ids=segment_ids, attn_gain=attn_gain, w_query=w_query, w_key=w_key, w_value=w_value, query_gain=query_gain, key_gain=key_gain, w_out=w_out, ffn_gain=ffn_gain, w_gate=w_gate, w_up=w_up, w_down=w_down, cotangent=cotangent)


EPS = 1e-05
THETA = 1000000.0

def outer(first_op, second_op):
    return lax.dot_general(first_op, second_op, (((0,), (0,)), ((), ())), preferred_element_type=jnp.float32)

def inner(first_op, second_op):
    return lax.dot_general(first_op, second_op, (((1,), (1,)), ((), ())), preferred_element_type=jnp.float32)

def rms_scale(values):
    return lax.rsqrt(lax.optimization_barrier(jnp.mean(values * values, axis=-1, keepdims=True)) + EPS)

def rms_back(upstream, values, inv_rms, gain_vec):
    normed = values * inv_rms
    weighted = upstream * gain_vec
    return inv_rms * (weighted - normed * lax.optimization_barrier(jnp.mean(weighted * normed, axis=-1, keepdims=True)))

def seq_layout(segment):
    length = segment.shape[0]
    ordinal = jnp.arange(length, dtype=jnp.int32)
    same_seq = segment[:, None] == segment[None, :]
    places = lax.optimization_barrier(jnp.sum((same_seq & (ordinal[None, :] < ordinal[:, None])).astype(jnp.int32), axis=1))
    allowed = same_seq & (ordinal[None, :] <= ordinal[:, None])
    return (places, allowed)

def rope_tables(places, head_size):
    frequency = jnp.exp(jnp.arange(head_size // 2, dtype=jnp.float32) * (-2.0 * math.log(THETA) / head_size))
    angles = places.astype(jnp.float32)[:, None] * frequency[None, :]
    angles = jnp.concatenate([angles, angles], axis=1)
    return (jnp.cos(angles), jnp.sin(angles))

def rotate(values, cosine, sine_table):
    half = values.shape[-1] // 2
    turned = jnp.concatenate([-values[..., half:], values[..., :half]], axis=-1)
    return values * cosine[:, None, :] + turned * sine_table[:, None, :]

def unrotate(incoming, cosine, sine_table):
    half = incoming.shape[-1] // 2
    scaled = incoming * sine_table[:, None, :]
    swapped = jnp.concatenate([scaled[..., half:], -scaled[..., :half]], axis=-1)
    return incoming * cosine[:, None, :] + swapped

def score_table(q_rot, k_rot, allowed, factor):
    raw = jnp.einsum('ikgd,jkd->kgij', q_rot.astype(jnp.float32), k_rot.astype(jnp.float32)) * factor
    return jnp.where(allowed[None, None], raw, -1e+30)

def layer(tok_rows, seg_rows, cot_rows, attn_gain, w_query, w_key, w_value, query_gain, key_gain, w_out, ffn_gain, w_gate, w_up, w_down):
    length = tok_rows.shape[0]
    groups = H // KV
    factor = 1.0 / math.sqrt(HD)
    places, allowed = seq_layout(seg_rows)
    cosine, sine_table = rope_tables(places, HD)
    tokens_wide = tok_rows.astype(jnp.float32)
    scale_one = rms_scale(tokens_wide)
    normed_one = (tokens_wide * scale_one * attn_gain).astype(jnp.bfloat16)
    q_raw = jnp.dot(normed_one, w_query, preferred_element_type=jnp.float32).reshape(length, H, HD)
    k_raw = jnp.dot(normed_one, w_key, preferred_element_type=jnp.float32).reshape(length, KV, HD)
    v_half = jnp.dot(normed_one, w_value, preferred_element_type=jnp.float32).astype(jnp.bfloat16).reshape(length, KV, HD)
    q_scale = rms_scale(q_raw)
    k_scale = rms_scale(k_raw)
    q_hat = q_raw * q_scale
    k_hat = k_raw * k_scale
    q_rot = rotate(q_hat * query_gain, cosine, sine_table).astype(jnp.bfloat16).reshape(length, KV, groups, HD)
    k_rot = rotate(k_hat * key_gain, cosine, sine_table).astype(jnp.bfloat16)
    scores = score_table(q_rot, k_rot, allowed, factor)
    row_peak = lax.optimization_barrier(jnp.max(scores, axis=-1, keepdims=True))
    log_total = row_peak + jnp.log(lax.optimization_barrier(jnp.sum(jnp.exp(scores - row_peak), axis=-1, keepdims=True)))
    attn_probs = jnp.exp(scores - log_total).astype(jnp.bfloat16)
    attn_mixed = jnp.einsum('kgij,jkd->ikgd', attn_probs.astype(jnp.float32), v_half.astype(jnp.float32))
    attn_mixed = attn_mixed.reshape(length, H * HD).astype(jnp.bfloat16)
    residual = tokens_wide + jnp.dot(attn_mixed, w_out, preferred_element_type=jnp.float32)
    scale_two = rms_scale(residual)
    normed_two = (residual * scale_two * ffn_gain).astype(jnp.bfloat16)
    gate_proj = jnp.dot(normed_two, w_gate, preferred_element_type=jnp.float32)
    up_proj = jnp.dot(normed_two, w_up, preferred_element_type=jnp.float32)
    gate_sigmoid = jax.nn.sigmoid(gate_proj)
    hidden = (gate_proj * gate_sigmoid * up_proj).astype(jnp.bfloat16)
    output = (residual + jnp.dot(hidden, w_down, preferred_element_type=jnp.float32)).astype(jnp.bfloat16)
    down_grad = outer(hidden, cot_rows)
    hidden_grad = inner(cot_rows, w_down)
    gate_grad = (hidden_grad * up_proj * gate_sigmoid * (1.0 + gate_proj * (1.0 - gate_sigmoid))).astype(jnp.bfloat16)
    up_grad = (hidden_grad * gate_proj * gate_sigmoid).astype(jnp.bfloat16)
    gate_w_grad = outer(normed_two, gate_grad)
    up_w_grad = outer(normed_two, up_grad)
    normed_two_grad = inner(gate_grad, w_gate) + inner(up_grad, w_up)
    ffn_grad = lax.optimization_barrier(jnp.sum(normed_two_grad * residual * scale_two, axis=0))
    residual_grad = cot_rows.astype(jnp.float32) + rms_back(normed_two_grad, residual, scale_two, ffn_gain)
    residual_half = residual_grad.astype(jnp.bfloat16)
    out_w_grad = outer(attn_mixed, residual_half)
    mixed_grad = inner(residual_half, w_out).astype(jnp.bfloat16).reshape(length, KV, groups, HD)
    attn_full = jnp.exp(score_table(q_rot, k_rot, allowed, factor) - log_total)
    probs_half = attn_full.astype(jnp.bfloat16)
    value_grad = jnp.einsum('kgij,ikgd->jkd', probs_half.astype(jnp.float32), mixed_grad.astype(jnp.float32)).astype(jnp.bfloat16)
    prob_grad = jnp.einsum('ikgd,jkd->kgij', mixed_grad.astype(jnp.float32), v_half.astype(jnp.float32))
    row_delta = lax.optimization_barrier(jnp.sum(attn_full * prob_grad, axis=-1, keepdims=True))
    score_grad = (attn_full * (prob_grad - row_delta) * factor).astype(jnp.bfloat16)
    q_rot_grad = jnp.einsum('kgij,jkd->ikgd', score_grad.astype(jnp.float32), k_rot.astype(jnp.float32)).reshape(length, H, HD)
    k_rot_grad = jnp.einsum('kgij,ikgd->jkd', score_grad.astype(jnp.float32), q_rot.astype(jnp.float32))
    q_norm_grad = unrotate(q_rot_grad, cosine, sine_table)
    k_norm_grad = unrotate(k_rot_grad, cosine, sine_table)
    qgain_grad = lax.optimization_barrier(jnp.sum(q_norm_grad * q_hat, axis=(0, 1)))
    kgain_grad = lax.optimization_barrier(jnp.sum(k_norm_grad * k_hat, axis=(0, 1)))
    q_grad = rms_back(q_norm_grad, q_raw, q_scale, query_gain).astype(jnp.bfloat16).reshape(length, H * HD)
    k_grad = rms_back(k_norm_grad, k_raw, k_scale, key_gain).astype(jnp.bfloat16).reshape(length, KV * HD)
    v_grad = value_grad.reshape(length, KV * HD)
    query_w_grad = outer(normed_one, q_grad)
    key_w_grad = outer(normed_one, k_grad)
    value_w_grad = outer(normed_one, v_grad)
    normed_one_grad = inner(q_grad, w_query) + inner(k_grad, w_key) + inner(v_grad, w_value)
    attn_grad = lax.optimization_barrier(jnp.sum(normed_one_grad * tokens_wide * scale_one, axis=0))
    input_grad = residual_grad + rms_back(normed_one_grad, tokens_wide, scale_one, attn_gain)
    grads = (attn_grad, query_w_grad, key_w_grad, value_w_grad, qgain_grad, kgain_grad, out_w_grad, ffn_grad, gate_w_grad, up_w_grad, down_grad)
    return (output, input_grad, grads)

def reference(tokens, segment_ids, attn_gain, w_query, w_key, w_value, query_gain, key_gain, w_out, ffn_gain, w_gate, w_up, w_down, cotangent):
    params = (attn_gain, w_query, w_key, w_value, query_gain, key_gain, w_out, ffn_gain, w_gate, w_up, w_down)
    tok_blocks = tokens.reshape(N_DP, TOK_DEV, D)
    seg_blocks = segment_ids.reshape(N_DP, TOK_DEV)
    cot_blocks = cotangent.reshape(N_DP, TOK_DEV, D)

    def one_rank(totals, blocks):
        tok_rows, seg_rows, cot_rows = blocks
        output, input_grad, grads = layer(tok_rows, seg_rows, cot_rows, *params)
        return (jax.tree.map(jnp.add, totals, grads), (output, input_grad))
    start_totals = jax.tree.map(lambda weight: jnp.zeros(weight.shape, jnp.float32), params)
    totals, (outputs, input_grads) = lax.scan(one_rank, start_totals, (tok_blocks, seg_blocks, cot_blocks))
    return (outputs.reshape(TOKENS, D), input_grads.reshape(TOKENS, D), totals[0], totals[1], totals[2], totals[3], totals[4], totals[5], totals[6], totals[7], totals[8], totals[9], totals[10])
```

```python
import math

import jax
import jax.numpy as jnp
from jax import lax
from jax.sharding import PartitionSpec as P

EPS = 1e-05
THETA = 1000000.0
TENSOR = ("ty", "tx")


def outer(first_op, second_op):
    return lax.dot_general(
        first_op, second_op, (((0,), (0,)), ((), ())), preferred_element_type=jnp.float32
    )


def inner(first_op, second_op):
    return lax.dot_general(
        first_op, second_op, (((1,), (1,)), ((), ())), preferred_element_type=jnp.float32
    )


def rms_scale(values):
    return lax.rsqrt(jnp.mean(values * values, axis=-1, keepdims=True) + EPS)


def rms_back(upstream, values, inv_rms, gain_vec):
    normed = values * inv_rms
    weighted = upstream * gain_vec
    return inv_rms * (weighted - normed * jnp.mean(weighted * normed, axis=-1, keepdims=True))


def seq_layout(segment):
    length = segment.shape[0]
    ordinal = jnp.arange(length, dtype=jnp.int32)
    same_seq = segment[:, None] == segment[None, :]
    places = jnp.sum((same_seq & (ordinal[None, :] < ordinal[:, None])).astype(jnp.int32), axis=1)
    allowed = same_seq & (ordinal[None, :] <= ordinal[:, None])
    return (places, allowed)


def rope_tables(places, head_size):
    frequency = jnp.exp(
        jnp.arange(head_size // 2, dtype=jnp.float32) * (-2.0 * math.log(THETA) / head_size)
    )
    angles = places.astype(jnp.float32)[:, None] * frequency[None, :]
    angles = jnp.concatenate([angles, angles], axis=1)
    return (jnp.cos(angles), jnp.sin(angles))


def rotate(values, cosine, sine_table):
    half = values.shape[-1] // 2
    turned = jnp.concatenate([-values[..., half:], values[..., :half]], axis=-1)
    return values * cosine[:, None, :] + turned * sine_table[:, None, :]


def unrotate(incoming, cosine, sine_table):
    half = incoming.shape[-1] // 2
    scaled = incoming * sine_table[:, None, :]
    swapped = jnp.concatenate([scaled[..., half:], -scaled[..., :half]], axis=-1)
    return incoming * cosine[:, None, :] + swapped


def score_table(q_rot, k_rot, allowed, factor):
    raw = jnp.einsum("ikgd,jkd->kgij", q_rot, k_rot, preferred_element_type=jnp.float32) * factor
    return jnp.where(allowed[None, None], raw, -1e30)


def ring(size, shift):
    return [(i, (i + shift) % size) for i in range(size)]


def tensor_sum(values, extra=None):
    rows, cols = values.shape
    ny = lax.axis_size("ty")
    nx = lax.axis_size("tx")
    y = lax.axis_index("ty")
    h = lax.axis_index("tx")
    leaf = rows // (2 * ny * nx)
    parts = values.reshape(2, ny, nx, leaf, cols)
    pairs = ring(nx, 1)
    total = extra
    accs = []
    for way, shift in ((0, 1), (1, -1)):
        chunks = parts[way]
        acc = lax.dynamic_index_in_dim(chunks, (y - shift) % ny, 0, keepdims=False)
        passing = extra
        for step in range(1, ny):
            if way == 0 and extra is not None:
                acc, passing = lax.ppermute((acc, passing), "ty", ring(ny, shift))
                total = total + passing
            else:
                acc = lax.ppermute(acc, "ty", ring(ny, shift))
            acc = acc + lax.dynamic_index_in_dim(chunks, (y - shift * (1 + step)) % ny, 0, keepdims=False)
        accs.append(acc)
    acc = jnp.stack(accs)
    keep = lax.dynamic_index_in_dim(acc, h, 1, keepdims=False)
    send = lax.dynamic_index_in_dim(acc, (h + 1) % nx, 1, keepdims=False)
    if extra is not None:
        got, got_total = lax.ppermute((send, total), "tx", pairs)
        total = total + got_total
    else:
        got = lax.ppermute(send, "tx", pairs)
    mine = keep + got
    other = lax.ppermute(mine, "tx", pairs)
    both = jnp.where(h == 0, jnp.stack([mine, other], 1), jnp.stack([other, mine], 1))
    outs = []
    for way, shift in ((0, 1), (1, -1)):
        cur = both[way]
        gathered = jnp.zeros((ny,) + cur.shape, values.dtype)
        gathered = lax.dynamic_update_index_in_dim(gathered, cur, y, 0)
        for step in range(1, ny):
            cur = lax.ppermute(cur, "ty", ring(ny, shift))
            gathered = lax.dynamic_update_index_in_dim(gathered, cur, (y - shift * step) % ny, 0)
        outs.append(gathered)
    result = jnp.stack(outs).reshape(rows, cols)
    if extra is None:
        return result
    return result, total


def per_device(
    tokens,
    segment_ids,
    attn_gain,
    w_query,
    w_key,
    w_value,
    query_gain,
    key_gain,
    w_out,
    ffn_gain,
    w_gate,
    w_up,
    w_down,
    cotangent,
):
    length = tokens.shape[0]
    head_size = query_gain.shape[0]
    q_heads = w_query.shape[1] // head_size
    kv_heads = w_key.shape[1] // head_size
    groups = q_heads // kv_heads
    factor = 1.0 / math.sqrt(head_size)
    places, allowed = seq_layout(segment_ids)
    cosine, sine_table = rope_tables(places, head_size)
    tokens_wide = tokens.astype(jnp.float32)
    scale_one = rms_scale(tokens_wide)
    normed_one = (tokens_wide * scale_one * attn_gain).astype(jnp.bfloat16)
    q_raw = jnp.dot(normed_one, w_query, preferred_element_type=jnp.float32).reshape(
        length, q_heads, head_size
    )
    k_raw = jnp.dot(normed_one, w_key, preferred_element_type=jnp.float32).reshape(
        length, kv_heads, head_size
    )
    v_half = (
        jnp.dot(normed_one, w_value, preferred_element_type=jnp.float32)
        .astype(jnp.bfloat16)
        .reshape(length, kv_heads, head_size)
    )
    q_scale = rms_scale(q_raw)
    k_scale = rms_scale(k_raw)
    q_hat = q_raw * q_scale
    k_hat = k_raw * k_scale
    q_rot = (
        rotate(q_hat * query_gain, cosine, sine_table)
        .astype(jnp.bfloat16)
        .reshape(length, kv_heads, groups, head_size)
    )
    k_rot = rotate(k_hat * key_gain, cosine, sine_table).astype(jnp.bfloat16)
    scores = score_table(q_rot, k_rot, allowed, factor)
    row_peak = jnp.max(scores, axis=-1, keepdims=True)
    log_total = row_peak + jnp.log(jnp.sum(jnp.exp(scores - row_peak), axis=-1, keepdims=True))
    attn_probs = jnp.exp(scores - log_total).astype(jnp.bfloat16)
    attn_mixed = jnp.einsum(
        "kgij,jkd->ikgd", attn_probs, v_half, preferred_element_type=jnp.float32
    )
    attn_mixed = attn_mixed.reshape(length, q_heads * head_size).astype(jnp.bfloat16)
    attn_sum = tensor_sum(jnp.dot(attn_mixed, w_out, preferred_element_type=jnp.float32))
    residual = tokens_wide + attn_sum
    scale_two = rms_scale(residual)
    normed_two = (residual * scale_two * ffn_gain).astype(jnp.bfloat16)
    gate_proj = jnp.dot(normed_two, w_gate, preferred_element_type=jnp.float32)
    up_proj = jnp.dot(normed_two, w_up, preferred_element_type=jnp.float32)
    gate_sigmoid = jax.nn.sigmoid(gate_proj)
    hidden = (gate_proj * gate_sigmoid * up_proj).astype(jnp.bfloat16)
    mlp_sum = tensor_sum(jnp.dot(hidden, w_down, preferred_element_type=jnp.float32))
    output = (residual + mlp_sum).astype(jnp.bfloat16)
    down_grad = outer(hidden, cotangent)
    hidden_grad = inner(cotangent, w_down)
    gate_grad = (
        hidden_grad * up_proj * gate_sigmoid * (1.0 + gate_proj * (1.0 - gate_sigmoid))
    ).astype(jnp.bfloat16)
    up_grad = (hidden_grad * gate_proj * gate_sigmoid).astype(jnp.bfloat16)
    gate_w_grad = outer(normed_two, gate_grad)
    up_w_grad = outer(normed_two, up_grad)
    normed_two_grad = tensor_sum(inner(gate_grad, w_gate) + inner(up_grad, w_up))
    ffn_grad = jnp.sum(normed_two_grad * residual * scale_two, axis=0)
    residual_grad = cotangent.astype(jnp.float32) + rms_back(
        normed_two_grad, residual, scale_two, ffn_gain
    )
    residual_half = residual_grad.astype(jnp.bfloat16)
    out_w_grad = outer(attn_mixed, residual_half)
    mixed_grad = (
        inner(residual_half, w_out)
        .astype(jnp.bfloat16)
        .reshape(length, kv_heads, groups, head_size)
    )
    attn_full = jnp.exp(score_table(q_rot, k_rot, allowed, factor) - log_total)
    probs_half = attn_full.astype(jnp.bfloat16)
    value_grad = jnp.einsum(
        "kgij,ikgd->jkd", probs_half, mixed_grad, preferred_element_type=jnp.float32
    ).astype(jnp.bfloat16)
    prob_grad = jnp.einsum("ikgd,jkd->kgij", mixed_grad, v_half, preferred_element_type=jnp.float32)
    row_delta = jnp.sum(attn_full * prob_grad, axis=-1, keepdims=True)
    score_grad = (attn_full * (prob_grad - row_delta) * factor).astype(jnp.bfloat16)
    q_rot_grad = jnp.einsum(
        "kgij,jkd->ikgd", score_grad, k_rot, preferred_element_type=jnp.float32
    ).reshape(length, q_heads, head_size)
    k_rot_grad = jnp.einsum("kgij,ikgd->jkd", score_grad, q_rot, preferred_element_type=jnp.float32)
    q_norm_grad = unrotate(q_rot_grad, cosine, sine_table)
    k_norm_grad = unrotate(k_rot_grad, cosine, sine_table)
    qgain_grad = jnp.sum(q_norm_grad * q_hat, axis=(0, 1))
    kgain_grad = jnp.sum(k_norm_grad * k_hat, axis=(0, 1))
    q_grad = (
        rms_back(q_norm_grad, q_raw, q_scale, query_gain)
        .astype(jnp.bfloat16)
        .reshape(length, q_heads * head_size)
    )
    k_grad = (
        rms_back(k_norm_grad, k_raw, k_scale, key_gain)
        .astype(jnp.bfloat16)
        .reshape(length, kv_heads * head_size)
    )
    v_grad = value_grad.reshape(length, kv_heads * head_size)
    query_w_grad = outer(normed_one, q_grad)
    key_w_grad = outer(normed_one, k_grad)
    value_w_grad = outer(normed_one, v_grad)
    normed_one_grad, gain_pair = tensor_sum(
        inner(q_grad, w_query) + inner(k_grad, w_key) + inner(v_grad, w_value),
        jnp.concatenate([qgain_grad, kgain_grad]),
    )
    attn_grad = jnp.sum(normed_one_grad * tokens_wide * scale_one, axis=0)
    input_grad = residual_grad + rms_back(normed_one_grad, tokens_wide, scale_one, attn_gain)
    down_grad, gate_w_grad, up_w_grad = lax.psum((down_grad, gate_w_grad, up_w_grad), "dp")
    width = attn_grad.shape[0]
    small = jnp.zeros((8, width), jnp.float32)
    small = small.at[0].set(attn_grad).at[1].set(ffn_grad)
    small = small.at[2, : gain_pair.shape[0]].set(gain_pair)
    out_rows = out_w_grad.shape[0]
    query_w_grad, key_w_grad, value_w_grad, out_pack = lax.psum(
        (query_w_grad, key_w_grad, value_w_grad, jnp.concatenate([out_w_grad, small])), "dp"
    )
    out_w_grad = out_pack[:out_rows]
    attn_grad = out_pack[out_rows]
    ffn_grad = out_pack[out_rows + 1]
    qgain_grad = out_pack[out_rows + 2, :head_size]
    kgain_grad = out_pack[out_rows + 2, head_size : 2 * head_size]
    return (
        output,
        input_grad,
        attn_grad,
        query_w_grad,
        key_w_grad,
        value_w_grad,
        qgain_grad,
        kgain_grad,
        out_w_grad,
        ffn_grad,
        gate_w_grad,
        up_w_grad,
        down_grad,
    )


def solution(mesh):
    from jax.sharding import Mesh

    dp_size, tensor_size = mesh.devices.shape
    split = Mesh(mesh.devices.reshape(dp_size, tensor_size // 2, 2), ("dp", "ty", "tx"))
    return jax.shard_map(
        per_device,
        mesh=split,
        in_specs=(
            P("dp", None),
            P("dp"),
            P(),
            P(None, TENSOR),
            P(None, TENSOR),
            P(None, TENSOR),
            P(),
            P(),
            P(TENSOR, None),
            P(),
            P(None, TENSOR),
            P(None, TENSOR),
            P(TENSOR, None),
            P("dp", None),
        ),
        out_specs=(
            P("dp", None),
            P("dp", None),
            P(),
            P(None, TENSOR),
            P(None, TENSOR),
            P(None, TENSOR),
            P(),
            P(),
            P(TENSOR, None),
            P(),
            P(None, TENSOR),
            P(None, TENSOR),
            P(TENSOR, None),
        ),
        check_vma=False,
    )
```

```python
import math

import jax
import jax.numpy as jnp
from jax import lax
from jax.sharding import PartitionSpec as P

EPS = 1e-05
THETA = 1000000.0
TENSOR = ("ty", "tx")


def outer(first_op, second_op):
    return lax.dot_general(
        first_op, second_op, (((0,), (0,)), ((), ())), preferred_element_type=jnp.float32
    )


def inner(first_op, second_op):
    return lax.dot_general(
        first_op, second_op, (((1,), (1,)), ((), ())), preferred_element_type=jnp.float32
    )


def rms_scale(values):
    return lax.rsqrt(jnp.mean(values * values, axis=-1, keepdims=True) + EPS)


def rms_back(upstream, values, inv_rms, gain_vec):
    normed = values * inv_rms
    weighted = upstream * gain_vec
    return inv_rms * (weighted - normed * jnp.mean(weighted * normed, axis=-1, keepdims=True))


def seq_layout(segment):
    length = segment.shape[0]
    ordinal = jnp.arange(length, dtype=jnp.int32)
    same_seq = segment[:, None] == segment[None, :]
    places = jnp.sum((same_seq & (ordinal[None, :] < ordinal[:, None])).astype(jnp.int32), axis=1)
    allowed = same_seq & (ordinal[None, :] <= ordinal[:, None])
    return (places, allowed)


def rope_tables(places, head_size):
    frequency = jnp.exp(
        jnp.arange(head_size // 2, dtype=jnp.float32) * (-2.0 * math.log(THETA) / head_size)
    )
    angles = places.astype(jnp.float32)[:, None] * frequency[None, :]
    angles = jnp.concatenate([angles, angles], axis=1)
    return (jnp.cos(angles), jnp.sin(angles))


def rotate(values, cosine, sine_table):
    half = values.shape[-1] // 2
    turned = jnp.concatenate([-values[..., half:], values[..., :half]], axis=-1)
    return values * cosine[:, None, :] + turned * sine_table[:, None, :]


def unrotate(incoming, cosine, sine_table):
    half = incoming.shape[-1] // 2
    scaled = incoming * sine_table[:, None, :]
    swapped = jnp.concatenate([scaled[..., half:], -scaled[..., :half]], axis=-1)
    return incoming * cosine[:, None, :] + swapped


def score_table(q_rot, k_rot, allowed, factor):
    raw = jnp.einsum("ikgd,jkd->kgij", q_rot, k_rot, preferred_element_type=jnp.float32) * factor
    return jnp.where(allowed[None, None], raw, -1e30)


def ring(size, shift):
    return [(i, (i + shift) % size) for i in range(size)]


def tensor_sum(values, extra=None):
    rows, cols = values.shape
    ny = lax.axis_size("ty")
    nx = lax.axis_size("tx")
    y = lax.axis_index("ty")
    h = lax.axis_index("tx")
    leaf = rows // (2 * ny * nx)
    parts = values.reshape(2, ny, nx, leaf, cols)
    pairs = ring(nx, 1)
    total = extra
    accs = []
    for way, shift in ((0, 1), (1, -1)):
        chunks = parts[way]
        acc = lax.dynamic_index_in_dim(chunks, (y - shift) % ny, 0, keepdims=False)
        passing = extra
        for step in range(1, ny):
            if way == 0 and extra is not None:
                acc, passing = lax.ppermute((acc, passing), "ty", ring(ny, shift))
                total = total + passing
            else:
                acc = lax.ppermute(acc, "ty", ring(ny, shift))
            acc = acc + lax.dynamic_index_in_dim(chunks, (y - shift * (1 + step)) % ny, 0, keepdims=False)
        accs.append(acc)
    acc = jnp.stack(accs)
    keep = lax.dynamic_index_in_dim(acc, h, 1, keepdims=False)
    send = lax.dynamic_index_in_dim(acc, (h + 1) % nx, 1, keepdims=False)
    if extra is not None:
        got, got_total = lax.ppermute((send, total), "tx", pairs)
        total = total + got_total
    else:
        got = lax.ppermute(send, "tx", pairs)
    mine = keep + got
    other = lax.ppermute(mine, "tx", pairs)
    both = jnp.where(h == 0, jnp.stack([mine, other], 1), jnp.stack([other, mine], 1))
    outs = []
    for way, shift in ((0, 1), (1, -1)):
        cur = both[way]
        gathered = jnp.zeros((ny,) + cur.shape, values.dtype)
        gathered = lax.dynamic_update_index_in_dim(gathered, cur, y, 0)
        for step in range(1, ny):
            cur = lax.ppermute(cur, "ty", ring(ny, shift))
            gathered = lax.dynamic_update_index_in_dim(gathered, cur, (y - shift * step) % ny, 0)
        outs.append(gathered)
    result = jnp.stack(outs).reshape(rows, cols)
    if extra is None:
        return result
    return result, total


def per_device(
    tokens,
    segment_ids,
    attn_gain,
    w_query,
    w_key,
    w_value,
    query_gain,
    key_gain,
    w_out,
    ffn_gain,
    w_gate,
    w_up,
    w_down,
    cotangent,
):
    length = tokens.shape[0]
    head_size = query_gain.shape[0]
    q_heads = w_query.shape[1] // head_size
    kv_heads = w_key.shape[1] // head_size
    groups = q_heads // kv_heads
    factor = 1.0 / math.sqrt(head_size)
    places, allowed = seq_layout(segment_ids)
    cosine, sine_table = rope_tables(places, head_size)
    tokens_wide = tokens.astype(jnp.float32)
    scale_one = rms_scale(tokens_wide)
    normed_one = (tokens_wide * scale_one * attn_gain).astype(jnp.bfloat16)
    q_raw = jnp.dot(normed_one, w_query, preferred_element_type=jnp.float32).reshape(
        length, q_heads, head_size
    )
    k_raw = jnp.dot(normed_one, w_key, preferred_element_type=jnp.float32).reshape(
        length, kv_heads, head_size
    )
    v_half = (
        jnp.dot(normed_one, w_value, preferred_element_type=jnp.float32)
        .astype(jnp.bfloat16)
        .reshape(length, kv_heads, head_size)
    )
    q_scale = rms_scale(q_raw)
    k_scale = rms_scale(k_raw)
    q_hat = q_raw * q_scale
    k_hat = k_raw * k_scale
    q_rot = (
        rotate(q_hat * query_gain, cosine, sine_table)
        .astype(jnp.bfloat16)
        .reshape(length, kv_heads, groups, head_size)
    )
    k_rot = rotate(k_hat * key_gain, cosine, sine_table).astype(jnp.bfloat16)
    scores = score_table(q_rot, k_rot, allowed, factor)
    row_peak = jnp.max(scores, axis=-1, keepdims=True)
    log_total = row_peak + jnp.log(jnp.sum(jnp.exp(scores - row_peak), axis=-1, keepdims=True))
    attn_probs = jnp.exp(scores - log_total).astype(jnp.bfloat16)
    attn_mixed = jnp.einsum(
        "kgij,jkd->ikgd", attn_probs, v_half, preferred_element_type=jnp.float32
    )
    attn_mixed = attn_mixed.reshape(length, q_heads * head_size).astype(jnp.bfloat16)
    attn_sum = tensor_sum(jnp.dot(attn_mixed, w_out, preferred_element_type=jnp.float32))
    residual = tokens_wide + attn_sum
    scale_two = rms_scale(residual)
    normed_two = (residual * scale_two * ffn_gain).astype(jnp.bfloat16)
    gate_proj = jnp.dot(normed_two, w_gate, preferred_element_type=jnp.float32)
    up_proj = jnp.dot(normed_two, w_up, preferred_element_type=jnp.float32)
    gate_sigmoid = jax.nn.sigmoid(gate_proj)
    hidden = (gate_proj * gate_sigmoid * up_proj).astype(jnp.bfloat16)
    mlp_sum = tensor_sum(jnp.dot(hidden, w_down, preferred_element_type=jnp.float32))
    output = (residual + mlp_sum).astype(jnp.bfloat16)
    down_grad = outer(hidden, cotangent)
    hidden_grad = inner(cotangent, w_down)
    gate_grad = (
        hidden_grad * up_proj * gate_sigmoid * (1.0 + gate_proj * (1.0 - gate_sigmoid))
    ).astype(jnp.bfloat16)
    up_grad = (hidden_grad * gate_proj * gate_sigmoid).astype(jnp.bfloat16)
    gate_w_grad = outer(normed_two, gate_grad)
    up_w_grad = outer(normed_two, up_grad)
    ffn_w_grads, two_partial = lax.optimization_barrier(
        ((down_grad, gate_w_grad, up_w_grad), inner(gate_grad, w_gate) + inner(up_grad, w_up))
    )
    down_grad, gate_w_grad, up_w_grad = lax.psum(ffn_w_grads, "dp")
    normed_two_grad = tensor_sum(two_partial)
    ffn_grad = jnp.sum(normed_two_grad * residual * scale_two, axis=0)
    residual_grad = cotangent.astype(jnp.float32) + rms_back(
        normed_two_grad, residual, scale_two, ffn_gain
    )
    residual_half = residual_grad.astype(jnp.bfloat16)
    out_w_grad = outer(attn_mixed, residual_half)
    mixed_grad = (
        inner(residual_half, w_out)
        .astype(jnp.bfloat16)
        .reshape(length, kv_heads, groups, head_size)
    )
    attn_full = jnp.exp(score_table(q_rot, k_rot, allowed, factor) - log_total)
    probs_half = attn_full.astype(jnp.bfloat16)
    value_grad = jnp.einsum(
        "kgij,ikgd->jkd", probs_half, mixed_grad, preferred_element_type=jnp.float32
    ).astype(jnp.bfloat16)
    prob_grad = jnp.einsum("ikgd,jkd->kgij", mixed_grad, v_half, preferred_element_type=jnp.float32)
    row_delta = jnp.sum(attn_full * prob_grad, axis=-1, keepdims=True)
    score_grad = (attn_full * (prob_grad - row_delta) * factor).astype(jnp.bfloat16)
    q_rot_grad = jnp.einsum(
        "kgij,jkd->ikgd", score_grad, k_rot, preferred_element_type=jnp.float32
    ).reshape(length, q_heads, head_size)
    k_rot_grad = jnp.einsum("kgij,ikgd->jkd", score_grad, q_rot, preferred_element_type=jnp.float32)
    q_norm_grad = unrotate(q_rot_grad, cosine, sine_table)
    k_norm_grad = unrotate(k_rot_grad, cosine, sine_table)
    qgain_grad = jnp.sum(q_norm_grad * q_hat, axis=(0, 1))
    kgain_grad = jnp.sum(k_norm_grad * k_hat, axis=(0, 1))
    q_grad = (
        rms_back(q_norm_grad, q_raw, q_scale, query_gain)
        .astype(jnp.bfloat16)
        .reshape(length, q_heads * head_size)
    )
    k_grad = (
        rms_back(k_norm_grad, k_raw, k_scale, key_gain)
        .astype(jnp.bfloat16)
        .reshape(length, kv_heads * head_size)
    )
    v_grad = value_grad.reshape(length, kv_heads * head_size)
    query_w_grad = outer(normed_one, q_grad)
    key_w_grad = outer(normed_one, k_grad)
    value_w_grad = outer(normed_one, v_grad)
    normed_one_grad, gain_pair = tensor_sum(
        inner(q_grad, w_query) + inner(k_grad, w_key) + inner(v_grad, w_value),
        jnp.concatenate([qgain_grad, kgain_grad]),
    )
    attn_grad = jnp.sum(normed_one_grad * tokens_wide * scale_one, axis=0)
    input_grad = residual_grad + rms_back(normed_one_grad, tokens_wide, scale_one, attn_gain)
    width = attn_grad.shape[0]
    small = jnp.zeros((8, width), jnp.float32)
    small = small.at[0].set(attn_grad).at[1].set(ffn_grad)
    small = small.at[2, : gain_pair.shape[0]].set(gain_pair)
    out_rows = out_w_grad.shape[0]
    attn_side = (query_w_grad, key_w_grad, value_w_grad, jnp.concatenate([out_w_grad, small]))
    _, attn_side = lax.optimization_barrier(((down_grad, gate_w_grad, up_w_grad), attn_side))
    query_w_grad, key_w_grad, value_w_grad, out_pack = lax.psum(attn_side, "dp")
    out_w_grad = out_pack[:out_rows]
    attn_grad = out_pack[out_rows]
    ffn_grad = out_pack[out_rows + 1]
    qgain_grad = out_pack[out_rows + 2, :head_size]
    kgain_grad = out_pack[out_rows + 2, head_size : 2 * head_size]
    return (
        output,
        input_grad,
        attn_grad,
        query_w_grad,
        key_w_grad,
        value_w_grad,
        qgain_grad,
        kgain_grad,
        out_w_grad,
        ffn_grad,
        gate_w_grad,
        up_w_grad,
        down_grad,
    )


def solution(mesh):
    from jax.sharding import Mesh

    dp_size, tensor_size = mesh.devices.shape
    split = Mesh(mesh.devices.reshape(dp_size, tensor_size // 2, 2), ("dp", "ty", "tx"))
    return jax.shard_map(
        per_device,
        mesh=split,
        in_specs=(
            P("dp", None),
            P("dp"),
            P(),
            P(None, TENSOR),
            P(None, TENSOR),
            P(None, TENSOR),
            P(),
            P(),
            P(TENSOR, None),
            P(),
            P(None, TENSOR),
            P(None, TENSOR),
            P(TENSOR, None),
            P("dp", None),
        ),
        out_specs=(
            P("dp", None),
            P("dp", None),
            P(),
            P(None, TENSOR),
            P(None, TENSOR),
            P(None, TENSOR),
            P(),
            P(),
            P(TENSOR, None),
            P(),
            P(None, TENSOR),
            P(None, TENSOR),
            P(TENSOR, None),
        ),
        check_vma=False,
    )
```

```python
import math

import jax
import jax.numpy as jnp
from jax import lax
from jax.sharding import PartitionSpec as P

EPS = 1e-05
THETA = 1000000.0
TENSOR = ("ty", "tx")


def outer(first_op, second_op):
    return lax.dot_general(
        first_op, second_op, (((0,), (0,)), ((), ())), preferred_element_type=jnp.float32
    )


def inner(first_op, second_op):
    return lax.dot_general(
        first_op, second_op, (((1,), (1,)), ((), ())), preferred_element_type=jnp.float32
    )


def rms_scale(values):
    return lax.rsqrt(jnp.mean(values * values, axis=-1, keepdims=True) + EPS)


def rms_back(upstream, values, inv_rms, gain_vec):
    normed = values * inv_rms
    weighted = upstream * gain_vec
    return inv_rms * (weighted - normed * jnp.mean(weighted * normed, axis=-1, keepdims=True))


def seq_layout(segment):
    length = segment.shape[0]
    ordinal = jnp.arange(length, dtype=jnp.int32)
    same_seq = segment[:, None] == segment[None, :]
    places = jnp.sum((same_seq & (ordinal[None, :] < ordinal[:, None])).astype(jnp.int32), axis=1)
    allowed = same_seq & (ordinal[None, :] <= ordinal[:, None])
    return (places, allowed)


def rope_tables(places, head_size):
    frequency = jnp.exp(
        jnp.arange(head_size // 2, dtype=jnp.float32) * (-2.0 * math.log(THETA) / head_size)
    )
    angles = places.astype(jnp.float32)[:, None] * frequency[None, :]
    angles = jnp.concatenate([angles, angles], axis=1)
    return (jnp.cos(angles), jnp.sin(angles))


def rotate(values, cosine, sine_table):
    half = values.shape[-1] // 2
    turned = jnp.concatenate([-values[..., half:], values[..., :half]], axis=-1)
    return values * cosine[:, None, :] + turned * sine_table[:, None, :]


def unrotate(incoming, cosine, sine_table):
    half = incoming.shape[-1] // 2
    scaled = incoming * sine_table[:, None, :]
    swapped = jnp.concatenate([scaled[..., half:], -scaled[..., :half]], axis=-1)
    return incoming * cosine[:, None, :] + swapped


def score_table(q_rot, k_rot, allowed, factor):
    raw = jnp.einsum("ikgd,jkd->kgij", q_rot, k_rot, preferred_element_type=jnp.float32) * factor
    return jnp.where(allowed[None, None], raw, -1e30)


def ring(size, shift):
    return [(i, (i + shift) % size) for i in range(size)]


def tensor_sum(values, extra=None):
    rows, cols = values.shape
    ny = lax.axis_size("ty")
    nx = lax.axis_size("tx")
    y = lax.axis_index("ty")
    h = lax.axis_index("tx")
    leaf = rows // (2 * ny * nx)
    parts = values.reshape(2, ny, nx, leaf, cols)
    pairs = ring(nx, 1)
    total = extra
    accs = []
    for way, shift in ((0, 1), (1, -1)):
        chunks = parts[way]
        acc = lax.dynamic_index_in_dim(chunks, (y - shift) % ny, 0, keepdims=False)
        passing = extra
        for step in range(1, ny):
            if way == 0 and extra is not None:
                acc, passing = lax.ppermute((acc, passing), "ty", ring(ny, shift))
                total = total + passing
            else:
                acc = lax.ppermute(acc, "ty", ring(ny, shift))
            acc = acc + lax.dynamic_index_in_dim(chunks, (y - shift * (1 + step)) % ny, 0, keepdims=False)
        accs.append(acc)
    acc = jnp.stack(accs)
    keep = lax.dynamic_index_in_dim(acc, h, 1, keepdims=False)
    send = lax.dynamic_index_in_dim(acc, (h + 1) % nx, 1, keepdims=False)
    if extra is not None:
        got, got_total = lax.ppermute((send, total), "tx", pairs)
        total = total + got_total
    else:
        got = lax.ppermute(send, "tx", pairs)
    mine = keep + got
    other = lax.ppermute(mine, "tx", pairs)
    both = jnp.where(h == 0, jnp.stack([mine, other], 1), jnp.stack([other, mine], 1))
    outs = []
    for way, shift in ((0, 1), (1, -1)):
        cur = both[way]
        gathered = jnp.zeros((ny,) + cur.shape, values.dtype)
        gathered = lax.dynamic_update_index_in_dim(gathered, cur, y, 0)
        for step in range(1, ny):
            cur = lax.ppermute(cur, "ty", ring(ny, shift))
            gathered = lax.dynamic_update_index_in_dim(gathered, cur, (y - shift * step) % ny, 0)
        outs.append(gathered)
    result = jnp.stack(outs).reshape(rows, cols)
    if extra is None:
        return result
    return result, total


def small_tensor_sum(values):
    ny = lax.axis_size("ty")
    nx = lax.axis_size("tx")
    dist = 1
    while dist < ny:
        values = values + lax.ppermute(values, "ty", [(i, i ^ dist) for i in range(ny)])
        dist *= 2
    dist = 1
    while dist < nx:
        values = values + lax.ppermute(values, "tx", [(i, i ^ dist) for i in range(nx)])
        dist *= 2
    return values


def per_device(
    tokens,
    segment_ids,
    attn_gain,
    w_query,
    w_key,
    w_value,
    query_gain,
    key_gain,
    w_out,
    ffn_gain,
    w_gate,
    w_up,
    w_down,
    cotangent,
):
    length = tokens.shape[0]
    head_size = query_gain.shape[0]
    q_heads = w_query.shape[1] // head_size
    kv_heads = w_key.shape[1] // head_size
    groups = q_heads // kv_heads
    factor = 1.0 / math.sqrt(head_size)
    places, allowed = seq_layout(segment_ids)
    cosine, sine_table = rope_tables(places, head_size)
    tokens_wide = tokens.astype(jnp.float32)
    scale_one = rms_scale(tokens_wide)
    normed_one = (tokens_wide * scale_one * attn_gain).astype(jnp.bfloat16)
    q_raw = jnp.dot(normed_one, w_query, preferred_element_type=jnp.float32).reshape(
        length, q_heads, head_size
    )
    k_raw = jnp.dot(normed_one, w_key, preferred_element_type=jnp.float32).reshape(
        length, kv_heads, head_size
    )
    v_half = (
        jnp.dot(normed_one, w_value, preferred_element_type=jnp.float32)
        .astype(jnp.bfloat16)
        .reshape(length, kv_heads, head_size)
    )
    q_scale = rms_scale(q_raw)
    k_scale = rms_scale(k_raw)
    q_hat = q_raw * q_scale
    k_hat = k_raw * k_scale
    q_rot = (
        rotate(q_hat * query_gain, cosine, sine_table)
        .astype(jnp.bfloat16)
        .reshape(length, kv_heads, groups, head_size)
    )
    k_rot = rotate(k_hat * key_gain, cosine, sine_table).astype(jnp.bfloat16)
    scores = score_table(q_rot, k_rot, allowed, factor)
    row_peak = jnp.max(scores, axis=-1, keepdims=True)
    log_total = row_peak + jnp.log(jnp.sum(jnp.exp(scores - row_peak), axis=-1, keepdims=True))
    attn_probs = jnp.exp(scores - log_total).astype(jnp.bfloat16)
    attn_mixed = jnp.einsum(
        "kgij,jkd->ikgd", attn_probs, v_half, preferred_element_type=jnp.float32
    )
    attn_mixed = attn_mixed.reshape(length, q_heads * head_size).astype(jnp.bfloat16)
    attn_sum = tensor_sum(jnp.dot(attn_mixed, w_out, preferred_element_type=jnp.float32))
    residual = tokens_wide + attn_sum
    scale_two = rms_scale(residual)
    normed_two = (residual * scale_two * ffn_gain).astype(jnp.bfloat16)
    gate_proj = jnp.dot(normed_two, w_gate, preferred_element_type=jnp.float32)
    up_proj = jnp.dot(normed_two, w_up, preferred_element_type=jnp.float32)
    gate_sigmoid = jax.nn.sigmoid(gate_proj)
    hidden = (gate_proj * gate_sigmoid * up_proj).astype(jnp.bfloat16)
    mlp_sum = tensor_sum(jnp.dot(hidden, w_down, preferred_element_type=jnp.float32))
    output = (residual + mlp_sum).astype(jnp.bfloat16)
    down_grad = outer(hidden, cotangent)
    hidden_grad = inner(cotangent, w_down)
    gate_grad = (
        hidden_grad * up_proj * gate_sigmoid * (1.0 + gate_proj * (1.0 - gate_sigmoid))
    ).astype(jnp.bfloat16)
    up_grad = (hidden_grad * gate_proj * gate_sigmoid).astype(jnp.bfloat16)
    gate_w_grad = outer(normed_two, gate_grad)
    up_w_grad = outer(normed_two, up_grad)
    normed_two_grad = tensor_sum(inner(gate_grad, w_gate) + inner(up_grad, w_up))
    ffn_grad = jnp.sum(normed_two_grad * residual * scale_two, axis=0)
    residual_grad = cotangent.astype(jnp.float32) + rms_back(
        normed_two_grad, residual, scale_two, ffn_gain
    )
    residual_half = residual_grad.astype(jnp.bfloat16)
    out_w_grad = outer(attn_mixed, residual_half)
    mixed_grad = (
        inner(residual_half, w_out)
        .astype(jnp.bfloat16)
        .reshape(length, kv_heads, groups, head_size)
    )
    attn_full = jnp.exp(score_table(q_rot, k_rot, allowed, factor) - log_total)
    probs_half = attn_full.astype(jnp.bfloat16)
    value_grad = jnp.einsum(
        "kgij,ikgd->jkd", probs_half, mixed_grad, preferred_element_type=jnp.float32
    ).astype(jnp.bfloat16)
    prob_grad = jnp.einsum("ikgd,jkd->kgij", mixed_grad, v_half, preferred_element_type=jnp.float32)
    row_delta = jnp.sum(attn_full * prob_grad, axis=-1, keepdims=True)
    score_grad = (attn_full * (prob_grad - row_delta) * factor).astype(jnp.bfloat16)
    q_rot_grad = jnp.einsum(
        "kgij,jkd->ikgd", score_grad, k_rot, preferred_element_type=jnp.float32
    ).reshape(length, q_heads, head_size)
    k_rot_grad = jnp.einsum("kgij,ikgd->jkd", score_grad, q_rot, preferred_element_type=jnp.float32)
    q_norm_grad = unrotate(q_rot_grad, cosine, sine_table)
    k_norm_grad = unrotate(k_rot_grad, cosine, sine_table)
    qgain_grad = jnp.sum(q_norm_grad * q_hat, axis=(0, 1))
    kgain_grad = jnp.sum(k_norm_grad * k_hat, axis=(0, 1))
    q_grad = (
        rms_back(q_norm_grad, q_raw, q_scale, query_gain)
        .astype(jnp.bfloat16)
        .reshape(length, q_heads * head_size)
    )
    k_grad = (
        rms_back(k_norm_grad, k_raw, k_scale, key_gain)
        .astype(jnp.bfloat16)
        .reshape(length, kv_heads * head_size)
    )
    v_grad = value_grad.reshape(length, kv_heads * head_size)
    query_w_grad = outer(normed_one, q_grad)
    key_w_grad = outer(normed_one, k_grad)
    value_w_grad = outer(normed_one, v_grad)
    one_partial = inner(q_grad, w_query) + inner(k_grad, w_key) + inner(v_grad, w_value)
    attn_part = jnp.sum(one_partial * tokens_wide * scale_one, axis=0)
    width = attn_part.shape[0]
    small = jnp.zeros((8, width), jnp.float32)
    small = small.at[0].set(ffn_grad).at[1].set(attn_part)
    small = small.at[2, :head_size].set(qgain_grad).at[2, head_size : 2 * head_size].set(kgain_grad)
    out_rows = out_w_grad.shape[0]
    dp_sums, one_partial = lax.optimization_barrier(
        (
            (
                query_w_grad,
                key_w_grad,
                value_w_grad,
                jnp.concatenate([out_w_grad, small]),
                gate_w_grad,
                up_w_grad,
                down_grad,
            ),
            one_partial,
        )
    )
    (
        query_w_grad,
        key_w_grad,
        value_w_grad,
        out_pack,
        gate_w_grad,
        up_w_grad,
        down_grad,
    ) = lax.psum(dp_sums, "dp")
    normed_one_grad = tensor_sum(one_partial)
    input_grad = residual_grad + rms_back(normed_one_grad, tokens_wide, scale_one, attn_gain)
    out_w_grad = out_pack[:out_rows]
    ffn_grad = out_pack[out_rows]
    gains = small_tensor_sum(out_pack[out_rows + 1 : out_rows + 3])
    attn_grad = gains[0]
    qgain_grad = gains[1, :head_size]
    kgain_grad = gains[1, head_size : 2 * head_size]
    return (
        output,
        input_grad,
        attn_grad,
        query_w_grad,
        key_w_grad,
        value_w_grad,
        qgain_grad,
        kgain_grad,
        out_w_grad,
        ffn_grad,
        gate_w_grad,
        up_w_grad,
        down_grad,
    )


def solution(mesh):
    from jax.sharding import Mesh

    dp_size, tensor_size = mesh.devices.shape
    split = Mesh(mesh.devices.reshape(dp_size, tensor_size // 2, 2), ("dp", "ty", "tx"))
    return jax.shard_map(
        per_device,
        mesh=split,
        in_specs=(
            P("dp", None),
            P("dp"),
            P(),
            P(None, TENSOR),
            P(None, TENSOR),
            P(None, TENSOR),
            P(),
            P(),
            P(TENSOR, None),
            P(),
            P(None, TENSOR),
            P(None, TENSOR),
            P(TENSOR, None),
            P("dp", None),
        ),
        out_specs=(
            P("dp", None),
            P("dp", None),
            P(),
            P(None, TENSOR),
            P(None, TENSOR),
            P(None, TENSOR),
            P(),
            P(),
            P(TENSOR, None),
            P(),
            P(None, TENSOR),
            P(None, TENSOR),
            P(TENSOR, None),
        ),
        check_vma=False,
    )
```

```python
import math

import jax
import jax.numpy as jnp
from jax import lax
from jax.sharding import PartitionSpec as P

EPS = 1e-05
THETA = 1000000.0
TENSOR = ("ty", "tx")


def outer(first_op, second_op):
    return lax.dot_general(
        first_op, second_op, (((0,), (0,)), ((), ())), preferred_element_type=jnp.float32
    )


def inner(first_op, second_op):
    return lax.dot_general(
        first_op, second_op, (((1,), (1,)), ((), ())), preferred_element_type=jnp.float32
    )


def rms_scale(values):
    return lax.rsqrt(jnp.mean(values * values, axis=-1, keepdims=True) + EPS)


def rms_back(upstream, values, inv_rms, gain_vec):
    normed = values * inv_rms
    weighted = upstream * gain_vec
    return inv_rms * (weighted - normed * jnp.mean(weighted * normed, axis=-1, keepdims=True))


def seq_layout(segment):
    length = segment.shape[0]
    ordinal = jnp.arange(length, dtype=jnp.int32)
    same_seq = segment[:, None] == segment[None, :]
    places = jnp.sum((same_seq & (ordinal[None, :] < ordinal[:, None])).astype(jnp.int32), axis=1)
    allowed = same_seq & (ordinal[None, :] <= ordinal[:, None])
    return (places, allowed)


def rope_tables(places, head_size):
    frequency = jnp.exp(
        jnp.arange(head_size // 2, dtype=jnp.float32) * (-2.0 * math.log(THETA) / head_size)
    )
    angles = places.astype(jnp.float32)[:, None] * frequency[None, :]
    angles = jnp.concatenate([angles, angles], axis=1)
    return (jnp.cos(angles), jnp.sin(angles))


def rotate(values, cosine, sine_table):
    half = values.shape[-1] // 2
    turned = jnp.concatenate([-values[..., half:], values[..., :half]], axis=-1)
    return values * cosine[:, None, :] + turned * sine_table[:, None, :]


def unrotate(incoming, cosine, sine_table):
    half = incoming.shape[-1] // 2
    scaled = incoming * sine_table[:, None, :]
    swapped = jnp.concatenate([scaled[..., half:], -scaled[..., :half]], axis=-1)
    return incoming * cosine[:, None, :] + swapped


def score_table(q_rot, k_rot, allowed, factor):
    raw = jnp.einsum("ikgd,jkd->kgij", q_rot, k_rot, preferred_element_type=jnp.float32) * factor
    return jnp.where(allowed[None, None], raw, -1e30)


def ring(size, shift):
    return [(i, (i + shift) % size) for i in range(size)]


def tensor_sum(values, extra=None):
    rows, cols = values.shape
    ny = lax.axis_size("ty")
    nx = lax.axis_size("tx")
    y = lax.axis_index("ty")
    h = lax.axis_index("tx")
    leaf = rows // (2 * ny * nx)
    parts = values.reshape(2, ny, nx, leaf, cols)
    pairs = ring(nx, 1)
    total = extra
    accs = []
    for way, shift in ((0, 1), (1, -1)):
        chunks = parts[way]
        acc = lax.dynamic_index_in_dim(chunks, (y - shift) % ny, 0, keepdims=False)
        passing = extra
        for step in range(1, ny):
            if way == 0 and extra is not None:
                acc, passing = lax.ppermute((acc, passing), "ty", ring(ny, shift))
                total = total + passing
            else:
                acc = lax.ppermute(acc, "ty", ring(ny, shift))
            acc = acc + lax.dynamic_index_in_dim(chunks, (y - shift * (1 + step)) % ny, 0, keepdims=False)
        accs.append(acc)
    acc = jnp.stack(accs)
    keep = lax.dynamic_index_in_dim(acc, h, 1, keepdims=False)
    send = lax.dynamic_index_in_dim(acc, (h + 1) % nx, 1, keepdims=False)
    if extra is not None:
        got, got_total = lax.ppermute((send, total), "tx", pairs)
        total = total + got_total
    else:
        got = lax.ppermute(send, "tx", pairs)
    mine = keep + got
    other = lax.ppermute(mine, "tx", pairs)
    both = jnp.where(h == 0, jnp.stack([mine, other], 1), jnp.stack([other, mine], 1))
    outs = []
    for way, shift in ((0, 1), (1, -1)):
        cur = both[way]
        gathered = jnp.zeros((ny,) + cur.shape, values.dtype)
        gathered = lax.dynamic_update_index_in_dim(gathered, cur, y, 0)
        for step in range(1, ny):
            cur = lax.ppermute(cur, "ty", ring(ny, shift))
            gathered = lax.dynamic_update_index_in_dim(gathered, cur, (y - shift * step) % ny, 0)
        outs.append(gathered)
    result = jnp.stack(outs).reshape(rows, cols)
    if extra is None:
        return result
    return result, total


def split_tensor_sum(values, pieces=2):
    blocks = jnp.split(values, pieces, axis=0)
    return jnp.concatenate([tensor_sum(block) for block in blocks], axis=0)


def small_tensor_sum(values):
    ny = lax.axis_size("ty")
    nx = lax.axis_size("tx")
    dist = 1
    while dist < ny:
        values = values + lax.ppermute(values, "ty", [(i, i ^ dist) for i in range(ny)])
        dist *= 2
    dist = 1
    while dist < nx:
        values = values + lax.ppermute(values, "tx", [(i, i ^ dist) for i in range(nx)])
        dist *= 2
    return values


def per_device(
    tokens,
    segment_ids,
    attn_gain,
    w_query,
    w_key,
    w_value,
    query_gain,
    key_gain,
    w_out,
    ffn_gain,
    w_gate,
    w_up,
    w_down,
    cotangent,
):
    length = tokens.shape[0]
    head_size = query_gain.shape[0]
    q_heads = w_query.shape[1] // head_size
    kv_heads = w_key.shape[1] // head_size
    groups = q_heads // kv_heads
    factor = 1.0 / math.sqrt(head_size)
    places, allowed = seq_layout(segment_ids)
    cosine, sine_table = rope_tables(places, head_size)
    tokens_wide = tokens.astype(jnp.float32)
    scale_one = rms_scale(tokens_wide)
    normed_one = (tokens_wide * scale_one * attn_gain).astype(jnp.bfloat16)
    q_raw = jnp.dot(normed_one, w_query, preferred_element_type=jnp.float32).reshape(
        length, q_heads, head_size
    )
    k_raw = jnp.dot(normed_one, w_key, preferred_element_type=jnp.float32).reshape(
        length, kv_heads, head_size
    )
    v_half = (
        jnp.dot(normed_one, w_value, preferred_element_type=jnp.float32)
        .astype(jnp.bfloat16)
        .reshape(length, kv_heads, head_size)
    )
    q_scale = rms_scale(q_raw)
    k_scale = rms_scale(k_raw)
    q_hat = q_raw * q_scale
    k_hat = k_raw * k_scale
    q_rot = (
        rotate(q_hat * query_gain, cosine, sine_table)
        .astype(jnp.bfloat16)
        .reshape(length, kv_heads, groups, head_size)
    )
    k_rot = rotate(k_hat * key_gain, cosine, sine_table).astype(jnp.bfloat16)
    scores = score_table(q_rot, k_rot, allowed, factor)
    row_peak = jnp.max(scores, axis=-1, keepdims=True)
    log_total = row_peak + jnp.log(jnp.sum(jnp.exp(scores - row_peak), axis=-1, keepdims=True))
    attn_probs = jnp.exp(scores - log_total).astype(jnp.bfloat16)
    attn_mixed = jnp.einsum(
        "kgij,jkd->ikgd", attn_probs, v_half, preferred_element_type=jnp.float32
    )
    attn_mixed = attn_mixed.reshape(length, q_heads * head_size).astype(jnp.bfloat16)
    attn_sum = split_tensor_sum(jnp.dot(attn_mixed, w_out, preferred_element_type=jnp.float32))
    residual = tokens_wide + attn_sum
    scale_two = rms_scale(residual)
    normed_two = (residual * scale_two * ffn_gain).astype(jnp.bfloat16)
    gate_proj = jnp.dot(normed_two, w_gate, preferred_element_type=jnp.float32)
    up_proj = jnp.dot(normed_two, w_up, preferred_element_type=jnp.float32)
    gate_sigmoid = jax.nn.sigmoid(gate_proj)
    hidden = (gate_proj * gate_sigmoid * up_proj).astype(jnp.bfloat16)
    mlp_sum = split_tensor_sum(jnp.dot(hidden, w_down, preferred_element_type=jnp.float32))
    output = (residual + mlp_sum).astype(jnp.bfloat16)
    down_grad = outer(hidden, cotangent)
    hidden_grad = inner(cotangent, w_down)
    gate_grad = (
        hidden_grad * up_proj * gate_sigmoid * (1.0 + gate_proj * (1.0 - gate_sigmoid))
    ).astype(jnp.bfloat16)
    up_grad = (hidden_grad * gate_proj * gate_sigmoid).astype(jnp.bfloat16)
    gate_w_grad = outer(normed_two, gate_grad)
    up_w_grad = outer(normed_two, up_grad)
    normed_two_grad = split_tensor_sum(inner(gate_grad, w_gate) + inner(up_grad, w_up))
    ffn_grad = jnp.sum(normed_two_grad * residual * scale_two, axis=0)
    residual_grad = cotangent.astype(jnp.float32) + rms_back(
        normed_two_grad, residual, scale_two, ffn_gain
    )
    residual_half = residual_grad.astype(jnp.bfloat16)
    out_w_grad = outer(attn_mixed, residual_half)
    mixed_grad = (
        inner(residual_half, w_out)
        .astype(jnp.bfloat16)
        .reshape(length, kv_heads, groups, head_size)
    )
    attn_full = jnp.exp(score_table(q_rot, k_rot, allowed, factor) - log_total)
    probs_half = attn_full.astype(jnp.bfloat16)
    value_grad = jnp.einsum(
        "kgij,ikgd->jkd", probs_half, mixed_grad, preferred_element_type=jnp.float32
    ).astype(jnp.bfloat16)
    prob_grad = jnp.einsum("ikgd,jkd->kgij", mixed_grad, v_half, preferred_element_type=jnp.float32)
    row_delta = jnp.sum(attn_full * prob_grad, axis=-1, keepdims=True)
    score_grad = (attn_full * (prob_grad - row_delta) * factor).astype(jnp.bfloat16)
    q_rot_grad = jnp.einsum(
        "kgij,jkd->ikgd", score_grad, k_rot, preferred_element_type=jnp.float32
    ).reshape(length, q_heads, head_size)
    k_rot_grad = jnp.einsum("kgij,ikgd->jkd", score_grad, q_rot, preferred_element_type=jnp.float32)
    q_norm_grad = unrotate(q_rot_grad, cosine, sine_table)
    k_norm_grad = unrotate(k_rot_grad, cosine, sine_table)
    qgain_grad = jnp.sum(q_norm_grad * q_hat, axis=(0, 1))
    kgain_grad = jnp.sum(k_norm_grad * k_hat, axis=(0, 1))
    q_grad = (
        rms_back(q_norm_grad, q_raw, q_scale, query_gain)
        .astype(jnp.bfloat16)
        .reshape(length, q_heads * head_size)
    )
    k_grad = (
        rms_back(k_norm_grad, k_raw, k_scale, key_gain)
        .astype(jnp.bfloat16)
        .reshape(length, kv_heads * head_size)
    )
    v_grad = value_grad.reshape(length, kv_heads * head_size)
    query_w_grad = outer(normed_one, q_grad)
    key_w_grad = outer(normed_one, k_grad)
    value_w_grad = outer(normed_one, v_grad)
    one_partial = inner(q_grad, w_query) + inner(k_grad, w_key) + inner(v_grad, w_value)
    attn_part = jnp.sum(one_partial * tokens_wide * scale_one, axis=0)
    width = attn_part.shape[0]
    small = jnp.zeros((8, width), jnp.float32)
    small = small.at[0].set(ffn_grad).at[1].set(attn_part)
    small = small.at[2, :head_size].set(qgain_grad).at[2, head_size : 2 * head_size].set(kgain_grad)
    out_rows = out_w_grad.shape[0]
    dp_sums, one_partial = lax.optimization_barrier(
        (
            (
                query_w_grad,
                key_w_grad,
                value_w_grad,
                jnp.concatenate([out_w_grad, small]),
                gate_w_grad,
                up_w_grad,
                down_grad,
            ),
            one_partial,
        )
    )
    (
        query_w_grad,
        key_w_grad,
        value_w_grad,
        out_pack,
        gate_w_grad,
        up_w_grad,
        down_grad,
    ) = lax.psum(dp_sums, "dp")
    normed_one_grad = split_tensor_sum(one_partial)
    input_grad = residual_grad + rms_back(normed_one_grad, tokens_wide, scale_one, attn_gain)
    out_w_grad = out_pack[:out_rows]
    ffn_grad = out_pack[out_rows]
    gains = small_tensor_sum(out_pack[out_rows + 1 : out_rows + 3])
    attn_grad = gains[0]
    qgain_grad = gains[1, :head_size]
    kgain_grad = gains[1, head_size : 2 * head_size]
    return (
        output,
        input_grad,
        attn_grad,
        query_w_grad,
        key_w_grad,
        value_w_grad,
        qgain_grad,
        kgain_grad,
        out_w_grad,
        ffn_grad,
        gate_w_grad,
        up_w_grad,
        down_grad,
    )


def solution(mesh):
    from jax.sharding import Mesh

    dp_size, tensor_size = mesh.devices.shape
    split = Mesh(mesh.devices.reshape(dp_size, tensor_size // 2, 2), ("dp", "ty", "tx"))
    return jax.shard_map(
        per_device,
        mesh=split,
        in_specs=(
            P("dp", None),
            P("dp"),
            P(),
            P(None, TENSOR),
            P(None, TENSOR),
            P(None, TENSOR),
            P(),
            P(),
            P(TENSOR, None),
            P(),
            P(None, TENSOR),
            P(None, TENSOR),
            P(TENSOR, None),
            P("dp", None),
        ),
        out_specs=(
            P("dp", None),
            P("dp", None),
            P(),
            P(None, TENSOR),
            P(None, TENSOR),
            P(None, TENSOR),
            P(),
            P(),
            P(TENSOR, None),
            P(),
            P(None, TENSOR),
            P(None, TENSOR),
            P(TENSOR, None),
        ),
        check_vma=False,
    )
```

```python
import math

import jax
import jax.numpy as jnp
from jax import lax
from jax.sharding import PartitionSpec as P

EPS = 1e-05
THETA = 1000000.0
TENSOR = ("ty", "tx")


def outer(first_op, second_op):
    return lax.dot_general(
        first_op, second_op, (((0,), (0,)), ((), ())), preferred_element_type=jnp.float32
    )


def inner(first_op, second_op):
    return lax.dot_general(
        first_op, second_op, (((1,), (1,)), ((), ())), preferred_element_type=jnp.float32
    )


def rms_scale(values):
    return lax.rsqrt(jnp.mean(values * values, axis=-1, keepdims=True) + EPS)


def rms_back(upstream, values, inv_rms, gain_vec):
    normed = values * inv_rms
    weighted = upstream * gain_vec
    return inv_rms * (weighted - normed * jnp.mean(weighted * normed, axis=-1, keepdims=True))


def seq_layout(segment):
    length = segment.shape[0]
    ordinal = jnp.arange(length, dtype=jnp.int32)
    same_seq = segment[:, None] == segment[None, :]
    places = jnp.sum((same_seq & (ordinal[None, :] < ordinal[:, None])).astype(jnp.int32), axis=1)
    allowed = same_seq & (ordinal[None, :] <= ordinal[:, None])
    return (places, allowed)


def rope_tables(places, head_size):
    frequency = jnp.exp(
        jnp.arange(head_size // 2, dtype=jnp.float32) * (-2.0 * math.log(THETA) / head_size)
    )
    angles = places.astype(jnp.float32)[:, None] * frequency[None, :]
    angles = jnp.concatenate([angles, angles], axis=1)
    return (jnp.cos(angles), jnp.sin(angles))


def rotate(values, cosine, sine_table):
    half = values.shape[-1] // 2
    turned = jnp.concatenate([-values[..., half:], values[..., :half]], axis=-1)
    return values * cosine[:, None, :] + turned * sine_table[:, None, :]


def unrotate(incoming, cosine, sine_table):
    half = incoming.shape[-1] // 2
    scaled = incoming * sine_table[:, None, :]
    swapped = jnp.concatenate([scaled[..., half:], -scaled[..., :half]], axis=-1)
    return incoming * cosine[:, None, :] + swapped


def score_table(q_rot, k_rot, allowed, factor):
    raw = jnp.einsum("ikgd,jkd->kgij", q_rot, k_rot, preferred_element_type=jnp.float32) * factor
    return jnp.where(allowed[None, None], raw, -1e30)


def ring(size, shift):
    return [(i, (i + shift) % size) for i in range(size)]


def tensor_sum(values, extra=None):
    rows, cols = values.shape
    ny = lax.axis_size("ty")
    nx = lax.axis_size("tx")
    y = lax.axis_index("ty")
    h = lax.axis_index("tx")
    leaf = rows // (2 * ny * nx)
    parts = values.reshape(2, ny, nx, leaf, cols)
    pairs = ring(nx, 1)
    total = extra
    accs = []
    for way, shift in ((0, 1), (1, -1)):
        chunks = parts[way]
        acc = lax.dynamic_index_in_dim(chunks, (y - shift) % ny, 0, keepdims=False)
        passing = extra
        for step in range(1, ny):
            if way == 0 and extra is not None:
                acc, passing = lax.ppermute((acc, passing), "ty", ring(ny, shift))
                total = total + passing
            else:
                acc = lax.ppermute(acc, "ty", ring(ny, shift))
            acc = acc + lax.dynamic_index_in_dim(chunks, (y - shift * (1 + step)) % ny, 0, keepdims=False)
        accs.append(acc)
    acc = jnp.stack(accs)
    keep = lax.dynamic_index_in_dim(acc, h, 1, keepdims=False)
    send = lax.dynamic_index_in_dim(acc, (h + 1) % nx, 1, keepdims=False)
    if extra is not None:
        got, got_total = lax.ppermute((send, total), "tx", pairs)
        total = total + got_total
    else:
        got = lax.ppermute(send, "tx", pairs)
    mine = keep + got
    other = lax.ppermute(mine, "tx", pairs)
    both = jnp.where(h == 0, jnp.stack([mine, other], 1), jnp.stack([other, mine], 1))
    outs = []
    for way, shift in ((0, 1), (1, -1)):
        cur = both[way]
        gathered = jnp.zeros((ny,) + cur.shape, values.dtype)
        gathered = lax.dynamic_update_index_in_dim(gathered, cur, y, 0)
        for step in range(1, ny):
            cur = lax.ppermute(cur, "ty", ring(ny, shift))
            gathered = lax.dynamic_update_index_in_dim(gathered, cur, (y - shift * step) % ny, 0)
        outs.append(gathered)
    result = jnp.stack(outs).reshape(rows, cols)
    if extra is None:
        return result
    return result, total


def split_tensor_sum(values, pieces=2):
    blocks = jnp.split(values, pieces, axis=0)
    return jnp.concatenate([tensor_sum(block) for block in blocks], axis=0)


def small_tensor_sum(values):
    ny = lax.axis_size("ty")
    nx = lax.axis_size("tx")
    dist = 1
    while dist < ny:
        values = values + lax.ppermute(values, "ty", [(i, i ^ dist) for i in range(ny)])
        dist *= 2
    dist = 1
    while dist < nx:
        values = values + lax.ppermute(values, "tx", [(i, i ^ dist) for i in range(nx)])
        dist *= 2
    return values


def per_device(
    tokens,
    segment_ids,
    attn_gain,
    w_query,
    w_key,
    w_value,
    query_gain,
    key_gain,
    w_out,
    ffn_gain,
    w_gate,
    w_up,
    w_down,
    cotangent,
):
    length = tokens.shape[0]
    head_size = query_gain.shape[0]
    q_heads = w_query.shape[1] // head_size
    kv_heads = w_key.shape[1] // head_size
    groups = q_heads // kv_heads
    factor = 1.0 / math.sqrt(head_size)
    places, allowed = seq_layout(segment_ids)
    cosine, sine_table = rope_tables(places, head_size)
    tokens_wide = tokens.astype(jnp.float32)
    scale_one = rms_scale(tokens_wide)
    normed_one = (tokens_wide * scale_one * attn_gain).astype(jnp.bfloat16)
    q_raw = jnp.dot(normed_one, w_query, preferred_element_type=jnp.float32).reshape(
        length, q_heads, head_size
    )
    k_raw = jnp.dot(normed_one, w_key, preferred_element_type=jnp.float32).reshape(
        length, kv_heads, head_size
    )
    v_half = (
        jnp.dot(normed_one, w_value, preferred_element_type=jnp.float32)
        .astype(jnp.bfloat16)
        .reshape(length, kv_heads, head_size)
    )
    q_scale = rms_scale(q_raw)
    k_scale = rms_scale(k_raw)
    q_hat = q_raw * q_scale
    k_hat = k_raw * k_scale
    q_rot = (
        rotate(q_hat * query_gain, cosine, sine_table)
        .astype(jnp.bfloat16)
        .reshape(length, kv_heads, groups, head_size)
    )
    k_rot = rotate(k_hat * key_gain, cosine, sine_table).astype(jnp.bfloat16)
    scores = score_table(q_rot, k_rot, allowed, factor)
    row_peak = jnp.max(scores, axis=-1, keepdims=True)
    log_total = row_peak + jnp.log(jnp.sum(jnp.exp(scores - row_peak), axis=-1, keepdims=True))
    attn_probs = jnp.exp(scores - log_total).astype(jnp.bfloat16)
    attn_mixed = jnp.einsum(
        "kgij,jkd->ikgd", attn_probs, v_half, preferred_element_type=jnp.float32
    )
    attn_mixed = attn_mixed.reshape(length, q_heads * head_size).astype(jnp.bfloat16)
    attn_sum = split_tensor_sum(jnp.dot(attn_mixed, w_out, preferred_element_type=jnp.float32))
    residual = tokens_wide + attn_sum
    scale_two = rms_scale(residual)
    normed_two = (residual * scale_two * ffn_gain).astype(jnp.bfloat16)
    gate_proj = jnp.dot(normed_two, w_gate, preferred_element_type=jnp.float32)
    up_proj = jnp.dot(normed_two, w_up, preferred_element_type=jnp.float32)
    gate_sigmoid = jax.nn.sigmoid(gate_proj)
    hidden = (gate_proj * gate_sigmoid * up_proj).astype(jnp.bfloat16)
    mlp_sum = split_tensor_sum(jnp.dot(hidden, w_down, preferred_element_type=jnp.float32))
    output = (residual + mlp_sum).astype(jnp.bfloat16)
    down_grad = outer(hidden, cotangent)
    hidden_grad = inner(cotangent, w_down)
    gate_grad = (
        hidden_grad * up_proj * gate_sigmoid * (1.0 + gate_proj * (1.0 - gate_sigmoid))
    ).astype(jnp.bfloat16)
    up_grad = (hidden_grad * gate_proj * gate_sigmoid).astype(jnp.bfloat16)
    gate_w_grad = outer(normed_two, gate_grad)
    up_w_grad = outer(normed_two, up_grad)
    ffn_w_grads, two_partial = lax.optimization_barrier(
        ((down_grad, gate_w_grad, up_w_grad), inner(gate_grad, w_gate) + inner(up_grad, w_up))
    )
    ffn_w_grads = lax.psum(ffn_w_grads, "dp")
    normed_two_grad = split_tensor_sum(two_partial)
    ffn_grad = jnp.sum(normed_two_grad * residual * scale_two, axis=0)
    residual_grad = cotangent.astype(jnp.float32) + rms_back(
        normed_two_grad, residual, scale_two, ffn_gain
    )
    residual_half = residual_grad.astype(jnp.bfloat16)
    out_w_grad = outer(attn_mixed, residual_half)
    mixed_grad = (
        inner(residual_half, w_out)
        .astype(jnp.bfloat16)
        .reshape(length, kv_heads, groups, head_size)
    )
    attn_full = jnp.exp(score_table(q_rot, k_rot, allowed, factor) - log_total)
    probs_half = attn_full.astype(jnp.bfloat16)
    value_grad = jnp.einsum(
        "kgij,ikgd->jkd", probs_half, mixed_grad, preferred_element_type=jnp.float32
    ).astype(jnp.bfloat16)
    prob_grad = jnp.einsum("ikgd,jkd->kgij", mixed_grad, v_half, preferred_element_type=jnp.float32)
    row_delta = jnp.sum(attn_full * prob_grad, axis=-1, keepdims=True)
    score_grad = (attn_full * (prob_grad - row_delta) * factor).astype(jnp.bfloat16)
    q_rot_grad = jnp.einsum(
        "kgij,jkd->ikgd", score_grad, k_rot, preferred_element_type=jnp.float32
    ).reshape(length, q_heads, head_size)
    k_rot_grad = jnp.einsum("kgij,ikgd->jkd", score_grad, q_rot, preferred_element_type=jnp.float32)
    q_norm_grad = unrotate(q_rot_grad, cosine, sine_table)
    k_norm_grad = unrotate(k_rot_grad, cosine, sine_table)
    qgain_grad = jnp.sum(q_norm_grad * q_hat, axis=(0, 1))
    kgain_grad = jnp.sum(k_norm_grad * k_hat, axis=(0, 1))
    q_grad = (
        rms_back(q_norm_grad, q_raw, q_scale, query_gain)
        .astype(jnp.bfloat16)
        .reshape(length, q_heads * head_size)
    )
    k_grad = (
        rms_back(k_norm_grad, k_raw, k_scale, key_gain)
        .astype(jnp.bfloat16)
        .reshape(length, kv_heads * head_size)
    )
    v_grad = value_grad.reshape(length, kv_heads * head_size)
    query_w_grad = outer(normed_one, q_grad)
    key_w_grad = outer(normed_one, k_grad)
    value_w_grad = outer(normed_one, v_grad)
    one_partial = inner(q_grad, w_query) + inner(k_grad, w_key) + inner(v_grad, w_value)
    attn_part = jnp.sum(one_partial * tokens_wide * scale_one, axis=0)
    width = attn_part.shape[0]
    small = jnp.zeros((8, width), jnp.float32)
    small = small.at[0].set(ffn_grad).at[1].set(attn_part)
    small = small.at[2, :head_size].set(qgain_grad).at[2, head_size : 2 * head_size].set(kgain_grad)
    out_rows = out_w_grad.shape[0]
    ffn_w_grads, dp_sums, one_partial = lax.optimization_barrier(
        (
            ffn_w_grads,
            (query_w_grad, key_w_grad, value_w_grad, jnp.concatenate([out_w_grad, small])),
            one_partial,
        )
    )
    query_w_grad, key_w_grad, value_w_grad, out_pack = lax.psum(dp_sums, "dp")
    down_grad, gate_w_grad, up_w_grad = ffn_w_grads
    normed_one_grad = split_tensor_sum(one_partial)
    input_grad = residual_grad + rms_back(normed_one_grad, tokens_wide, scale_one, attn_gain)
    out_w_grad = out_pack[:out_rows]
    ffn_grad = out_pack[out_rows]
    gains = small_tensor_sum(out_pack[out_rows + 1 : out_rows + 3])
    attn_grad = gains[0]
    qgain_grad = gains[1, :head_size]
    kgain_grad = gains[1, head_size : 2 * head_size]
    return (
        output,
        input_grad,
        attn_grad,
        query_w_grad,
        key_w_grad,
        value_w_grad,
        qgain_grad,
        kgain_grad,
        out_w_grad,
        ffn_grad,
        gate_w_grad,
        up_w_grad,
        down_grad,
    )


def solution(mesh):
    from jax.sharding import Mesh

    dp_size, tensor_size = mesh.devices.shape
    split = Mesh(mesh.devices.reshape(dp_size, tensor_size // 2, 2), ("dp", "ty", "tx"))
    return jax.shard_map(
        per_device,
        mesh=split,
        in_specs=(
            P("dp", None),
            P("dp"),
            P(),
            P(None, TENSOR),
            P(None, TENSOR),
            P(None, TENSOR),
            P(),
            P(),
            P(TENSOR, None),
            P(),
            P(None, TENSOR),
            P(None, TENSOR),
            P(TENSOR, None),
            P("dp", None),
        ),
        out_specs=(
            P("dp", None),
            P("dp", None),
            P(),
            P(None, TENSOR),
            P(None, TENSOR),
            P(None, TENSOR),
            P(),
            P(),
            P(TENSOR, None),
            P(),
            P(None, TENSOR),
            P(None, TENSOR),
            P(TENSOR, None),
        ),
        check_vma=False,
    )
```

```python
import math

import jax
import jax.numpy as jnp
from jax import lax
from jax.sharding import PartitionSpec as P

EPS = 1e-05
THETA = 1000000.0
TENSOR = ("ty", "tx")
DP = ("dx", "dz", "dc")


def outer(first_op, second_op):
    return lax.dot_general(
        first_op, second_op, (((0,), (0,)), ((), ())), preferred_element_type=jnp.float32
    )


def inner(first_op, second_op):
    return lax.dot_general(
        first_op, second_op, (((1,), (1,)), ((), ())), preferred_element_type=jnp.float32
    )


def rms_scale(values):
    return lax.rsqrt(jnp.mean(values * values, axis=-1, keepdims=True) + EPS)


def rms_back(upstream, values, inv_rms, gain_vec):
    normed = values * inv_rms
    weighted = upstream * gain_vec
    return inv_rms * (weighted - normed * jnp.mean(weighted * normed, axis=-1, keepdims=True))


def seq_layout(segment):
    length = segment.shape[0]
    ordinal = jnp.arange(length, dtype=jnp.int32)
    same_seq = segment[:, None] == segment[None, :]
    places = jnp.sum((same_seq & (ordinal[None, :] < ordinal[:, None])).astype(jnp.int32), axis=1)
    allowed = same_seq & (ordinal[None, :] <= ordinal[:, None])
    return (places, allowed)


def rope_tables(places, head_size):
    frequency = jnp.exp(
        jnp.arange(head_size // 2, dtype=jnp.float32) * (-2.0 * math.log(THETA) / head_size)
    )
    angles = places.astype(jnp.float32)[:, None] * frequency[None, :]
    angles = jnp.concatenate([angles, angles], axis=1)
    return (jnp.cos(angles), jnp.sin(angles))


def rotate(values, cosine, sine_table):
    half = values.shape[-1] // 2
    turned = jnp.concatenate([-values[..., half:], values[..., :half]], axis=-1)
    return values * cosine[:, None, :] + turned * sine_table[:, None, :]


def unrotate(incoming, cosine, sine_table):
    half = incoming.shape[-1] // 2
    scaled = incoming * sine_table[:, None, :]
    swapped = jnp.concatenate([scaled[..., half:], -scaled[..., :half]], axis=-1)
    return incoming * cosine[:, None, :] + swapped


def score_table(q_rot, k_rot, allowed, factor):
    raw = jnp.einsum("ikgd,jkd->kgij", q_rot, k_rot, preferred_element_type=jnp.float32) * factor
    return jnp.where(allowed[None, None], raw, -1e30)


def ring(size, shift):
    return [(i, (i + shift) % size) for i in range(size)]


def tensor_sum(values, extra=None):
    rows, cols = values.shape
    ny = lax.axis_size("ty")
    nx = lax.axis_size("tx")
    y = lax.axis_index("ty")
    h = lax.axis_index("tx")
    leaf = rows // (2 * ny * nx)
    parts = values.reshape(2, ny, nx, leaf, cols)
    pairs = ring(nx, 1)
    total = extra
    accs = []
    for way, shift in ((0, 1), (1, -1)):
        chunks = parts[way]
        acc = lax.dynamic_index_in_dim(chunks, (y - shift) % ny, 0, keepdims=False)
        passing = extra
        for step in range(1, ny):
            if way == 0 and extra is not None:
                acc, passing = lax.ppermute((acc, passing), "ty", ring(ny, shift))
                total = total + passing
            else:
                acc = lax.ppermute(acc, "ty", ring(ny, shift))
            acc = acc + lax.dynamic_index_in_dim(chunks, (y - shift * (1 + step)) % ny, 0, keepdims=False)
        accs.append(acc)
    acc = jnp.stack(accs)
    keep = lax.dynamic_index_in_dim(acc, h, 1, keepdims=False)
    send = lax.dynamic_index_in_dim(acc, (h + 1) % nx, 1, keepdims=False)
    if extra is not None:
        got, got_total = lax.ppermute((send, total), "tx", pairs)
        total = total + got_total
    else:
        got = lax.ppermute(send, "tx", pairs)
    mine = keep + got
    other = lax.ppermute(mine, "tx", pairs)
    both = jnp.where(h == 0, jnp.stack([mine, other], 1), jnp.stack([other, mine], 1))
    outs = []
    for way, shift in ((0, 1), (1, -1)):
        cur = both[way]
        gathered = jnp.zeros((ny,) + cur.shape, values.dtype)
        gathered = lax.dynamic_update_index_in_dim(gathered, cur, y, 0)
        for step in range(1, ny):
            cur = lax.ppermute(cur, "ty", ring(ny, shift))
            gathered = lax.dynamic_update_index_in_dim(gathered, cur, (y - shift * step) % ny, 0)
        outs.append(gathered)
    result = jnp.stack(outs).reshape(rows, cols)
    if extra is None:
        return result
    return result, total


def split_tensor_sum(values, pieces=2):
    blocks = jnp.split(values, pieces, axis=0)
    return jnp.concatenate([tensor_sum(block) for block in blocks], axis=0)


def ring_sum(values, ring_axis, pair_axes):
    rows, cols = values.shape
    size = lax.axis_size(ring_axis)
    here = lax.axis_index(ring_axis)
    parts = values.reshape(2, size, rows // (2 * size), cols)
    accs = []
    for way, shift in ((0, 1), (1, -1)):
        chunks = parts[way]
        acc = lax.dynamic_index_in_dim(chunks, (here - shift) % size, 0, keepdims=False)
        for step in range(1, size):
            acc = lax.ppermute(acc, ring_axis, ring(size, shift))
            acc = acc + lax.dynamic_index_in_dim(chunks, (here - shift * (1 + step)) % size, 0, keepdims=False)
        accs.append(acc)
    acc = jnp.stack(accs)
    sides = []
    for axis in pair_axes:
        side = lax.axis_index(axis)
        halves = acc.reshape(2, 2, acc.shape[1] // 2, cols)
        keep = lax.dynamic_index_in_dim(halves, side, 1, keepdims=False)
        send = lax.dynamic_index_in_dim(halves, 1 - side, 1, keepdims=False)
        acc = keep + lax.ppermute(send, axis, [(0, 1), (1, 0)])
        sides.append(side)
    for axis, side in zip(pair_axes[::-1], sides[::-1]):
        other = lax.ppermute(acc, axis, [(0, 1), (1, 0)])
        both = jnp.where(side == 0, jnp.stack([acc, other], 1), jnp.stack([other, acc], 1))
        acc = both.reshape(2, 2 * acc.shape[1], cols)
    outs = []
    for way, shift in ((0, 1), (1, -1)):
        cur = acc[way]
        gathered = jnp.zeros((size,) + cur.shape, values.dtype)
        gathered = lax.dynamic_update_index_in_dim(gathered, cur, here, 0)
        for step in range(1, size):
            cur = lax.ppermute(cur, ring_axis, ring(size, shift))
            gathered = lax.dynamic_update_index_in_dim(gathered, cur, (here - shift * step) % size, 0)
        outs.append(gathered)
    return jnp.stack(outs).reshape(rows, cols)


def small_tensor_sum(values):
    ny = lax.axis_size("ty")
    nx = lax.axis_size("tx")
    dist = 1
    while dist < ny:
        values = values + lax.ppermute(values, "ty", [(i, i ^ dist) for i in range(ny)])
        dist *= 2
    dist = 1
    while dist < nx:
        values = values + lax.ppermute(values, "tx", [(i, i ^ dist) for i in range(nx)])
        dist *= 2
    return values


def per_device(
    tokens,
    segment_ids,
    attn_gain,
    w_query,
    w_key,
    w_value,
    query_gain,
    key_gain,
    w_out,
    ffn_gain,
    w_gate,
    w_up,
    w_down,
    cotangent,
):
    length = tokens.shape[0]
    head_size = query_gain.shape[0]
    q_heads = w_query.shape[1] // head_size
    kv_heads = w_key.shape[1] // head_size
    groups = q_heads // kv_heads
    factor = 1.0 / math.sqrt(head_size)
    places, allowed = seq_layout(segment_ids)
    cosine, sine_table = rope_tables(places, head_size)
    tokens_wide = tokens.astype(jnp.float32)
    scale_one = rms_scale(tokens_wide)
    normed_one = (tokens_wide * scale_one * attn_gain).astype(jnp.bfloat16)
    q_raw = jnp.dot(normed_one, w_query, preferred_element_type=jnp.float32).reshape(
        length, q_heads, head_size
    )
    k_raw = jnp.dot(normed_one, w_key, preferred_element_type=jnp.float32).reshape(
        length, kv_heads, head_size
    )
    v_half = (
        jnp.dot(normed_one, w_value, preferred_element_type=jnp.float32)
        .astype(jnp.bfloat16)
        .reshape(length, kv_heads, head_size)
    )
    q_scale = rms_scale(q_raw)
    k_scale = rms_scale(k_raw)
    q_hat = q_raw * q_scale
    k_hat = k_raw * k_scale
    q_rot = (
        rotate(q_hat * query_gain, cosine, sine_table)
        .astype(jnp.bfloat16)
        .reshape(length, kv_heads, groups, head_size)
    )
    k_rot = rotate(k_hat * key_gain, cosine, sine_table).astype(jnp.bfloat16)
    scores = score_table(q_rot, k_rot, allowed, factor)
    row_peak = jnp.max(scores, axis=-1, keepdims=True)
    log_total = row_peak + jnp.log(jnp.sum(jnp.exp(scores - row_peak), axis=-1, keepdims=True))
    attn_probs = jnp.exp(scores - log_total).astype(jnp.bfloat16)
    attn_mixed = jnp.einsum(
        "kgij,jkd->ikgd", attn_probs, v_half, preferred_element_type=jnp.float32
    )
    attn_mixed = attn_mixed.reshape(length, q_heads * head_size).astype(jnp.bfloat16)
    attn_sum = split_tensor_sum(jnp.dot(attn_mixed, w_out, preferred_element_type=jnp.float32))
    residual = tokens_wide + attn_sum
    scale_two = rms_scale(residual)
    normed_two = (residual * scale_two * ffn_gain).astype(jnp.bfloat16)
    gate_proj = jnp.dot(normed_two, w_gate, preferred_element_type=jnp.float32)
    up_proj = jnp.dot(normed_two, w_up, preferred_element_type=jnp.float32)
    gate_sigmoid = jax.nn.sigmoid(gate_proj)
    hidden = (gate_proj * gate_sigmoid * up_proj).astype(jnp.bfloat16)
    mlp_sum = split_tensor_sum(jnp.dot(hidden, w_down, preferred_element_type=jnp.float32))
    output = (residual + mlp_sum).astype(jnp.bfloat16)
    down_grad = outer(hidden, cotangent)
    hidden_grad = inner(cotangent, w_down)
    gate_grad = (
        hidden_grad * up_proj * gate_sigmoid * (1.0 + gate_proj * (1.0 - gate_sigmoid))
    ).astype(jnp.bfloat16)
    up_grad = (hidden_grad * gate_proj * gate_sigmoid).astype(jnp.bfloat16)
    gate_w_grad = outer(normed_two, gate_grad)
    up_w_grad = outer(normed_two, up_grad)
    ffn_w_grads, two_partial = lax.optimization_barrier(
        ((down_grad, gate_w_grad, up_w_grad), inner(gate_grad, w_gate) + inner(up_grad, w_up))
    )
    ffn_w_grads = lax.psum(ffn_w_grads, DP)
    normed_two_grad = split_tensor_sum(two_partial)
    ffn_grad = jnp.sum(normed_two_grad * residual * scale_two, axis=0)
    residual_grad = cotangent.astype(jnp.float32) + rms_back(
        normed_two_grad, residual, scale_two, ffn_gain
    )
    residual_half = residual_grad.astype(jnp.bfloat16)
    out_w_grad = outer(attn_mixed, residual_half)
    mixed_grad = (
        inner(residual_half, w_out)
        .astype(jnp.bfloat16)
        .reshape(length, kv_heads, groups, head_size)
    )
    attn_full = jnp.exp(score_table(q_rot, k_rot, allowed, factor) - log_total)
    probs_half = attn_full.astype(jnp.bfloat16)
    value_grad = jnp.einsum(
        "kgij,ikgd->jkd", probs_half, mixed_grad, preferred_element_type=jnp.float32
    ).astype(jnp.bfloat16)
    prob_grad = jnp.einsum("ikgd,jkd->kgij", mixed_grad, v_half, preferred_element_type=jnp.float32)
    row_delta = jnp.sum(attn_full * prob_grad, axis=-1, keepdims=True)
    score_grad = (attn_full * (prob_grad - row_delta) * factor).astype(jnp.bfloat16)
    q_rot_grad = jnp.einsum(
        "kgij,jkd->ikgd", score_grad, k_rot, preferred_element_type=jnp.float32
    ).reshape(length, q_heads, head_size)
    k_rot_grad = jnp.einsum("kgij,ikgd->jkd", score_grad, q_rot, preferred_element_type=jnp.float32)
    q_norm_grad = unrotate(q_rot_grad, cosine, sine_table)
    k_norm_grad = unrotate(k_rot_grad, cosine, sine_table)
    qgain_grad = jnp.sum(q_norm_grad * q_hat, axis=(0, 1))
    kgain_grad = jnp.sum(k_norm_grad * k_hat, axis=(0, 1))
    q_grad = (
        rms_back(q_norm_grad, q_raw, q_scale, query_gain)
        .astype(jnp.bfloat16)
        .reshape(length, q_heads * head_size)
    )
    k_grad = (
        rms_back(k_norm_grad, k_raw, k_scale, key_gain)
        .astype(jnp.bfloat16)
        .reshape(length, kv_heads * head_size)
    )
    v_grad = value_grad.reshape(length, kv_heads * head_size)
    query_w_grad = outer(normed_one, q_grad)
    key_w_grad = outer(normed_one, k_grad)
    value_w_grad = outer(normed_one, v_grad)
    one_partial = inner(q_grad, w_query) + inner(k_grad, w_key) + inner(v_grad, w_value)
    attn_part = jnp.sum(one_partial * tokens_wide * scale_one, axis=0)
    width = attn_part.shape[0]
    small = jnp.zeros((8, width), jnp.float32)
    small = small.at[0].set(ffn_grad).at[1].set(attn_part)
    small = small.at[2, :head_size].set(qgain_grad).at[2, head_size : 2 * head_size].set(kgain_grad)
    out_rows = out_w_grad.shape[0]
    ffn_w_grads, dp_sums, one_partial = lax.optimization_barrier(
        (
            ffn_w_grads,
            (query_w_grad, key_w_grad, value_w_grad, jnp.concatenate([out_w_grad, small])),
            one_partial,
        )
    )
    query_w_grad, key_w_grad, value_w_grad, out_pack = dp_sums
    q_cols = query_w_grad.shape[1]
    k_cols = key_w_grad.shape[1]
    width = out_pack.shape[1]
    flat = jnp.concatenate([query_w_grad, key_w_grad, value_w_grad], axis=1).reshape(-1, width)
    flat_rows = flat.shape[0]
    packed = jnp.concatenate([flat, out_pack], axis=0)
    padded_rows = -(-packed.shape[0] // 256) * 256
    packed = jnp.pad(packed, ((0, padded_rows - packed.shape[0]), (0, 0)))
    packed = ring_sum(packed, "dz", ("dc", "dx"))
    flat = packed[:flat_rows].reshape(query_w_grad.shape[0], -1)
    query_w_grad = flat[:, :q_cols]
    key_w_grad = flat[:, q_cols : q_cols + k_cols]
    value_w_grad = flat[:, q_cols + k_cols :]
    out_pack = packed[flat_rows : flat_rows + out_pack.shape[0]]
    down_grad, gate_w_grad, up_w_grad = ffn_w_grads
    normed_one_grad = split_tensor_sum(one_partial)
    input_grad = residual_grad + rms_back(normed_one_grad, tokens_wide, scale_one, attn_gain)
    out_w_grad = out_pack[:out_rows]
    ffn_grad = out_pack[out_rows]
    gains = small_tensor_sum(out_pack[out_rows + 1 : out_rows + 3])
    attn_grad = gains[0]
    qgain_grad = gains[1, :head_size]
    kgain_grad = gains[1, head_size : 2 * head_size]
    return (
        output,
        input_grad,
        attn_grad,
        query_w_grad,
        key_w_grad,
        value_w_grad,
        qgain_grad,
        kgain_grad,
        out_w_grad,
        ffn_grad,
        gate_w_grad,
        up_w_grad,
        down_grad,
    )


def solution(mesh):
    from jax.sharding import Mesh

    dp_size, tensor_size = mesh.devices.shape
    split = Mesh(
        mesh.devices.reshape(2, dp_size // 4, 2, tensor_size // 2, 2), DP + TENSOR
    )
    return jax.shard_map(
        per_device,
        mesh=split,
        in_specs=(
            P(DP, None),
            P(DP),
            P(),
            P(None, TENSOR),
            P(None, TENSOR),
            P(None, TENSOR),
            P(),
            P(),
            P(TENSOR, None),
            P(),
            P(None, TENSOR),
            P(None, TENSOR),
            P(TENSOR, None),
            P(DP, None),
        ),
        out_specs=(
            P(DP, None),
            P(DP, None),
            P(),
            P(None, TENSOR),
            P(None, TENSOR),
            P(None, TENSOR),
            P(),
            P(),
            P(TENSOR, None),
            P(),
            P(None, TENSOR),
            P(None, TENSOR),
            P(TENSOR, None),
        ),
        check_vma=False,
    )
```

```python
import math

import jax
import jax.numpy as jnp
from jax import lax
from jax.sharding import PartitionSpec as P

EPS = 1e-05
THETA = 1000000.0
TENSOR = ("ty", "tx")
DP = ("dx", "dz", "dc")


def outer(first_op, second_op):
    return lax.dot_general(
        first_op, second_op, (((0,), (0,)), ((), ())), preferred_element_type=jnp.float32
    )


def inner(first_op, second_op):
    return lax.dot_general(
        first_op, second_op, (((1,), (1,)), ((), ())), preferred_element_type=jnp.float32
    )


def rms_scale(values):
    return lax.rsqrt(jnp.mean(values * values, axis=-1, keepdims=True) + EPS)


def rms_back(upstream, values, inv_rms, gain_vec):
    normed = values * inv_rms
    weighted = upstream * gain_vec
    return inv_rms * (weighted - normed * jnp.mean(weighted * normed, axis=-1, keepdims=True))


def seq_layout(segment):
    length = segment.shape[0]
    ordinal = jnp.arange(length, dtype=jnp.int32)
    same_seq = segment[:, None] == segment[None, :]
    places = jnp.sum((same_seq & (ordinal[None, :] < ordinal[:, None])).astype(jnp.int32), axis=1)
    allowed = same_seq & (ordinal[None, :] <= ordinal[:, None])
    return (places, allowed)


def rope_tables(places, head_size):
    frequency = jnp.exp(
        jnp.arange(head_size // 2, dtype=jnp.float32) * (-2.0 * math.log(THETA) / head_size)
    )
    angles = places.astype(jnp.float32)[:, None] * frequency[None, :]
    angles = jnp.concatenate([angles, angles], axis=1)
    return (jnp.cos(angles), jnp.sin(angles))


def rotate(values, cosine, sine_table):
    half = values.shape[-1] // 2
    turned = jnp.concatenate([-values[..., half:], values[..., :half]], axis=-1)
    return values * cosine[:, None, :] + turned * sine_table[:, None, :]


def unrotate(incoming, cosine, sine_table):
    half = incoming.shape[-1] // 2
    scaled = incoming * sine_table[:, None, :]
    swapped = jnp.concatenate([scaled[..., half:], -scaled[..., :half]], axis=-1)
    return incoming * cosine[:, None, :] + swapped


def score_table(q_rot, k_rot, allowed, factor):
    raw = jnp.einsum("ikgd,jkd->kgij", q_rot, k_rot, preferred_element_type=jnp.float32) * factor
    return jnp.where(allowed[None, None], raw, -1e30)


def ring(size, shift):
    return [(i, (i + shift) % size) for i in range(size)]


def tensor_sum(values, extra=None):
    rows, cols = values.shape
    ny = lax.axis_size("ty")
    nx = lax.axis_size("tx")
    y = lax.axis_index("ty")
    h = lax.axis_index("tx")
    leaf = rows // (2 * ny * nx)
    parts = values.reshape(2, ny, nx, leaf, cols)
    pairs = ring(nx, 1)
    total = extra
    accs = []
    for way, shift in ((0, 1), (1, -1)):
        chunks = parts[way]
        acc = lax.dynamic_index_in_dim(chunks, (y - shift) % ny, 0, keepdims=False)
        passing = extra
        for step in range(1, ny):
            if way == 0 and extra is not None:
                acc, passing = lax.ppermute((acc, passing), "ty", ring(ny, shift))
                total = total + passing
            else:
                acc = lax.ppermute(acc, "ty", ring(ny, shift))
            acc = acc + lax.dynamic_index_in_dim(chunks, (y - shift * (1 + step)) % ny, 0, keepdims=False)
        accs.append(acc)
    acc = jnp.stack(accs)
    keep = lax.dynamic_index_in_dim(acc, h, 1, keepdims=False)
    send = lax.dynamic_index_in_dim(acc, (h + 1) % nx, 1, keepdims=False)
    if extra is not None:
        got, got_total = lax.ppermute((send, total), "tx", pairs)
        total = total + got_total
    else:
        got = lax.ppermute(send, "tx", pairs)
    mine = keep + got
    other = lax.ppermute(mine, "tx", pairs)
    both = jnp.where(h == 0, jnp.stack([mine, other], 1), jnp.stack([other, mine], 1))
    outs = []
    for way, shift in ((0, 1), (1, -1)):
        cur = both[way]
        gathered = jnp.zeros((ny,) + cur.shape, values.dtype)
        gathered = lax.dynamic_update_index_in_dim(gathered, cur, y, 0)
        for step in range(1, ny):
            cur = lax.ppermute(cur, "ty", ring(ny, shift))
            gathered = lax.dynamic_update_index_in_dim(gathered, cur, (y - shift * step) % ny, 0)
        outs.append(gathered)
    result = jnp.stack(outs).reshape(rows, cols)
    if extra is None:
        return result
    return result, total


def split_tensor_sum(values, pieces=2):
    blocks = jnp.split(values, pieces, axis=0)
    return jnp.concatenate([tensor_sum(block) for block in blocks], axis=0)


def ring_sum(values, ring_axis, pair_axes):
    rows, cols = values.shape
    size = lax.axis_size(ring_axis)
    here = lax.axis_index(ring_axis)
    parts = values.reshape(2, size, rows // (2 * size), cols)
    accs = []
    for way, shift in ((0, 1), (1, -1)):
        chunks = parts[way]
        acc = lax.dynamic_index_in_dim(chunks, (here - shift) % size, 0, keepdims=False)
        for step in range(1, size):
            acc = lax.ppermute(acc, ring_axis, ring(size, shift))
            acc = acc + lax.dynamic_index_in_dim(chunks, (here - shift * (1 + step)) % size, 0, keepdims=False)
        accs.append(acc)
    acc = jnp.stack(accs)
    sides = []
    for axis in pair_axes:
        side = lax.axis_index(axis)
        halves = acc.reshape(2, 2, acc.shape[1] // 2, cols)
        keep = lax.dynamic_index_in_dim(halves, side, 1, keepdims=False)
        send = lax.dynamic_index_in_dim(halves, 1 - side, 1, keepdims=False)
        acc = keep + lax.ppermute(send, axis, [(0, 1), (1, 0)])
        sides.append(side)
    for axis, side in zip(pair_axes[::-1], sides[::-1]):
        other = lax.ppermute(acc, axis, [(0, 1), (1, 0)])
        both = jnp.where(side == 0, jnp.stack([acc, other], 1), jnp.stack([other, acc], 1))
        acc = both.reshape(2, 2 * acc.shape[1], cols)
    outs = []
    for way, shift in ((0, 1), (1, -1)):
        cur = acc[way]
        gathered = jnp.zeros((size,) + cur.shape, values.dtype)
        gathered = lax.dynamic_update_index_in_dim(gathered, cur, here, 0)
        for step in range(1, size):
            cur = lax.ppermute(cur, ring_axis, ring(size, shift))
            gathered = lax.dynamic_update_index_in_dim(gathered, cur, (here - shift * step) % size, 0)
        outs.append(gathered)
    return jnp.stack(outs).reshape(rows, cols)


def small_tensor_sum(values):
    ny = lax.axis_size("ty")
    nx = lax.axis_size("tx")
    dist = 1
    while dist < ny:
        values = values + lax.ppermute(values, "ty", [(i, i ^ dist) for i in range(ny)])
        dist *= 2
    dist = 1
    while dist < nx:
        values = values + lax.ppermute(values, "tx", [(i, i ^ dist) for i in range(nx)])
        dist *= 2
    return values


def per_device(
    tokens,
    segment_ids,
    attn_gain,
    w_query,
    w_key,
    w_value,
    query_gain,
    key_gain,
    w_out,
    ffn_gain,
    w_gate,
    w_up,
    w_down,
    cotangent,
):
    length = tokens.shape[0]
    head_size = query_gain.shape[0]
    q_heads = w_query.shape[1] // head_size
    kv_heads = w_key.shape[1] // head_size
    groups = q_heads // kv_heads
    factor = 1.0 / math.sqrt(head_size)
    places, allowed = seq_layout(segment_ids)
    cosine, sine_table = rope_tables(places, head_size)
    tokens_wide = tokens.astype(jnp.float32)
    scale_one = rms_scale(tokens_wide)
    normed_one = (tokens_wide * scale_one * attn_gain).astype(jnp.bfloat16)
    q_raw = jnp.dot(normed_one, w_query, preferred_element_type=jnp.float32).reshape(
        length, q_heads, head_size
    )
    k_raw = jnp.dot(normed_one, w_key, preferred_element_type=jnp.float32).reshape(
        length, kv_heads, head_size
    )
    v_half = (
        jnp.dot(normed_one, w_value, preferred_element_type=jnp.float32)
        .astype(jnp.bfloat16)
        .reshape(length, kv_heads, head_size)
    )
    q_scale = rms_scale(q_raw)
    k_scale = rms_scale(k_raw)
    q_hat = q_raw * q_scale
    k_hat = k_raw * k_scale
    q_rot = (
        rotate(q_hat * query_gain, cosine, sine_table)
        .astype(jnp.bfloat16)
        .reshape(length, kv_heads, groups, head_size)
    )
    k_rot = rotate(k_hat * key_gain, cosine, sine_table).astype(jnp.bfloat16)
    scores = score_table(q_rot, k_rot, allowed, factor)
    row_peak = jnp.max(scores, axis=-1, keepdims=True)
    log_total = row_peak + jnp.log(jnp.sum(jnp.exp(scores - row_peak), axis=-1, keepdims=True))
    attn_probs = jnp.exp(scores - log_total).astype(jnp.bfloat16)
    attn_mixed = jnp.einsum(
        "kgij,jkd->ikgd", attn_probs, v_half, preferred_element_type=jnp.float32
    )
    attn_mixed = attn_mixed.reshape(length, q_heads * head_size).astype(jnp.bfloat16)
    attn_sum = split_tensor_sum(jnp.dot(attn_mixed, w_out, preferred_element_type=jnp.float32))
    residual = tokens_wide + attn_sum
    scale_two = rms_scale(residual)
    normed_two = (residual * scale_two * ffn_gain).astype(jnp.bfloat16)
    gate_proj = jnp.dot(normed_two, w_gate, preferred_element_type=jnp.float32)
    up_proj = jnp.dot(normed_two, w_up, preferred_element_type=jnp.float32)
    gate_sigmoid = jax.nn.sigmoid(gate_proj)
    hidden = (gate_proj * gate_sigmoid * up_proj).astype(jnp.bfloat16)
    mlp_sum = tensor_sum(jnp.dot(hidden, w_down, preferred_element_type=jnp.float32))
    output = (residual + mlp_sum).astype(jnp.bfloat16)
    down_grad = outer(hidden, cotangent)
    hidden_grad = inner(cotangent, w_down)
    gate_grad = (
        hidden_grad * up_proj * gate_sigmoid * (1.0 + gate_proj * (1.0 - gate_sigmoid))
    ).astype(jnp.bfloat16)
    up_grad = (hidden_grad * gate_proj * gate_sigmoid).astype(jnp.bfloat16)
    gate_w_grad = outer(normed_two, gate_grad)
    up_w_grad = outer(normed_two, up_grad)
    ffn_w_grads, two_partial = lax.optimization_barrier(
        ((down_grad, gate_w_grad, up_w_grad), inner(gate_grad, w_gate) + inner(up_grad, w_up))
    )
    ffn_w_grads = lax.psum(ffn_w_grads, DP)
    normed_two_grad = tensor_sum(two_partial)
    ffn_grad = jnp.sum(normed_two_grad * residual * scale_two, axis=0)
    residual_grad = cotangent.astype(jnp.float32) + rms_back(
        normed_two_grad, residual, scale_two, ffn_gain
    )
    residual_half = residual_grad.astype(jnp.bfloat16)
    out_w_grad = outer(attn_mixed, residual_half)
    mixed_grad = (
        inner(residual_half, w_out)
        .astype(jnp.bfloat16)
        .reshape(length, kv_heads, groups, head_size)
    )
    attn_full = jnp.exp(score_table(q_rot, k_rot, allowed, factor) - log_total)
    probs_half = attn_full.astype(jnp.bfloat16)
    value_grad = jnp.einsum(
        "kgij,ikgd->jkd", probs_half, mixed_grad, preferred_element_type=jnp.float32
    ).astype(jnp.bfloat16)
    prob_grad = jnp.einsum("ikgd,jkd->kgij", mixed_grad, v_half, preferred_element_type=jnp.float32)
    row_delta = jnp.sum(attn_full * prob_grad, axis=-1, keepdims=True)
    score_grad = (attn_full * (prob_grad - row_delta) * factor).astype(jnp.bfloat16)
    q_rot_grad = jnp.einsum(
        "kgij,jkd->ikgd", score_grad, k_rot, preferred_element_type=jnp.float32
    ).reshape(length, q_heads, head_size)
    k_rot_grad = jnp.einsum("kgij,ikgd->jkd", score_grad, q_rot, preferred_element_type=jnp.float32)
    q_norm_grad = unrotate(q_rot_grad, cosine, sine_table)
    k_norm_grad = unrotate(k_rot_grad, cosine, sine_table)
    qgain_grad = jnp.sum(q_norm_grad * q_hat, axis=(0, 1))
    kgain_grad = jnp.sum(k_norm_grad * k_hat, axis=(0, 1))
    q_grad = (
        rms_back(q_norm_grad, q_raw, q_scale, query_gain)
        .astype(jnp.bfloat16)
        .reshape(length, q_heads * head_size)
    )
    k_grad = (
        rms_back(k_norm_grad, k_raw, k_scale, key_gain)
        .astype(jnp.bfloat16)
        .reshape(length, kv_heads * head_size)
    )
    v_grad = value_grad.reshape(length, kv_heads * head_size)
    query_w_grad = outer(normed_one, q_grad)
    key_w_grad = outer(normed_one, k_grad)
    value_w_grad = outer(normed_one, v_grad)
    one_partial = inner(q_grad, w_query) + inner(k_grad, w_key) + inner(v_grad, w_value)
    attn_part = jnp.sum(one_partial * tokens_wide * scale_one, axis=0)
    width = attn_part.shape[0]
    small = jnp.zeros((8, width), jnp.float32)
    small = small.at[0].set(ffn_grad).at[1].set(attn_part)
    small = small.at[2, :head_size].set(qgain_grad).at[2, head_size : 2 * head_size].set(kgain_grad)
    out_rows = out_w_grad.shape[0]
    ffn_w_grads, dp_sums, one_partial = lax.optimization_barrier(
        (
            ffn_w_grads,
            (query_w_grad, key_w_grad, value_w_grad, jnp.concatenate([out_w_grad, small])),
            one_partial,
        )
    )
    query_w_grad, key_w_grad, value_w_grad, out_pack = dp_sums
    q_cols = query_w_grad.shape[1]
    k_cols = key_w_grad.shape[1]
    width = out_pack.shape[1]
    flat = jnp.concatenate([query_w_grad, key_w_grad, value_w_grad], axis=1).reshape(-1, width)
    flat_rows = flat.shape[0]
    packed = jnp.concatenate([flat, out_pack], axis=0)
    padded_rows = -(-packed.shape[0] // 256) * 256
    packed = jnp.pad(packed, ((0, padded_rows - packed.shape[0]), (0, 0)))
    packed = ring_sum(packed, "dz", ("dc", "dx"))
    flat = packed[:flat_rows].reshape(query_w_grad.shape[0], -1)
    query_w_grad = flat[:, :q_cols]
    key_w_grad = flat[:, q_cols : q_cols + k_cols]
    value_w_grad = flat[:, q_cols + k_cols :]
    out_pack = packed[flat_rows : flat_rows + out_pack.shape[0]]
    down_grad, gate_w_grad, up_w_grad = ffn_w_grads
    normed_one_grad = tensor_sum(one_partial)
    input_grad = residual_grad + rms_back(normed_one_grad, tokens_wide, scale_one, attn_gain)
    out_w_grad = out_pack[:out_rows]
    ffn_grad = out_pack[out_rows]
    gains = small_tensor_sum(out_pack[out_rows + 1 : out_rows + 3])
    attn_grad = gains[0]
    qgain_grad = gains[1, :head_size]
    kgain_grad = gains[1, head_size : 2 * head_size]
    return (
        output,
        input_grad,
        attn_grad,
        query_w_grad,
        key_w_grad,
        value_w_grad,
        qgain_grad,
        kgain_grad,
        out_w_grad,
        ffn_grad,
        gate_w_grad,
        up_w_grad,
        down_grad,
    )


def solution(mesh):
    from jax.sharding import Mesh

    dp_size, tensor_size = mesh.devices.shape
    split = Mesh(
        mesh.devices.reshape(2, dp_size // 4, 2, tensor_size // 2, 2), DP + TENSOR
    )
    return jax.shard_map(
        per_device,
        mesh=split,
        in_specs=(
            P(DP, None),
            P(DP),
            P(),
            P(None, TENSOR),
            P(None, TENSOR),
            P(None, TENSOR),
            P(),
            P(),
            P(TENSOR, None),
            P(),
            P(None, TENSOR),
            P(None, TENSOR),
            P(TENSOR, None),
            P(DP, None),
        ),
        out_specs=(
            P(DP, None),
            P(DP, None),
            P(),
            P(None, TENSOR),
            P(None, TENSOR),
            P(None, TENSOR),
            P(),
            P(),
            P(TENSOR, None),
            P(),
            P(None, TENSOR),
            P(None, TENSOR),
            P(TENSOR, None),
        ),
        check_vma=False,
    )
```

```python
import math

import jax
import jax.numpy as jnp
from jax import lax
from jax.sharding import PartitionSpec as P

EPS = 1e-05
THETA = 1000000.0
TENSOR = ("ty", "tx")
DP = ("dx", "dz", "dc")


def outer(first_op, second_op):
    return lax.dot_general(
        first_op, second_op, (((0,), (0,)), ((), ())), preferred_element_type=jnp.float32
    )


def inner(first_op, second_op):
    return lax.dot_general(
        first_op, second_op, (((1,), (1,)), ((), ())), preferred_element_type=jnp.float32
    )


def rms_scale(values):
    return lax.rsqrt(jnp.mean(values * values, axis=-1, keepdims=True) + EPS)


def rms_back(upstream, values, inv_rms, gain_vec):
    normed = values * inv_rms
    weighted = upstream * gain_vec
    return inv_rms * (weighted - normed * jnp.mean(weighted * normed, axis=-1, keepdims=True))


def seq_layout(segment):
    length = segment.shape[0]
    ordinal = jnp.arange(length, dtype=jnp.int32)
    same_seq = segment[:, None] == segment[None, :]
    places = jnp.sum((same_seq & (ordinal[None, :] < ordinal[:, None])).astype(jnp.int32), axis=1)
    allowed = same_seq & (ordinal[None, :] <= ordinal[:, None])
    return (places, allowed)


def rope_tables(places, head_size):
    frequency = jnp.exp(
        jnp.arange(head_size // 2, dtype=jnp.float32) * (-2.0 * math.log(THETA) / head_size)
    )
    angles = places.astype(jnp.float32)[:, None] * frequency[None, :]
    angles = jnp.concatenate([angles, angles], axis=1)
    return (jnp.cos(angles), jnp.sin(angles))


def rotate(values, cosine, sine_table):
    half = values.shape[-1] // 2
    turned = jnp.concatenate([-values[..., half:], values[..., :half]], axis=-1)
    return values * cosine[:, None, :] + turned * sine_table[:, None, :]


def unrotate(incoming, cosine, sine_table):
    half = incoming.shape[-1] // 2
    scaled = incoming * sine_table[:, None, :]
    swapped = jnp.concatenate([scaled[..., half:], -scaled[..., :half]], axis=-1)
    return incoming * cosine[:, None, :] + swapped


def score_table(q_rot, k_rot, allowed, factor):
    raw = jnp.einsum("ikgd,jkd->kgij", q_rot, k_rot, preferred_element_type=jnp.float32) * factor
    return jnp.where(allowed[None, None], raw, -1e30)


def ring(size, shift):
    return [(i, (i + shift) % size) for i in range(size)]


def tensor_sum(values, extra=None):
    rows, cols = values.shape
    ny = lax.axis_size("ty")
    nx = lax.axis_size("tx")
    y = lax.axis_index("ty")
    h = lax.axis_index("tx")
    leaf = rows // (2 * ny * nx)
    parts = values.reshape(2, ny, nx, leaf, cols)
    pairs = ring(nx, 1)
    total = extra
    accs = []
    for way, shift in ((0, 1), (1, -1)):
        chunks = parts[way]
        acc = lax.dynamic_index_in_dim(chunks, (y - shift) % ny, 0, keepdims=False)
        passing = extra
        for step in range(1, ny):
            if way == 0 and extra is not None:
                acc, passing = lax.ppermute((acc, passing), "ty", ring(ny, shift))
                total = total + passing
            else:
                acc = lax.ppermute(acc, "ty", ring(ny, shift))
            acc = acc + lax.dynamic_index_in_dim(chunks, (y - shift * (1 + step)) % ny, 0, keepdims=False)
        accs.append(acc)
    acc = jnp.stack(accs)
    keep = lax.dynamic_index_in_dim(acc, h, 1, keepdims=False)
    send = lax.dynamic_index_in_dim(acc, (h + 1) % nx, 1, keepdims=False)
    if extra is not None:
        got, got_total = lax.ppermute((send, total), "tx", pairs)
        total = total + got_total
    else:
        got = lax.ppermute(send, "tx", pairs)
    mine = keep + got
    other = lax.ppermute(mine, "tx", pairs)
    both = jnp.where(h == 0, jnp.stack([mine, other], 1), jnp.stack([other, mine], 1))
    outs = []
    for way, shift in ((0, 1), (1, -1)):
        cur = both[way]
        gathered = jnp.zeros((ny,) + cur.shape, values.dtype)
        gathered = lax.dynamic_update_index_in_dim(gathered, cur, y, 0)
        for step in range(1, ny):
            cur = lax.ppermute(cur, "ty", ring(ny, shift))
            gathered = lax.dynamic_update_index_in_dim(gathered, cur, (y - shift * step) % ny, 0)
        outs.append(gathered)
    result = jnp.stack(outs).reshape(rows, cols)
    if extra is None:
        return result
    return result, total


def split_tensor_sum(values, pieces=2):
    blocks = jnp.split(values, pieces, axis=0)
    return jnp.concatenate([tensor_sum(block) for block in blocks], axis=0)


def ring_sum(values, ring_axis, pair_axes):
    rows, cols = values.shape
    size = lax.axis_size(ring_axis)
    here = lax.axis_index(ring_axis)
    parts = values.reshape(2, size, rows // (2 * size), cols)
    accs = []
    for way, shift in ((0, 1), (1, -1)):
        chunks = parts[way]
        acc = lax.dynamic_index_in_dim(chunks, (here - shift) % size, 0, keepdims=False)
        for step in range(1, size):
            acc = lax.ppermute(acc, ring_axis, ring(size, shift))
            acc = acc + lax.dynamic_index_in_dim(chunks, (here - shift * (1 + step)) % size, 0, keepdims=False)
        accs.append(acc)
    acc = jnp.stack(accs)
    sides = []
    for axis in pair_axes:
        side = lax.axis_index(axis)
        halves = acc.reshape(2, 2, acc.shape[1] // 2, cols)
        keep = lax.dynamic_index_in_dim(halves, side, 1, keepdims=False)
        send = lax.dynamic_index_in_dim(halves, 1 - side, 1, keepdims=False)
        acc = keep + lax.ppermute(send, axis, [(0, 1), (1, 0)])
        sides.append(side)
    for axis, side in zip(pair_axes[::-1], sides[::-1]):
        other = lax.ppermute(acc, axis, [(0, 1), (1, 0)])
        both = jnp.where(side == 0, jnp.stack([acc, other], 1), jnp.stack([other, acc], 1))
        acc = both.reshape(2, 2 * acc.shape[1], cols)
    outs = []
    for way, shift in ((0, 1), (1, -1)):
        cur = acc[way]
        gathered = jnp.zeros((size,) + cur.shape, values.dtype)
        gathered = lax.dynamic_update_index_in_dim(gathered, cur, here, 0)
        for step in range(1, size):
            cur = lax.ppermute(cur, ring_axis, ring(size, shift))
            gathered = lax.dynamic_update_index_in_dim(gathered, cur, (here - shift * step) % size, 0)
        outs.append(gathered)
    return jnp.stack(outs).reshape(rows, cols)


def small_tensor_sum(values):
    ny = lax.axis_size("ty")
    nx = lax.axis_size("tx")
    dist = 1
    while dist < ny:
        values = values + lax.ppermute(values, "ty", [(i, i ^ dist) for i in range(ny)])
        dist *= 2
    dist = 1
    while dist < nx:
        values = values + lax.ppermute(values, "tx", [(i, i ^ dist) for i in range(nx)])
        dist *= 2
    return values


def per_device(
    tokens,
    segment_ids,
    attn_gain,
    w_query,
    w_key,
    w_value,
    query_gain,
    key_gain,
    w_out,
    ffn_gain,
    w_gate,
    w_up,
    w_down,
    cotangent,
):
    length = tokens.shape[0]
    head_size = query_gain.shape[0]
    q_heads = w_query.shape[1] // head_size
    kv_heads = w_key.shape[1] // head_size
    groups = q_heads // kv_heads
    factor = 1.0 / math.sqrt(head_size)
    places, allowed = seq_layout(segment_ids)
    cosine, sine_table = rope_tables(places, head_size)
    tokens_wide = tokens.astype(jnp.float32)
    scale_one = rms_scale(tokens_wide)
    normed_one = (tokens_wide * scale_one * attn_gain).astype(jnp.bfloat16)
    q_raw = jnp.dot(normed_one, w_query, preferred_element_type=jnp.float32).reshape(
        length, q_heads, head_size
    )
    k_raw = jnp.dot(normed_one, w_key, preferred_element_type=jnp.float32).reshape(
        length, kv_heads, head_size
    )
    v_half = (
        jnp.dot(normed_one, w_value, preferred_element_type=jnp.float32)
        .astype(jnp.bfloat16)
        .reshape(length, kv_heads, head_size)
    )
    q_scale = rms_scale(q_raw)
    k_scale = rms_scale(k_raw)
    q_hat = q_raw * q_scale
    k_hat = k_raw * k_scale
    q_rot = (
        rotate(q_hat * query_gain, cosine, sine_table)
        .astype(jnp.bfloat16)
        .reshape(length, kv_heads, groups, head_size)
    )
    k_rot = rotate(k_hat * key_gain, cosine, sine_table).astype(jnp.bfloat16)
    scores = score_table(q_rot, k_rot, allowed, factor)
    row_peak = jnp.max(scores, axis=-1, keepdims=True)
    log_total = row_peak + jnp.log(jnp.sum(jnp.exp(scores - row_peak), axis=-1, keepdims=True))
    attn_probs = jnp.exp(scores - log_total).astype(jnp.bfloat16)
    attn_mixed = jnp.einsum(
        "kgij,jkd->ikgd", attn_probs, v_half, preferred_element_type=jnp.float32
    )
    attn_mixed = attn_mixed.reshape(length, q_heads * head_size).astype(jnp.bfloat16)
    attn_sum = split_tensor_sum(jnp.dot(attn_mixed, w_out, preferred_element_type=jnp.float32))
    residual = tokens_wide + attn_sum
    scale_two = rms_scale(residual)
    normed_two = (residual * scale_two * ffn_gain).astype(jnp.bfloat16)
    gate_proj = jnp.dot(normed_two, w_gate, preferred_element_type=jnp.float32)
    up_proj = jnp.dot(normed_two, w_up, preferred_element_type=jnp.float32)
    gate_sigmoid = jax.nn.sigmoid(gate_proj)
    hidden = (gate_proj * gate_sigmoid * up_proj).astype(jnp.bfloat16)
    mlp_partial = jnp.dot(hidden, w_down, preferred_element_type=jnp.float32)
    down_grad = outer(hidden, cotangent)
    hidden_grad = inner(cotangent, w_down)
    gate_grad = (
        hidden_grad * up_proj * gate_sigmoid * (1.0 + gate_proj * (1.0 - gate_sigmoid))
    ).astype(jnp.bfloat16)
    up_grad = (hidden_grad * gate_proj * gate_sigmoid).astype(jnp.bfloat16)
    gate_w_grad = outer(normed_two, gate_grad)
    up_w_grad = outer(normed_two, up_grad)
    ffn_w_grads, two_partial = lax.optimization_barrier(
        ((down_grad, gate_w_grad, up_w_grad), inner(gate_grad, w_gate) + inner(up_grad, w_up))
    )
    ffn_w_grads = lax.psum(ffn_w_grads, DP)
    normed_two_grad = split_tensor_sum(two_partial)
    mlp_partial, normed_two_grad = lax.optimization_barrier((mlp_partial, normed_two_grad))
    mlp_sum = tensor_sum(mlp_partial)
    output = (residual + mlp_sum).astype(jnp.bfloat16)
    ffn_grad = jnp.sum(normed_two_grad * residual * scale_two, axis=0)
    residual_grad = cotangent.astype(jnp.float32) + rms_back(
        normed_two_grad, residual, scale_two, ffn_gain
    )
    residual_half = residual_grad.astype(jnp.bfloat16)
    out_w_grad = outer(attn_mixed, residual_half)
    mixed_grad = (
        inner(residual_half, w_out)
        .astype(jnp.bfloat16)
        .reshape(length, kv_heads, groups, head_size)
    )
    attn_full = jnp.exp(score_table(q_rot, k_rot, allowed, factor) - log_total)
    probs_half = attn_full.astype(jnp.bfloat16)
    value_grad = jnp.einsum(
        "kgij,ikgd->jkd", probs_half, mixed_grad, preferred_element_type=jnp.float32
    ).astype(jnp.bfloat16)
    prob_grad = jnp.einsum("ikgd,jkd->kgij", mixed_grad, v_half, preferred_element_type=jnp.float32)
    row_delta = jnp.sum(attn_full * prob_grad, axis=-1, keepdims=True)
    score_grad = (attn_full * (prob_grad - row_delta) * factor).astype(jnp.bfloat16)
    q_rot_grad = jnp.einsum(
        "kgij,jkd->ikgd", score_grad, k_rot, preferred_element_type=jnp.float32
    ).reshape(length, q_heads, head_size)
    k_rot_grad = jnp.einsum("kgij,ikgd->jkd", score_grad, q_rot, preferred_element_type=jnp.float32)
    q_norm_grad = unrotate(q_rot_grad, cosine, sine_table)
    k_norm_grad = unrotate(k_rot_grad, cosine, sine_table)
    qgain_grad = jnp.sum(q_norm_grad * q_hat, axis=(0, 1))
    kgain_grad = jnp.sum(k_norm_grad * k_hat, axis=(0, 1))
    q_grad = (
        rms_back(q_norm_grad, q_raw, q_scale, query_gain)
        .astype(jnp.bfloat16)
        .reshape(length, q_heads * head_size)
    )
    k_grad = (
        rms_back(k_norm_grad, k_raw, k_scale, key_gain)
        .astype(jnp.bfloat16)
        .reshape(length, kv_heads * head_size)
    )
    v_grad = value_grad.reshape(length, kv_heads * head_size)
    query_w_grad = outer(normed_one, q_grad)
    key_w_grad = outer(normed_one, k_grad)
    value_w_grad = outer(normed_one, v_grad)
    one_partial = inner(q_grad, w_query) + inner(k_grad, w_key) + inner(v_grad, w_value)
    attn_part = jnp.sum(one_partial * tokens_wide * scale_one, axis=0)
    width = attn_part.shape[0]
    small = jnp.zeros((8, width), jnp.float32)
    small = small.at[0].set(ffn_grad).at[1].set(attn_part)
    small = small.at[2, :head_size].set(qgain_grad).at[2, head_size : 2 * head_size].set(kgain_grad)
    out_rows = out_w_grad.shape[0]
    ffn_w_grads, dp_sums, one_partial = lax.optimization_barrier(
        (
            ffn_w_grads,
            (query_w_grad, key_w_grad, value_w_grad, jnp.concatenate([out_w_grad, small])),
            one_partial,
        )
    )
    query_w_grad, key_w_grad, value_w_grad, out_pack = dp_sums
    q_cols = query_w_grad.shape[1]
    k_cols = key_w_grad.shape[1]
    width = out_pack.shape[1]
    flat = jnp.concatenate([query_w_grad, key_w_grad, value_w_grad], axis=1).reshape(-1, width)
    flat_rows = flat.shape[0]
    packed = jnp.concatenate([flat, out_pack], axis=0)
    padded_rows = -(-packed.shape[0] // 256) * 256
    packed = jnp.pad(packed, ((0, padded_rows - packed.shape[0]), (0, 0)))
    packed = ring_sum(packed, "dz", ("dc", "dx"))
    flat = packed[:flat_rows].reshape(query_w_grad.shape[0], -1)
    query_w_grad = flat[:, :q_cols]
    key_w_grad = flat[:, q_cols : q_cols + k_cols]
    value_w_grad = flat[:, q_cols + k_cols :]
    out_pack = packed[flat_rows : flat_rows + out_pack.shape[0]]
    down_grad, gate_w_grad, up_w_grad = ffn_w_grads
    normed_one_grad = split_tensor_sum(one_partial)
    input_grad = residual_grad + rms_back(normed_one_grad, tokens_wide, scale_one, attn_gain)
    out_w_grad = out_pack[:out_rows]
    ffn_grad = out_pack[out_rows]
    gains = small_tensor_sum(out_pack[out_rows + 1 : out_rows + 3])
    attn_grad = gains[0]
    qgain_grad = gains[1, :head_size]
    kgain_grad = gains[1, head_size : 2 * head_size]
    return (
        output,
        input_grad,
        attn_grad,
        query_w_grad,
        key_w_grad,
        value_w_grad,
        qgain_grad,
        kgain_grad,
        out_w_grad,
        ffn_grad,
        gate_w_grad,
        up_w_grad,
        down_grad,
    )


def solution(mesh):
    from jax.sharding import Mesh

    dp_size, tensor_size = mesh.devices.shape
    split = Mesh(
        mesh.devices.reshape(2, dp_size // 4, 2, tensor_size // 2, 2), DP + TENSOR
    )
    return jax.shard_map(
        per_device,
        mesh=split,
        in_specs=(
            P(DP, None),
            P(DP),
            P(),
            P(None, TENSOR),
            P(None, TENSOR),
            P(None, TENSOR),
            P(),
            P(),
            P(TENSOR, None),
            P(),
            P(None, TENSOR),
            P(None, TENSOR),
            P(TENSOR, None),
            P(DP, None),
        ),
        out_specs=(
            P(DP, None),
            P(DP, None),
            P(),
            P(None, TENSOR),
            P(None, TENSOR),
            P(None, TENSOR),
            P(),
            P(),
            P(TENSOR, None),
            P(),
            P(None, TENSOR),
            P(None, TENSOR),
            P(TENSOR, None),
        ),
        check_vma=False,
    )
```

```python
import math

import jax
import jax.numpy as jnp
from jax import lax
from jax.sharding import PartitionSpec as P

EPS = 1e-05
THETA = 1000000.0
TENSOR = ("ty", "tx")
DP = ("dx", "dz", "dc")


def outer(first_op, second_op):
    return lax.dot_general(
        first_op, second_op, (((0,), (0,)), ((), ())), preferred_element_type=jnp.float32
    )


def inner(first_op, second_op):
    return lax.dot_general(
        first_op, second_op, (((1,), (1,)), ((), ())), preferred_element_type=jnp.float32
    )


def rms_scale(values):
    return lax.rsqrt(jnp.mean(values * values, axis=-1, keepdims=True) + EPS)


def rms_back(upstream, values, inv_rms, gain_vec):
    normed = values * inv_rms
    weighted = upstream * gain_vec
    return inv_rms * (weighted - normed * jnp.mean(weighted * normed, axis=-1, keepdims=True))


def seq_layout(segment):
    length = segment.shape[0]
    ordinal = jnp.arange(length, dtype=jnp.int32)
    same_seq = segment[:, None] == segment[None, :]
    places = jnp.sum((same_seq & (ordinal[None, :] < ordinal[:, None])).astype(jnp.int32), axis=1)
    allowed = same_seq & (ordinal[None, :] <= ordinal[:, None])
    return (places, allowed)


def rope_tables(places, head_size):
    frequency = jnp.exp(
        jnp.arange(head_size // 2, dtype=jnp.float32) * (-2.0 * math.log(THETA) / head_size)
    )
    angles = places.astype(jnp.float32)[:, None] * frequency[None, :]
    angles = jnp.concatenate([angles, angles], axis=1)
    return (jnp.cos(angles), jnp.sin(angles))


def rotate(values, cosine, sine_table):
    half = values.shape[-1] // 2
    turned = jnp.concatenate([-values[..., half:], values[..., :half]], axis=-1)
    return values * cosine[:, None, :] + turned * sine_table[:, None, :]


def unrotate(incoming, cosine, sine_table):
    half = incoming.shape[-1] // 2
    scaled = incoming * sine_table[:, None, :]
    swapped = jnp.concatenate([scaled[..., half:], -scaled[..., :half]], axis=-1)
    return incoming * cosine[:, None, :] + swapped


def score_table(q_rot, k_rot, allowed, factor):
    raw = jnp.einsum("ikgd,jkd->kgij", q_rot, k_rot, preferred_element_type=jnp.float32) * factor
    return jnp.where(allowed[None, None], raw, -1e30)


def ring(size, shift):
    return [(i, (i + shift) % size) for i in range(size)]


def tensor_sum(values, extra=None):
    rows, cols = values.shape
    ny = lax.axis_size("ty")
    nx = lax.axis_size("tx")
    y = lax.axis_index("ty")
    h = lax.axis_index("tx")
    leaf = rows // (2 * ny * nx)
    parts = values.reshape(2, ny, nx, leaf, cols)
    pairs = ring(nx, 1)
    total = extra
    accs = []
    for way, shift in ((0, 1), (1, -1)):
        chunks = parts[way]
        acc = lax.dynamic_index_in_dim(chunks, (y - shift) % ny, 0, keepdims=False)
        passing = extra
        for step in range(1, ny):
            if way == 0 and extra is not None:
                acc, passing = lax.ppermute((acc, passing), "ty", ring(ny, shift))
                total = total + passing
            else:
                acc = lax.ppermute(acc, "ty", ring(ny, shift))
            acc = acc + lax.dynamic_index_in_dim(chunks, (y - shift * (1 + step)) % ny, 0, keepdims=False)
        accs.append(acc)
    acc = jnp.stack(accs)
    keep = lax.dynamic_index_in_dim(acc, h, 1, keepdims=False)
    send = lax.dynamic_index_in_dim(acc, (h + 1) % nx, 1, keepdims=False)
    if extra is not None:
        got, got_total = lax.ppermute((send, total), "tx", pairs)
        total = total + got_total
    else:
        got = lax.ppermute(send, "tx", pairs)
    mine = keep + got
    other = lax.ppermute(mine, "tx", pairs)
    both = jnp.where(h == 0, jnp.stack([mine, other], 1), jnp.stack([other, mine], 1))
    outs = []
    for way, shift in ((0, 1), (1, -1)):
        cur = both[way]
        gathered = jnp.zeros((ny,) + cur.shape, values.dtype)
        gathered = lax.dynamic_update_index_in_dim(gathered, cur, y, 0)
        for step in range(1, ny):
            cur = lax.ppermute(cur, "ty", ring(ny, shift))
            gathered = lax.dynamic_update_index_in_dim(gathered, cur, (y - shift * step) % ny, 0)
        outs.append(gathered)
    result = jnp.stack(outs).reshape(rows, cols)
    if extra is None:
        return result
    return result, total


def split_tensor_sum(values, pieces=2):
    blocks = jnp.split(values, pieces, axis=0)
    return jnp.concatenate([tensor_sum(block) for block in blocks], axis=0)


def ring_sum(values, ring_axis, pair_axes):
    rows, cols = values.shape
    size = lax.axis_size(ring_axis)
    here = lax.axis_index(ring_axis)
    parts = values.reshape(2, size, rows // (2 * size), cols)
    accs = []
    for way, shift in ((0, 1), (1, -1)):
        chunks = parts[way]
        acc = lax.dynamic_index_in_dim(chunks, (here - shift) % size, 0, keepdims=False)
        for step in range(1, size):
            acc = lax.ppermute(acc, ring_axis, ring(size, shift))
            acc = acc + lax.dynamic_index_in_dim(chunks, (here - shift * (1 + step)) % size, 0, keepdims=False)
        accs.append(acc)
    acc = jnp.stack(accs)
    sides = []
    for axis in pair_axes:
        side = lax.axis_index(axis)
        halves = acc.reshape(2, 2, acc.shape[1] // 2, cols)
        keep = lax.dynamic_index_in_dim(halves, side, 1, keepdims=False)
        send = lax.dynamic_index_in_dim(halves, 1 - side, 1, keepdims=False)
        acc = keep + lax.ppermute(send, axis, [(0, 1), (1, 0)])
        sides.append(side)
    for axis, side in zip(pair_axes[::-1], sides[::-1]):
        other = lax.ppermute(acc, axis, [(0, 1), (1, 0)])
        both = jnp.where(side == 0, jnp.stack([acc, other], 1), jnp.stack([other, acc], 1))
        acc = both.reshape(2, 2 * acc.shape[1], cols)
    outs = []
    for way, shift in ((0, 1), (1, -1)):
        cur = acc[way]
        gathered = jnp.zeros((size,) + cur.shape, values.dtype)
        gathered = lax.dynamic_update_index_in_dim(gathered, cur, here, 0)
        for step in range(1, size):
            cur = lax.ppermute(cur, ring_axis, ring(size, shift))
            gathered = lax.dynamic_update_index_in_dim(gathered, cur, (here - shift * step) % size, 0)
        outs.append(gathered)
    return jnp.stack(outs).reshape(rows, cols)


def small_tensor_sum(values):
    ny = lax.axis_size("ty")
    nx = lax.axis_size("tx")
    dist = 1
    while dist < ny:
        values = values + lax.ppermute(values, "ty", [(i, i ^ dist) for i in range(ny)])
        dist *= 2
    dist = 1
    while dist < nx:
        values = values + lax.ppermute(values, "tx", [(i, i ^ dist) for i in range(nx)])
        dist *= 2
    return values


def per_device(
    tokens,
    segment_ids,
    attn_gain,
    w_query,
    w_key,
    w_value,
    query_gain,
    key_gain,
    w_out,
    ffn_gain,
    w_gate,
    w_up,
    w_down,
    cotangent,
):
    length = tokens.shape[0]
    head_size = query_gain.shape[0]
    q_heads = w_query.shape[1] // head_size
    kv_heads = w_key.shape[1] // head_size
    groups = q_heads // kv_heads
    factor = 1.0 / math.sqrt(head_size)
    places, allowed = seq_layout(segment_ids)
    cosine, sine_table = rope_tables(places, head_size)
    tokens_wide = tokens.astype(jnp.float32)
    scale_one = rms_scale(tokens_wide)
    normed_one = (tokens_wide * scale_one * attn_gain).astype(jnp.bfloat16)
    q_raw = jnp.dot(normed_one, w_query, preferred_element_type=jnp.float32).reshape(
        length, q_heads, head_size
    )
    k_raw = jnp.dot(normed_one, w_key, preferred_element_type=jnp.float32).reshape(
        length, kv_heads, head_size
    )
    v_half = (
        jnp.dot(normed_one, w_value, preferred_element_type=jnp.float32)
        .astype(jnp.bfloat16)
        .reshape(length, kv_heads, head_size)
    )
    q_scale = rms_scale(q_raw)
    k_scale = rms_scale(k_raw)
    q_hat = q_raw * q_scale
    k_hat = k_raw * k_scale
    q_rot = (
        rotate(q_hat * query_gain, cosine, sine_table)
        .astype(jnp.bfloat16)
        .reshape(length, kv_heads, groups, head_size)
    )
    k_rot = rotate(k_hat * key_gain, cosine, sine_table).astype(jnp.bfloat16)
    block = length // 2
    log_blocks, mixed_blocks, sum_blocks = [], [], []
    for first in range(0, length, block):
        seen = first + block
        scores = score_table(
            q_rot[first:seen], k_rot[:seen], allowed[first:seen, :seen], factor
        )
        row_peak = jnp.max(scores, axis=-1, keepdims=True)
        log_block = row_peak + jnp.log(
            jnp.sum(jnp.exp(scores - row_peak), axis=-1, keepdims=True)
        )
        attn_probs = jnp.exp(scores - log_block).astype(jnp.bfloat16)
        mixed = jnp.einsum(
            "kgij,jkd->ikgd", attn_probs, v_half[:seen], preferred_element_type=jnp.float32
        )
        mixed = mixed.reshape(block, q_heads * head_size).astype(jnp.bfloat16)
        log_blocks.append(log_block)
        mixed_blocks.append(mixed)
        sum_blocks.append(tensor_sum(jnp.dot(mixed, w_out, preferred_element_type=jnp.float32)))
    log_total = jnp.concatenate(log_blocks, axis=2)
    attn_mixed = jnp.concatenate(mixed_blocks, axis=0)
    attn_sum = jnp.concatenate(sum_blocks, axis=0)
    residual = tokens_wide + attn_sum
    scale_two = rms_scale(residual)
    normed_two = (residual * scale_two * ffn_gain).astype(jnp.bfloat16)
    gate_proj = jnp.dot(normed_two, w_gate, preferred_element_type=jnp.float32)
    up_proj = jnp.dot(normed_two, w_up, preferred_element_type=jnp.float32)
    gate_sigmoid = jax.nn.sigmoid(gate_proj)
    hidden = (gate_proj * gate_sigmoid * up_proj).astype(jnp.bfloat16)
    mlp_sum = split_tensor_sum(jnp.dot(hidden, w_down, preferred_element_type=jnp.float32))
    output = (residual + mlp_sum).astype(jnp.bfloat16)
    down_grad = outer(hidden, cotangent)
    hidden_grad = inner(cotangent, w_down)
    gate_grad = (
        hidden_grad * up_proj * gate_sigmoid * (1.0 + gate_proj * (1.0 - gate_sigmoid))
    ).astype(jnp.bfloat16)
    up_grad = (hidden_grad * gate_proj * gate_sigmoid).astype(jnp.bfloat16)
    gate_w_grad = outer(normed_two, gate_grad)
    up_w_grad = outer(normed_two, up_grad)
    ffn_w_grads, two_partial = lax.optimization_barrier(
        ((down_grad, gate_w_grad, up_w_grad), inner(gate_grad, w_gate) + inner(up_grad, w_up))
    )
    ffn_w_grads = lax.psum(ffn_w_grads, DP)
    normed_two_grad = split_tensor_sum(two_partial)
    ffn_grad = jnp.sum(normed_two_grad * residual * scale_two, axis=0)
    residual_grad = cotangent.astype(jnp.float32) + rms_back(
        normed_two_grad, residual, scale_two, ffn_gain
    )
    residual_half = residual_grad.astype(jnp.bfloat16)
    out_w_grad = outer(attn_mixed, residual_half)
    mixed_grad = (
        inner(residual_half, w_out)
        .astype(jnp.bfloat16)
        .reshape(length, kv_heads, groups, head_size)
    )
    attn_full = jnp.exp(score_table(q_rot, k_rot, allowed, factor) - log_total)
    probs_half = attn_full.astype(jnp.bfloat16)
    value_grad = jnp.einsum(
        "kgij,ikgd->jkd", probs_half, mixed_grad, preferred_element_type=jnp.float32
    ).astype(jnp.bfloat16)
    prob_grad = jnp.einsum("ikgd,jkd->kgij", mixed_grad, v_half, preferred_element_type=jnp.float32)
    row_delta = jnp.sum(attn_full * prob_grad, axis=-1, keepdims=True)
    score_grad = (attn_full * (prob_grad - row_delta) * factor).astype(jnp.bfloat16)
    q_rot_grad = jnp.einsum(
        "kgij,jkd->ikgd", score_grad, k_rot, preferred_element_type=jnp.float32
    ).reshape(length, q_heads, head_size)
    k_rot_grad = jnp.einsum("kgij,ikgd->jkd", score_grad, q_rot, preferred_element_type=jnp.float32)
    q_norm_grad = unrotate(q_rot_grad, cosine, sine_table)
    k_norm_grad = unrotate(k_rot_grad, cosine, sine_table)
    qgain_grad = jnp.sum(q_norm_grad * q_hat, axis=(0, 1))
    kgain_grad = jnp.sum(k_norm_grad * k_hat, axis=(0, 1))
    q_grad = (
        rms_back(q_norm_grad, q_raw, q_scale, query_gain)
        .astype(jnp.bfloat16)
        .reshape(length, q_heads * head_size)
    )
    k_grad = (
        rms_back(k_norm_grad, k_raw, k_scale, key_gain)
        .astype(jnp.bfloat16)
        .reshape(length, kv_heads * head_size)
    )
    v_grad = value_grad.reshape(length, kv_heads * head_size)
    query_w_grad = outer(normed_one, q_grad)
    key_w_grad = outer(normed_one, k_grad)
    value_w_grad = outer(normed_one, v_grad)
    one_partial = inner(q_grad, w_query) + inner(k_grad, w_key) + inner(v_grad, w_value)
    attn_part = jnp.sum(one_partial * tokens_wide * scale_one, axis=0)
    width = attn_part.shape[0]
    small = jnp.zeros((8, width), jnp.float32)
    small = small.at[0].set(ffn_grad).at[1].set(attn_part)
    small = small.at[2, :head_size].set(qgain_grad).at[2, head_size : 2 * head_size].set(kgain_grad)
    out_rows = out_w_grad.shape[0]
    ffn_w_grads, dp_sums, one_partial = lax.optimization_barrier(
        (
            ffn_w_grads,
            (query_w_grad, key_w_grad, value_w_grad, jnp.concatenate([out_w_grad, small])),
            one_partial,
        )
    )
    query_w_grad, key_w_grad, value_w_grad, out_pack = dp_sums
    q_cols = query_w_grad.shape[1]
    k_cols = key_w_grad.shape[1]
    width = out_pack.shape[1]
    flat = jnp.concatenate([query_w_grad, key_w_grad, value_w_grad], axis=1).reshape(-1, width)
    flat_rows = flat.shape[0]
    packed = jnp.concatenate([flat, out_pack], axis=0)
    padded_rows = -(-packed.shape[0] // 256) * 256
    packed = jnp.pad(packed, ((0, padded_rows - packed.shape[0]), (0, 0)))
    packed = ring_sum(packed, "dz", ("dc", "dx"))
    flat = packed[:flat_rows].reshape(query_w_grad.shape[0], -1)
    query_w_grad = flat[:, :q_cols]
    key_w_grad = flat[:, q_cols : q_cols + k_cols]
    value_w_grad = flat[:, q_cols + k_cols :]
    out_pack = packed[flat_rows : flat_rows + out_pack.shape[0]]
    down_grad, gate_w_grad, up_w_grad = ffn_w_grads
    normed_one_grad = split_tensor_sum(one_partial)
    input_grad = residual_grad + rms_back(normed_one_grad, tokens_wide, scale_one, attn_gain)
    out_w_grad = out_pack[:out_rows]
    ffn_grad = out_pack[out_rows]
    gains = small_tensor_sum(out_pack[out_rows + 1 : out_rows + 3])
    attn_grad = gains[0]
    qgain_grad = gains[1, :head_size]
    kgain_grad = gains[1, head_size : 2 * head_size]
    return (
        output,
        input_grad,
        attn_grad,
        query_w_grad,
        key_w_grad,
        value_w_grad,
        qgain_grad,
        kgain_grad,
        out_w_grad,
        ffn_grad,
        gate_w_grad,
        up_w_grad,
        down_grad,
    )


def solution(mesh):
    from jax.sharding import Mesh

    dp_size, tensor_size = mesh.devices.shape
    split = Mesh(
        mesh.devices.reshape(2, dp_size // 4, 2, tensor_size // 2, 2), DP + TENSOR
    )
    return jax.shard_map(
        per_device,
        mesh=split,
        in_specs=(
            P(DP, None),
            P(DP),
            P(),
            P(None, TENSOR),
            P(None, TENSOR),
            P(None, TENSOR),
            P(),
            P(),
            P(TENSOR, None),
            P(),
            P(None, TENSOR),
            P(None, TENSOR),
            P(TENSOR, None),
            P(DP, None),
        ),
        out_specs=(
            P(DP, None),
            P(DP, None),
            P(),
            P(None, TENSOR),
            P(None, TENSOR),
            P(None, TENSOR),
            P(),
            P(),
            P(TENSOR, None),
            P(),
            P(None, TENSOR),
            P(None, TENSOR),
            P(TENSOR, None),
        ),
        check_vma=False,
    )
```

```python
import math

import jax
import jax.numpy as jnp
from jax import lax
from jax.sharding import PartitionSpec as P

EPS = 1e-05
THETA = 1000000.0
TENSOR = ("ty", "tx")
DP = ("dx", "dz", "dc")


def outer(first_op, second_op):
    return lax.dot_general(
        first_op, second_op, (((0,), (0,)), ((), ())), preferred_element_type=jnp.float32
    )


def inner(first_op, second_op):
    return lax.dot_general(
        first_op, second_op, (((1,), (1,)), ((), ())), preferred_element_type=jnp.float32
    )


def rms_scale(values):
    return lax.rsqrt(jnp.mean(values * values, axis=-1, keepdims=True) + EPS)


def rms_back(upstream, values, inv_rms, gain_vec):
    normed = values * inv_rms
    weighted = upstream * gain_vec
    return inv_rms * (weighted - normed * jnp.mean(weighted * normed, axis=-1, keepdims=True))


def seq_layout(segment):
    length = segment.shape[0]
    ordinal = jnp.arange(length, dtype=jnp.int32)
    same_seq = segment[:, None] == segment[None, :]
    places = jnp.sum((same_seq & (ordinal[None, :] < ordinal[:, None])).astype(jnp.int32), axis=1)
    allowed = same_seq & (ordinal[None, :] <= ordinal[:, None])
    return (places, allowed)


def rope_tables(places, head_size):
    frequency = jnp.exp(
        jnp.arange(head_size // 2, dtype=jnp.float32) * (-2.0 * math.log(THETA) / head_size)
    )
    angles = places.astype(jnp.float32)[:, None] * frequency[None, :]
    angles = jnp.concatenate([angles, angles], axis=1)
    return (jnp.cos(angles), jnp.sin(angles))


def rotate(values, cosine, sine_table):
    half = values.shape[-1] // 2
    turned = jnp.concatenate([-values[..., half:], values[..., :half]], axis=-1)
    return values * cosine[:, None, :] + turned * sine_table[:, None, :]


def unrotate(incoming, cosine, sine_table):
    half = incoming.shape[-1] // 2
    scaled = incoming * sine_table[:, None, :]
    swapped = jnp.concatenate([scaled[..., half:], -scaled[..., :half]], axis=-1)
    return incoming * cosine[:, None, :] + swapped


def score_table(q_rot, k_rot, allowed, factor):
    raw = jnp.einsum("ikgd,jkd->kgij", q_rot, k_rot, preferred_element_type=jnp.float32) * factor
    return jnp.where(allowed[None, None], raw, -1e30)


def ring(size, shift):
    return [(i, (i + shift) % size) for i in range(size)]


def tensor_sum(values, extra=None):
    rows, cols = values.shape
    ny = lax.axis_size("ty")
    nx = lax.axis_size("tx")
    y = lax.axis_index("ty")
    h = lax.axis_index("tx")
    leaf = rows // (2 * ny * nx)
    parts = values.reshape(2, ny, nx, leaf, cols)
    pairs = ring(nx, 1)
    total = extra
    accs = []
    for way, shift in ((0, 1), (1, -1)):
        chunks = parts[way]
        acc = lax.dynamic_index_in_dim(chunks, (y - shift) % ny, 0, keepdims=False)
        passing = extra
        for step in range(1, ny):
            if way == 0 and extra is not None:
                acc, passing = lax.ppermute((acc, passing), "ty", ring(ny, shift))
                total = total + passing
            else:
                acc = lax.ppermute(acc, "ty", ring(ny, shift))
            acc = acc + lax.dynamic_index_in_dim(chunks, (y - shift * (1 + step)) % ny, 0, keepdims=False)
        accs.append(acc)
    acc = jnp.stack(accs)
    keep = lax.dynamic_index_in_dim(acc, h, 1, keepdims=False)
    send = lax.dynamic_index_in_dim(acc, (h + 1) % nx, 1, keepdims=False)
    if extra is not None:
        got, got_total = lax.ppermute((send, total), "tx", pairs)
        total = total + got_total
    else:
        got = lax.ppermute(send, "tx", pairs)
    mine = keep + got
    other = lax.ppermute(mine, "tx", pairs)
    both = jnp.where(h == 0, jnp.stack([mine, other], 1), jnp.stack([other, mine], 1))
    outs = []
    for way, shift in ((0, 1), (1, -1)):
        cur = both[way]
        gathered = jnp.zeros((ny,) + cur.shape, values.dtype)
        gathered = lax.dynamic_update_index_in_dim(gathered, cur, y, 0)
        for step in range(1, ny):
            cur = lax.ppermute(cur, "ty", ring(ny, shift))
            gathered = lax.dynamic_update_index_in_dim(gathered, cur, (y - shift * step) % ny, 0)
        outs.append(gathered)
    result = jnp.stack(outs).reshape(rows, cols)
    if extra is None:
        return result
    return result, total


def split_tensor_sum(values, pieces=2):
    blocks = jnp.split(values, pieces, axis=0)
    return jnp.concatenate([tensor_sum(block) for block in blocks], axis=0)


def ring_sum(values, ring_axis, pair_axes):
    rows, cols = values.shape
    size = lax.axis_size(ring_axis)
    here = lax.axis_index(ring_axis)
    parts = values.reshape(2, size, rows // (2 * size), cols)
    accs = []
    for way, shift in ((0, 1), (1, -1)):
        chunks = parts[way]
        acc = lax.dynamic_index_in_dim(chunks, (here - shift) % size, 0, keepdims=False)
        for step in range(1, size):
            acc = lax.ppermute(acc, ring_axis, ring(size, shift))
            acc = acc + lax.dynamic_index_in_dim(chunks, (here - shift * (1 + step)) % size, 0, keepdims=False)
        accs.append(acc)
    acc = jnp.stack(accs)
    sides = []
    for axis in pair_axes:
        side = lax.axis_index(axis)
        halves = acc.reshape(2, 2, acc.shape[1] // 2, cols)
        keep = lax.dynamic_index_in_dim(halves, side, 1, keepdims=False)
        send = lax.dynamic_index_in_dim(halves, 1 - side, 1, keepdims=False)
        acc = keep + lax.ppermute(send, axis, [(0, 1), (1, 0)])
        sides.append(side)
    for axis, side in zip(pair_axes[::-1], sides[::-1]):
        other = lax.ppermute(acc, axis, [(0, 1), (1, 0)])
        both = jnp.where(side == 0, jnp.stack([acc, other], 1), jnp.stack([other, acc], 1))
        acc = both.reshape(2, 2 * acc.shape[1], cols)
    outs = []
    for way, shift in ((0, 1), (1, -1)):
        cur = acc[way]
        gathered = jnp.zeros((size,) + cur.shape, values.dtype)
        gathered = lax.dynamic_update_index_in_dim(gathered, cur, here, 0)
        for step in range(1, size):
            cur = lax.ppermute(cur, ring_axis, ring(size, shift))
            gathered = lax.dynamic_update_index_in_dim(gathered, cur, (here - shift * step) % size, 0)
        outs.append(gathered)
    return jnp.stack(outs).reshape(rows, cols)


def small_tensor_sum(values):
    ny = lax.axis_size("ty")
    nx = lax.axis_size("tx")
    dist = 1
    while dist < ny:
        values = values + lax.ppermute(values, "ty", [(i, i ^ dist) for i in range(ny)])
        dist *= 2
    dist = 1
    while dist < nx:
        values = values + lax.ppermute(values, "tx", [(i, i ^ dist) for i in range(nx)])
        dist *= 2
    return values


def per_device(
    tokens,
    segment_ids,
    attn_gain,
    w_query,
    w_key,
    w_value,
    query_gain,
    key_gain,
    w_out,
    ffn_gain,
    w_gate,
    w_up,
    w_down,
    cotangent,
):
    length = tokens.shape[0]
    head_size = query_gain.shape[0]
    q_heads = w_query.shape[1] // head_size
    kv_heads = w_key.shape[1] // head_size
    groups = q_heads // kv_heads
    factor = 1.0 / math.sqrt(head_size)
    places, allowed = seq_layout(segment_ids)
    cosine, sine_table = rope_tables(places, head_size)
    tokens_wide = tokens.astype(jnp.float32)
    scale_one = rms_scale(tokens_wide)
    normed_one = (tokens_wide * scale_one * attn_gain).astype(jnp.bfloat16)
    q_raw = jnp.dot(normed_one, w_query, preferred_element_type=jnp.float32).reshape(
        length, q_heads, head_size
    )
    k_raw = jnp.dot(normed_one, w_key, preferred_element_type=jnp.float32).reshape(
        length, kv_heads, head_size
    )
    v_half = (
        jnp.dot(normed_one, w_value, preferred_element_type=jnp.float32)
        .astype(jnp.bfloat16)
        .reshape(length, kv_heads, head_size)
    )
    q_scale = rms_scale(q_raw)
    k_scale = rms_scale(k_raw)
    q_hat = q_raw * q_scale
    k_hat = k_raw * k_scale
    q_rot = (
        rotate(q_hat * query_gain, cosine, sine_table)
        .astype(jnp.bfloat16)
        .reshape(length, kv_heads, groups, head_size)
    )
    k_rot = rotate(k_hat * key_gain, cosine, sine_table).astype(jnp.bfloat16)
    scores = score_table(q_rot, k_rot, allowed, factor)
    row_peak = jnp.max(scores, axis=-1, keepdims=True)
    log_total = row_peak + jnp.log(jnp.sum(jnp.exp(scores - row_peak), axis=-1, keepdims=True))
    attn_probs = jnp.exp(scores - log_total).astype(jnp.bfloat16)
    attn_mixed = jnp.einsum(
        "kgij,jkd->ikgd", attn_probs, v_half, preferred_element_type=jnp.float32
    )
    attn_mixed = attn_mixed.reshape(length, q_heads * head_size).astype(jnp.bfloat16)
    attn_sum = split_tensor_sum(jnp.dot(attn_mixed, w_out, preferred_element_type=jnp.float32))
    residual = tokens_wide + attn_sum
    scale_two = rms_scale(residual)
    normed_two = (residual * scale_two * ffn_gain).astype(jnp.bfloat16)
    gate_proj = jnp.dot(normed_two, w_gate, preferred_element_type=jnp.float32)
    up_proj = jnp.dot(normed_two, w_up, preferred_element_type=jnp.float32)
    gate_sigmoid = jax.nn.sigmoid(gate_proj)
    hidden = (gate_proj * gate_sigmoid * up_proj).astype(jnp.bfloat16)
    mlp_sum = split_tensor_sum(jnp.dot(hidden, w_down, preferred_element_type=jnp.float32))
    output = (residual + mlp_sum).astype(jnp.bfloat16)
    down_grad = outer(hidden, cotangent)
    hidden_grad = inner(cotangent, w_down)
    gate_grad = (
        hidden_grad * up_proj * gate_sigmoid * (1.0 + gate_proj * (1.0 - gate_sigmoid))
    ).astype(jnp.bfloat16)
    up_grad = (hidden_grad * gate_proj * gate_sigmoid).astype(jnp.bfloat16)
    gate_w_grad = outer(normed_two, gate_grad)
    up_w_grad = outer(normed_two, up_grad)
    ffn_w_grads, two_partial = lax.optimization_barrier(
        ((down_grad, gate_w_grad, up_w_grad), inner(gate_grad, w_gate) + inner(up_grad, w_up))
    )
    ffn_w_grads = lax.psum(ffn_w_grads, DP)
    normed_two_grad = split_tensor_sum(two_partial)
    ffn_grad = jnp.sum(normed_two_grad * residual * scale_two, axis=0)
    residual_grad = cotangent.astype(jnp.float32) + rms_back(
        normed_two_grad, residual, scale_two, ffn_gain
    )
    residual_half = residual_grad.astype(jnp.bfloat16)
    out_w_grad = outer(attn_mixed, residual_half)
    mixed_grad = (
        inner(residual_half, w_out)
        .astype(jnp.bfloat16)
        .reshape(length, kv_heads, groups, head_size)
    )
    attn_full = jnp.exp(score_table(q_rot, k_rot, allowed, factor) - log_total)
    probs_half = attn_full.astype(jnp.bfloat16)
    value_grad = jnp.einsum(
        "kgij,ikgd->jkd", probs_half, mixed_grad, preferred_element_type=jnp.float32
    ).astype(jnp.bfloat16)
    prob_grad = jnp.einsum("ikgd,jkd->kgij", mixed_grad, v_half, preferred_element_type=jnp.float32)
    row_delta = jnp.sum(attn_full * prob_grad, axis=-1, keepdims=True)
    score_grad = (attn_full * (prob_grad - row_delta) * factor).astype(jnp.bfloat16)
    q_rot_grad = jnp.einsum(
        "kgij,jkd->ikgd", score_grad, k_rot, preferred_element_type=jnp.float32
    ).reshape(length, q_heads, head_size)
    k_rot_grad = jnp.einsum("kgij,ikgd->jkd", score_grad, q_rot, preferred_element_type=jnp.float32)
    q_norm_grad = unrotate(q_rot_grad, cosine, sine_table)
    k_norm_grad = unrotate(k_rot_grad, cosine, sine_table)
    qgain_grad = jnp.sum(q_norm_grad * q_hat, axis=(0, 1))
    kgain_grad = jnp.sum(k_norm_grad * k_hat, axis=(0, 1))
    q_grad = (
        rms_back(q_norm_grad, q_raw, q_scale, query_gain)
        .astype(jnp.bfloat16)
        .reshape(length, q_heads * head_size)
    )
    k_grad = (
        rms_back(k_norm_grad, k_raw, k_scale, key_gain)
        .astype(jnp.bfloat16)
        .reshape(length, kv_heads * head_size)
    )
    v_grad = value_grad.reshape(length, kv_heads * head_size)
    query_w_grad = outer(normed_one, q_grad)
    key_w_grad = outer(normed_one, k_grad)
    value_w_grad = outer(normed_one, v_grad)
    one_partial = inner(q_grad, w_query) + inner(k_grad, w_key) + inner(v_grad, w_value)
    attn_part = jnp.sum(one_partial * tokens_wide * scale_one, axis=0)
    width = attn_part.shape[0]
    small = jnp.zeros((8, width), jnp.float32)
    small = small.at[0].set(ffn_grad).at[1].set(attn_part)
    small = small.at[2, :head_size].set(qgain_grad).at[2, head_size : 2 * head_size].set(kgain_grad)
    out_rows = out_w_grad.shape[0]
    ffn_w_grads, dp_sums, one_partial = lax.optimization_barrier(
        (
            ffn_w_grads,
            (query_w_grad, key_w_grad, value_w_grad, jnp.concatenate([out_w_grad, small])),
            one_partial,
        )
    )
    query_w_grad, key_w_grad, value_w_grad, out_pack = dp_sums
    q_cols = query_w_grad.shape[1]
    k_cols = key_w_grad.shape[1]
    width = out_pack.shape[1]
    flat = jnp.concatenate([query_w_grad, key_w_grad, value_w_grad], axis=1).reshape(-1, width)
    flat_rows = flat.shape[0]
    packed = jnp.concatenate([flat, out_pack], axis=0)
    padded_rows = -(-packed.shape[0] // 256) * 256
    packed = jnp.pad(packed, ((0, padded_rows - packed.shape[0]), (0, 0)))
    packed = ring_sum(packed, "dz", ("dc", "dx"))
    flat = packed[:flat_rows].reshape(query_w_grad.shape[0], -1)
    query_w_grad = flat[:, :q_cols]
    key_w_grad = flat[:, q_cols : q_cols + k_cols]
    value_w_grad = flat[:, q_cols + k_cols :]
    out_pack = packed[flat_rows : flat_rows + out_pack.shape[0]]
    down_grad, gate_w_grad, up_w_grad = ffn_w_grads
    normed_one_grad = tensor_sum(one_partial)
    input_grad = residual_grad + rms_back(normed_one_grad, tokens_wide, scale_one, attn_gain)
    out_w_grad = out_pack[:out_rows]
    ffn_grad = out_pack[out_rows]
    gains = small_tensor_sum(out_pack[out_rows + 1 : out_rows + 3])
    attn_grad = gains[0]
    qgain_grad = gains[1, :head_size]
    kgain_grad = gains[1, head_size : 2 * head_size]
    return (
        output,
        input_grad,
        attn_grad,
        query_w_grad,
        key_w_grad,
        value_w_grad,
        qgain_grad,
        kgain_grad,
        out_w_grad,
        ffn_grad,
        gate_w_grad,
        up_w_grad,
        down_grad,
    )


def solution(mesh):
    from jax.sharding import Mesh

    dp_size, tensor_size = mesh.devices.shape
    split = Mesh(
        mesh.devices.reshape(2, dp_size // 4, 2, tensor_size // 2, 2), DP + TENSOR
    )
    return jax.shard_map(
        per_device,
        mesh=split,
        in_specs=(
            P(DP, None),
            P(DP),
            P(),
            P(None, TENSOR),
            P(None, TENSOR),
            P(None, TENSOR),
            P(),
            P(),
            P(TENSOR, None),
            P(),
            P(None, TENSOR),
            P(None, TENSOR),
            P(TENSOR, None),
            P(DP, None),
        ),
        out_specs=(
            P(DP, None),
            P(DP, None),
            P(),
            P(None, TENSOR),
            P(None, TENSOR),
            P(None, TENSOR),
            P(),
            P(),
            P(TENSOR, None),
            P(),
            P(None, TENSOR),
            P(None, TENSOR),
            P(TENSOR, None),
        ),
        check_vma=False,
    )
```

```python
import math

import jax
import jax.numpy as jnp
from jax import lax
from jax.sharding import PartitionSpec as P

EPS = 1e-05
THETA = 1000000.0
TENSOR = ("ty", "tx")
DP = ("dx", "dz", "dc")


def outer(first_op, second_op):
    return lax.dot_general(
        first_op, second_op, (((0,), (0,)), ((), ())), preferred_element_type=jnp.float32
    )


def inner(first_op, second_op):
    return lax.dot_general(
        first_op, second_op, (((1,), (1,)), ((), ())), preferred_element_type=jnp.float32
    )


def rms_scale(values):
    return lax.rsqrt(jnp.mean(values * values, axis=-1, keepdims=True) + EPS)


def rms_back(upstream, values, inv_rms, gain_vec):
    normed = values * inv_rms
    weighted = upstream * gain_vec
    return inv_rms * (weighted - normed * jnp.mean(weighted * normed, axis=-1, keepdims=True))


def seq_layout(segment):
    length = segment.shape[0]
    ordinal = jnp.arange(length, dtype=jnp.int32)
    same_seq = segment[:, None] == segment[None, :]
    places = jnp.sum((same_seq & (ordinal[None, :] < ordinal[:, None])).astype(jnp.int32), axis=1)
    allowed = same_seq & (ordinal[None, :] <= ordinal[:, None])
    return (places, allowed)


def rope_tables(places, head_size):
    frequency = jnp.exp(
        jnp.arange(head_size // 2, dtype=jnp.float32) * (-2.0 * math.log(THETA) / head_size)
    )
    angles = places.astype(jnp.float32)[:, None] * frequency[None, :]
    angles = jnp.concatenate([angles, angles], axis=1)
    return (jnp.cos(angles), jnp.sin(angles))


def rotate(values, cosine, sine_table):
    half = values.shape[-1] // 2
    turned = jnp.concatenate([-values[..., half:], values[..., :half]], axis=-1)
    return values * cosine[:, None, :] + turned * sine_table[:, None, :]


def unrotate(incoming, cosine, sine_table):
    half = incoming.shape[-1] // 2
    scaled = incoming * sine_table[:, None, :]
    swapped = jnp.concatenate([scaled[..., half:], -scaled[..., :half]], axis=-1)
    return incoming * cosine[:, None, :] + swapped


def score_table(q_rot, k_rot, allowed, factor):
    raw = jnp.einsum("ikgd,jkd->kgij", q_rot, k_rot, preferred_element_type=jnp.float32) * factor
    return jnp.where(allowed[None, None], raw, -1e30)


def ring(size, shift):
    return [(i, (i + shift) % size) for i in range(size)]


def tensor_sum(values, extra=None):
    rows, cols = values.shape
    ny = lax.axis_size("ty")
    nx = lax.axis_size("tx")
    y = lax.axis_index("ty")
    h = lax.axis_index("tx")
    leaf = rows // (2 * ny * nx)
    parts = values.reshape(2, ny, nx, leaf, cols)
    pairs = ring(nx, 1)
    total = extra
    accs = []
    for way, shift in ((0, 1), (1, -1)):
        chunks = parts[way]
        acc = lax.dynamic_index_in_dim(chunks, (y - shift) % ny, 0, keepdims=False)
        passing = extra
        for step in range(1, ny):
            if way == 0 and extra is not None:
                acc, passing = lax.ppermute((acc, passing), "ty", ring(ny, shift))
                total = total + passing
            else:
                acc = lax.ppermute(acc, "ty", ring(ny, shift))
            acc = acc + lax.dynamic_index_in_dim(chunks, (y - shift * (1 + step)) % ny, 0, keepdims=False)
        accs.append(acc)
    acc = jnp.stack(accs)
    keep = lax.dynamic_index_in_dim(acc, h, 1, keepdims=False)
    send = lax.dynamic_index_in_dim(acc, (h + 1) % nx, 1, keepdims=False)
    if extra is not None:
        got, got_total = lax.ppermute((send, total), "tx", pairs)
        total = total + got_total
    else:
        got = lax.ppermute(send, "tx", pairs)
    mine = keep + got
    other = lax.ppermute(mine, "tx", pairs)
    both = jnp.where(h == 0, jnp.stack([mine, other], 1), jnp.stack([other, mine], 1))
    outs = []
    for way, shift in ((0, 1), (1, -1)):
        cur = both[way]
        gathered = jnp.zeros((ny,) + cur.shape, values.dtype)
        gathered = lax.dynamic_update_index_in_dim(gathered, cur, y, 0)
        for step in range(1, ny):
            cur = lax.ppermute(cur, "ty", ring(ny, shift))
            gathered = lax.dynamic_update_index_in_dim(gathered, cur, (y - shift * step) % ny, 0)
        outs.append(gathered)
    result = jnp.stack(outs).reshape(rows, cols)
    if extra is None:
        return result
    return result, total


def split_tensor_sum(values, pieces=2):
    blocks = jnp.split(values, pieces, axis=0)
    return jnp.concatenate([tensor_sum(block) for block in blocks], axis=0)


def ring_sum(values, ring_axis, pair_axes):
    rows, cols = values.shape
    size = lax.axis_size(ring_axis)
    here = lax.axis_index(ring_axis)
    parts = values.reshape(2, size, rows // (2 * size), cols)
    accs = []
    for way, shift in ((0, 1), (1, -1)):
        chunks = parts[way]
        acc = lax.dynamic_index_in_dim(chunks, (here - shift) % size, 0, keepdims=False)
        for step in range(1, size):
            acc = lax.ppermute(acc, ring_axis, ring(size, shift))
            acc = acc + lax.dynamic_index_in_dim(chunks, (here - shift * (1 + step)) % size, 0, keepdims=False)
        accs.append(acc)
    acc = jnp.stack(accs)
    sides = []
    for axis in pair_axes:
        side = lax.axis_index(axis)
        halves = acc.reshape(2, 2, acc.shape[1] // 2, cols)
        keep = lax.dynamic_index_in_dim(halves, side, 1, keepdims=False)
        send = lax.dynamic_index_in_dim(halves, 1 - side, 1, keepdims=False)
        acc = keep + lax.ppermute(send, axis, [(0, 1), (1, 0)])
        sides.append(side)
    for axis, side in zip(pair_axes[::-1], sides[::-1]):
        other = lax.ppermute(acc, axis, [(0, 1), (1, 0)])
        both = jnp.where(side == 0, jnp.stack([acc, other], 1), jnp.stack([other, acc], 1))
        acc = both.reshape(2, 2 * acc.shape[1], cols)
    outs = []
    for way, shift in ((0, 1), (1, -1)):
        cur = acc[way]
        gathered = jnp.zeros((size,) + cur.shape, values.dtype)
        gathered = lax.dynamic_update_index_in_dim(gathered, cur, here, 0)
        for step in range(1, size):
            cur = lax.ppermute(cur, ring_axis, ring(size, shift))
            gathered = lax.dynamic_update_index_in_dim(gathered, cur, (here - shift * step) % size, 0)
        outs.append(gathered)
    return jnp.stack(outs).reshape(rows, cols)


def small_tensor_sum(values):
    ny = lax.axis_size("ty")
    nx = lax.axis_size("tx")
    dist = 1
    while dist < ny:
        values = values + lax.ppermute(values, "ty", [(i, i ^ dist) for i in range(ny)])
        dist *= 2
    dist = 1
    while dist < nx:
        values = values + lax.ppermute(values, "tx", [(i, i ^ dist) for i in range(nx)])
        dist *= 2
    return values


def per_device(
    tokens,
    segment_ids,
    attn_gain,
    w_query,
    w_key,
    w_value,
    query_gain,
    key_gain,
    w_out,
    ffn_gain,
    w_gate,
    w_up,
    w_down,
    cotangent,
):
    length = tokens.shape[0]
    head_size = query_gain.shape[0]
    q_heads = w_query.shape[1] // head_size
    kv_heads = w_key.shape[1] // head_size
    groups = q_heads // kv_heads
    factor = 1.0 / math.sqrt(head_size)
    places, allowed = seq_layout(segment_ids)
    cosine, sine_table = rope_tables(places, head_size)
    tokens_wide = tokens.astype(jnp.float32)
    scale_one = rms_scale(tokens_wide)
    normed_one = (tokens_wide * scale_one * attn_gain).astype(jnp.bfloat16)
    q_raw = jnp.dot(normed_one, w_query, preferred_element_type=jnp.float32).reshape(
        length, q_heads, head_size
    )
    k_raw = jnp.dot(normed_one, w_key, preferred_element_type=jnp.float32).reshape(
        length, kv_heads, head_size
    )
    v_half = (
        jnp.dot(normed_one, w_value, preferred_element_type=jnp.float32)
        .astype(jnp.bfloat16)
        .reshape(length, kv_heads, head_size)
    )
    q_scale = rms_scale(q_raw)
    k_scale = rms_scale(k_raw)
    q_hat = q_raw * q_scale
    k_hat = k_raw * k_scale
    q_rot = (
        rotate(q_hat * query_gain, cosine, sine_table)
        .astype(jnp.bfloat16)
        .reshape(length, kv_heads, groups, head_size)
    )
    k_rot = rotate(k_hat * key_gain, cosine, sine_table).astype(jnp.bfloat16)
    scores = score_table(q_rot, k_rot, allowed, factor)
    row_peak = jnp.max(scores, axis=-1, keepdims=True)
    log_total = row_peak + jnp.log(jnp.sum(jnp.exp(scores - row_peak), axis=-1, keepdims=True))
    attn_probs = jnp.exp(scores - log_total).astype(jnp.bfloat16)
    attn_mixed = jnp.einsum(
        "kgij,jkd->ikgd", attn_probs, v_half, preferred_element_type=jnp.float32
    )
    attn_mixed = attn_mixed.reshape(length, q_heads * head_size).astype(jnp.bfloat16)
    attn_sum = split_tensor_sum(jnp.dot(attn_mixed, w_out, preferred_element_type=jnp.float32))
    residual = tokens_wide + attn_sum
    scale_two = rms_scale(residual)
    normed_two = (residual * scale_two * ffn_gain).astype(jnp.bfloat16)
    gate_proj = jnp.dot(normed_two, w_gate, preferred_element_type=jnp.float32)
    up_proj = jnp.dot(normed_two, w_up, preferred_element_type=jnp.float32)
    gate_sigmoid = jax.nn.sigmoid(gate_proj)
    hidden = (gate_proj * gate_sigmoid * up_proj).astype(jnp.bfloat16)
    mlp_sum = tensor_sum(jnp.dot(hidden, w_down, preferred_element_type=jnp.float32))
    output = (residual + mlp_sum).astype(jnp.bfloat16)
    down_grad = outer(hidden, cotangent)
    hidden_grad = inner(cotangent, w_down)
    gate_grad = (
        hidden_grad * up_proj * gate_sigmoid * (1.0 + gate_proj * (1.0 - gate_sigmoid))
    ).astype(jnp.bfloat16)
    up_grad = (hidden_grad * gate_proj * gate_sigmoid).astype(jnp.bfloat16)
    gate_w_grad = outer(normed_two, gate_grad)
    up_w_grad = outer(normed_two, up_grad)
    ffn_w_grads, two_partial = lax.optimization_barrier(
        ((down_grad, gate_w_grad, up_w_grad), inner(gate_grad, w_gate) + inner(up_grad, w_up))
    )
    ffn_w_grads = lax.psum(ffn_w_grads, DP)
    normed_two_grad = split_tensor_sum(two_partial)
    ffn_grad = jnp.sum(normed_two_grad * residual * scale_two, axis=0)
    residual_grad = cotangent.astype(jnp.float32) + rms_back(
        normed_two_grad, residual, scale_two, ffn_gain
    )
    residual_half = residual_grad.astype(jnp.bfloat16)
    out_w_grad = outer(attn_mixed, residual_half)
    mixed_grad = (
        inner(residual_half, w_out)
        .astype(jnp.bfloat16)
        .reshape(length, kv_heads, groups, head_size)
    )
    attn_full = jnp.exp(score_table(q_rot, k_rot, allowed, factor) - log_total)
    probs_half = attn_full.astype(jnp.bfloat16)
    value_grad = jnp.einsum(
        "kgij,ikgd->jkd", probs_half, mixed_grad, preferred_element_type=jnp.float32
    ).astype(jnp.bfloat16)
    prob_grad = jnp.einsum("ikgd,jkd->kgij", mixed_grad, v_half, preferred_element_type=jnp.float32)
    row_delta = jnp.sum(attn_full * prob_grad, axis=-1, keepdims=True)
    score_grad = (attn_full * (prob_grad - row_delta) * factor).astype(jnp.bfloat16)
    q_rot_grad = jnp.einsum(
        "kgij,jkd->ikgd", score_grad, k_rot, preferred_element_type=jnp.float32
    ).reshape(length, q_heads, head_size)
    k_rot_grad = jnp.einsum("kgij,ikgd->jkd", score_grad, q_rot, preferred_element_type=jnp.float32)
    q_norm_grad = unrotate(q_rot_grad, cosine, sine_table)
    k_norm_grad = unrotate(k_rot_grad, cosine, sine_table)
    qgain_grad = jnp.sum(q_norm_grad * q_hat, axis=(0, 1))
    kgain_grad = jnp.sum(k_norm_grad * k_hat, axis=(0, 1))
    q_grad = (
        rms_back(q_norm_grad, q_raw, q_scale, query_gain)
        .astype(jnp.bfloat16)
        .reshape(length, q_heads * head_size)
    )
    k_grad = (
        rms_back(k_norm_grad, k_raw, k_scale, key_gain)
        .astype(jnp.bfloat16)
        .reshape(length, kv_heads * head_size)
    )
    v_grad = value_grad.reshape(length, kv_heads * head_size)
    query_w_grad = outer(normed_one, q_grad)
    key_w_grad = outer(normed_one, k_grad)
    value_w_grad = outer(normed_one, v_grad)
    one_partial = inner(q_grad, w_query) + inner(k_grad, w_key) + inner(v_grad, w_value)
    attn_part = jnp.sum(one_partial * tokens_wide * scale_one, axis=0)
    width = attn_part.shape[0]
    small = jnp.zeros((8, width), jnp.float32)
    small = small.at[0].set(ffn_grad).at[1].set(attn_part)
    small = small.at[2, :head_size].set(qgain_grad).at[2, head_size : 2 * head_size].set(kgain_grad)
    out_rows = out_w_grad.shape[0]
    ffn_w_grads, dp_sums, one_partial = lax.optimization_barrier(
        (
            ffn_w_grads,
            (query_w_grad, key_w_grad, value_w_grad, jnp.concatenate([out_w_grad, small])),
            one_partial,
        )
    )
    query_w_grad, key_w_grad, value_w_grad, out_pack = dp_sums
    q_cols = query_w_grad.shape[1]
    k_cols = key_w_grad.shape[1]
    width = out_pack.shape[1]
    flat = jnp.concatenate([query_w_grad, key_w_grad, value_w_grad], axis=1).reshape(-1, width)
    flat_rows = flat.shape[0]
    packed = jnp.concatenate([flat, out_pack], axis=0)
    padded_rows = -(-packed.shape[0] // 256) * 256
    packed = jnp.pad(packed, ((0, padded_rows - packed.shape[0]), (0, 0)))
    packed = ring_sum(packed, "dz", ("dc", "dx"))
    flat = packed[:flat_rows].reshape(query_w_grad.shape[0], -1)
    query_w_grad = flat[:, :q_cols]
    key_w_grad = flat[:, q_cols : q_cols + k_cols]
    value_w_grad = flat[:, q_cols + k_cols :]
    out_pack = packed[flat_rows : flat_rows + out_pack.shape[0]]
    down_grad, gate_w_grad, up_w_grad = ffn_w_grads
    normed_one_grad = split_tensor_sum(one_partial)
    input_grad = residual_grad + rms_back(normed_one_grad, tokens_wide, scale_one, attn_gain)
    out_w_grad = out_pack[:out_rows]
    ffn_grad = out_pack[out_rows]
    gains = small_tensor_sum(out_pack[out_rows + 1 : out_rows + 3])
    attn_grad = gains[0]
    qgain_grad = gains[1, :head_size]
    kgain_grad = gains[1, head_size : 2 * head_size]
    return (
        output,
        input_grad,
        attn_grad,
        query_w_grad,
        key_w_grad,
        value_w_grad,
        qgain_grad,
        kgain_grad,
        out_w_grad,
        ffn_grad,
        gate_w_grad,
        up_w_grad,
        down_grad,
    )


def solution(mesh):
    from jax.sharding import Mesh

    dp_size, tensor_size = mesh.devices.shape
    split = Mesh(
        mesh.devices.reshape(2, dp_size // 4, 2, tensor_size // 2, 2), DP + TENSOR
    )
    return jax.shard_map(
        per_device,
        mesh=split,
        in_specs=(
            P(DP, None),
            P(DP),
            P(),
            P(None, TENSOR),
            P(None, TENSOR),
            P(None, TENSOR),
            P(),
            P(),
            P(TENSOR, None),
            P(),
            P(None, TENSOR),
            P(None, TENSOR),
            P(TENSOR, None),
            P(DP, None),
        ),
        out_specs=(
            P(DP, None),
            P(DP, None),
            P(),
            P(None, TENSOR),
            P(None, TENSOR),
            P(None, TENSOR),
            P(),
            P(),
            P(TENSOR, None),
            P(),
            P(None, TENSOR),
            P(None, TENSOR),
            P(TENSOR, None),
        ),
        check_vma=False,
    )
```

```python
import math

import jax
import jax.numpy as jnp
from jax import lax
from jax.sharding import PartitionSpec as P

EPS = 1e-05
THETA = 1000000.0
TENSOR = ("ty", "tx")
DP = ("dx", "dz", "dc")


def outer(first_op, second_op):
    return lax.dot_general(
        first_op, second_op, (((0,), (0,)), ((), ())), preferred_element_type=jnp.float32
    )


def inner(first_op, second_op):
    return lax.dot_general(
        first_op, second_op, (((1,), (1,)), ((), ())), preferred_element_type=jnp.float32
    )


def rms_scale(values):
    return lax.rsqrt(jnp.mean(values * values, axis=-1, keepdims=True) + EPS)


def rms_back(upstream, values, inv_rms, gain_vec):
    normed = values * inv_rms
    weighted = upstream * gain_vec
    return inv_rms * (weighted - normed * jnp.mean(weighted * normed, axis=-1, keepdims=True))


def seq_layout(segment):
    length = segment.shape[0]
    ordinal = jnp.arange(length, dtype=jnp.int32)
    same_seq = segment[:, None] == segment[None, :]
    places = jnp.sum((same_seq & (ordinal[None, :] < ordinal[:, None])).astype(jnp.int32), axis=1)
    allowed = same_seq & (ordinal[None, :] <= ordinal[:, None])
    return (places, allowed)


def rope_tables(places, head_size):
    frequency = jnp.exp(
        jnp.arange(head_size // 2, dtype=jnp.float32) * (-2.0 * math.log(THETA) / head_size)
    )
    angles = places.astype(jnp.float32)[:, None] * frequency[None, :]
    angles = jnp.concatenate([angles, angles], axis=1)
    return (jnp.cos(angles), jnp.sin(angles))


def rotate(values, cosine, sine_table):
    half = values.shape[-1] // 2
    turned = jnp.concatenate([-values[..., half:], values[..., :half]], axis=-1)
    return values * cosine[:, None, :] + turned * sine_table[:, None, :]


def unrotate(incoming, cosine, sine_table):
    half = incoming.shape[-1] // 2
    scaled = incoming * sine_table[:, None, :]
    swapped = jnp.concatenate([scaled[..., half:], -scaled[..., :half]], axis=-1)
    return incoming * cosine[:, None, :] + swapped


def score_table(q_rot, k_rot, allowed, factor):
    raw = jnp.einsum("ikgd,jkd->kgij", q_rot, k_rot, preferred_element_type=jnp.float32) * factor
    return jnp.where(allowed[None, None], raw, -1e30)


def ring(size, shift):
    return [(i, (i + shift) % size) for i in range(size)]


def tensor_sum(values, extra=None):
    rows, cols = values.shape
    ny = lax.axis_size("ty")
    nx = lax.axis_size("tx")
    y = lax.axis_index("ty")
    h = lax.axis_index("tx")
    leaf = rows // (2 * ny * nx)
    parts = values.reshape(2, ny, nx, leaf, cols)
    pairs = ring(nx, 1)
    total = extra
    accs = []
    for way, shift in ((0, 1), (1, -1)):
        chunks = parts[way]
        acc = lax.dynamic_index_in_dim(chunks, (y - shift) % ny, 0, keepdims=False)
        passing = extra
        for step in range(1, ny):
            if way == 0 and extra is not None:
                acc, passing = lax.ppermute((acc, passing), "ty", ring(ny, shift))
                total = total + passing
            else:
                acc = lax.ppermute(acc, "ty", ring(ny, shift))
            acc = acc + lax.dynamic_index_in_dim(chunks, (y - shift * (1 + step)) % ny, 0, keepdims=False)
        accs.append(acc)
    acc = jnp.stack(accs)
    keep = lax.dynamic_index_in_dim(acc, h, 1, keepdims=False)
    send = lax.dynamic_index_in_dim(acc, (h + 1) % nx, 1, keepdims=False)
    if extra is not None:
        got, got_total = lax.ppermute((send, total), "tx", pairs)
        total = total + got_total
    else:
        got = lax.ppermute(send, "tx", pairs)
    mine = keep + got
    other = lax.ppermute(mine, "tx", pairs)
    both = jnp.where(h == 0, jnp.stack([mine, other], 1), jnp.stack([other, mine], 1))
    outs = []
    for way, shift in ((0, 1), (1, -1)):
        cur = both[way]
        gathered = jnp.zeros((ny,) + cur.shape, values.dtype)
        gathered = lax.dynamic_update_index_in_dim(gathered, cur, y, 0)
        for step in range(1, ny):
            cur = lax.ppermute(cur, "ty", ring(ny, shift))
            gathered = lax.dynamic_update_index_in_dim(gathered, cur, (y - shift * step) % ny, 0)
        outs.append(gathered)
    result = jnp.stack(outs).reshape(rows, cols)
    if extra is None:
        return result
    return result, total


def split_tensor_sum(values, pieces=2):
    blocks = jnp.split(values, pieces, axis=0)
    return jnp.concatenate([tensor_sum(block) for block in blocks], axis=0)


def ring_sum(values, ring_axis, pair_axes):
    rows, cols = values.shape
    size = lax.axis_size(ring_axis)
    here = lax.axis_index(ring_axis)
    parts = values.reshape(2, size, rows // (2 * size), cols)
    accs = []
    for way, shift in ((0, 1), (1, -1)):
        chunks = parts[way]
        acc = lax.dynamic_index_in_dim(chunks, (here - shift) % size, 0, keepdims=False)
        for step in range(1, size):
            acc = lax.ppermute(acc, ring_axis, ring(size, shift))
            acc = acc + lax.dynamic_index_in_dim(chunks, (here - shift * (1 + step)) % size, 0, keepdims=False)
        accs.append(acc)
    acc = jnp.stack(accs)
    for axis in pair_axes:
        acc = acc + lax.ppermute(acc, axis, [(0, 1), (1, 0)])
    outs = []
    for way, shift in ((0, 1), (1, -1)):
        cur = acc[way]
        gathered = jnp.zeros((size,) + cur.shape, values.dtype)
        gathered = lax.dynamic_update_index_in_dim(gathered, cur, here, 0)
        for step in range(1, size):
            cur = lax.ppermute(cur, ring_axis, ring(size, shift))
            gathered = lax.dynamic_update_index_in_dim(gathered, cur, (here - shift * step) % size, 0)
        outs.append(gathered)
    return jnp.stack(outs).reshape(rows, cols)


def small_tensor_sum(values):
    ny = lax.axis_size("ty")
    nx = lax.axis_size("tx")
    dist = 1
    while dist < ny:
        values = values + lax.ppermute(values, "ty", [(i, i ^ dist) for i in range(ny)])
        dist *= 2
    dist = 1
    while dist < nx:
        values = values + lax.ppermute(values, "tx", [(i, i ^ dist) for i in range(nx)])
        dist *= 2
    return values


def per_device(
    tokens,
    segment_ids,
    attn_gain,
    w_query,
    w_key,
    w_value,
    query_gain,
    key_gain,
    w_out,
    ffn_gain,
    w_gate,
    w_up,
    w_down,
    cotangent,
):
    length = tokens.shape[0]
    head_size = query_gain.shape[0]
    q_heads = w_query.shape[1] // head_size
    kv_heads = w_key.shape[1] // head_size
    groups = q_heads // kv_heads
    factor = 1.0 / math.sqrt(head_size)
    places, allowed = seq_layout(segment_ids)
    cosine, sine_table = rope_tables(places, head_size)
    tokens_wide = tokens.astype(jnp.float32)
    scale_one = rms_scale(tokens_wide)
    normed_one = (tokens_wide * scale_one * attn_gain).astype(jnp.bfloat16)
    q_raw = jnp.dot(normed_one, w_query, preferred_element_type=jnp.float32).reshape(
        length, q_heads, head_size
    )
    k_raw = jnp.dot(normed_one, w_key, preferred_element_type=jnp.float32).reshape(
        length, kv_heads, head_size
    )
    v_half = (
        jnp.dot(normed_one, w_value, preferred_element_type=jnp.float32)
        .astype(jnp.bfloat16)
        .reshape(length, kv_heads, head_size)
    )
    q_scale = rms_scale(q_raw)
    k_scale = rms_scale(k_raw)
    q_hat = q_raw * q_scale
    k_hat = k_raw * k_scale
    q_rot = (
        rotate(q_hat * query_gain, cosine, sine_table)
        .astype(jnp.bfloat16)
        .reshape(length, kv_heads, groups, head_size)
    )
    k_rot = rotate(k_hat * key_gain, cosine, sine_table).astype(jnp.bfloat16)
    scores = score_table(q_rot, k_rot, allowed, factor)
    row_peak = jnp.max(scores, axis=-1, keepdims=True)
    log_total = row_peak + jnp.log(jnp.sum(jnp.exp(scores - row_peak), axis=-1, keepdims=True))
    attn_probs = jnp.exp(scores - log_total).astype(jnp.bfloat16)
    attn_mixed = jnp.einsum(
        "kgij,jkd->ikgd", attn_probs, v_half, preferred_element_type=jnp.float32
    )
    attn_mixed = attn_mixed.reshape(length, q_heads * head_size).astype(jnp.bfloat16)
    attn_sum = split_tensor_sum(jnp.dot(attn_mixed, w_out, preferred_element_type=jnp.float32))
    residual = tokens_wide + attn_sum
    scale_two = rms_scale(residual)
    normed_two = (residual * scale_two * ffn_gain).astype(jnp.bfloat16)
    gate_proj = jnp.dot(normed_two, w_gate, preferred_element_type=jnp.float32)
    up_proj = jnp.dot(normed_two, w_up, preferred_element_type=jnp.float32)
    gate_sigmoid = jax.nn.sigmoid(gate_proj)
    hidden = (gate_proj * gate_sigmoid * up_proj).astype(jnp.bfloat16)
    mlp_sum = tensor_sum(jnp.dot(hidden, w_down, preferred_element_type=jnp.float32))
    output = (residual + mlp_sum).astype(jnp.bfloat16)
    down_grad = outer(hidden, cotangent)
    hidden_grad = inner(cotangent, w_down)
    gate_grad = (
        hidden_grad * up_proj * gate_sigmoid * (1.0 + gate_proj * (1.0 - gate_sigmoid))
    ).astype(jnp.bfloat16)
    up_grad = (hidden_grad * gate_proj * gate_sigmoid).astype(jnp.bfloat16)
    gate_w_grad = outer(normed_two, gate_grad)
    up_w_grad = outer(normed_two, up_grad)
    ffn_w_grads, two_partial = lax.optimization_barrier(
        ((down_grad, gate_w_grad, up_w_grad), inner(gate_grad, w_gate) + inner(up_grad, w_up))
    )
    ffn_w_grads = lax.psum(ffn_w_grads, DP)
    normed_two_grad = split_tensor_sum(two_partial)
    ffn_grad = jnp.sum(normed_two_grad * residual * scale_two, axis=0)
    residual_grad = cotangent.astype(jnp.float32) + rms_back(
        normed_two_grad, residual, scale_two, ffn_gain
    )
    residual_half = residual_grad.astype(jnp.bfloat16)
    out_w_grad = outer(attn_mixed, residual_half)
    mixed_grad = (
        inner(residual_half, w_out)
        .astype(jnp.bfloat16)
        .reshape(length, kv_heads, groups, head_size)
    )
    attn_full = jnp.exp(score_table(q_rot, k_rot, allowed, factor) - log_total)
    probs_half = attn_full.astype(jnp.bfloat16)
    value_grad = jnp.einsum(
        "kgij,ikgd->jkd", probs_half, mixed_grad, preferred_element_type=jnp.float32
    ).astype(jnp.bfloat16)
    prob_grad = jnp.einsum("ikgd,jkd->kgij", mixed_grad, v_half, preferred_element_type=jnp.float32)
    row_delta = jnp.sum(attn_full * prob_grad, axis=-1, keepdims=True)
    score_grad = (attn_full * (prob_grad - row_delta) * factor).astype(jnp.bfloat16)
    q_rot_grad = jnp.einsum(
        "kgij,jkd->ikgd", score_grad, k_rot, preferred_element_type=jnp.float32
    ).reshape(length, q_heads, head_size)
    k_rot_grad = jnp.einsum("kgij,ikgd->jkd", score_grad, q_rot, preferred_element_type=jnp.float32)
    q_norm_grad = unrotate(q_rot_grad, cosine, sine_table)
    k_norm_grad = unrotate(k_rot_grad, cosine, sine_table)
    qgain_grad = jnp.sum(q_norm_grad * q_hat, axis=(0, 1))
    kgain_grad = jnp.sum(k_norm_grad * k_hat, axis=(0, 1))
    q_grad = (
        rms_back(q_norm_grad, q_raw, q_scale, query_gain)
        .astype(jnp.bfloat16)
        .reshape(length, q_heads * head_size)
    )
    k_grad = (
        rms_back(k_norm_grad, k_raw, k_scale, key_gain)
        .astype(jnp.bfloat16)
        .reshape(length, kv_heads * head_size)
    )
    v_grad = value_grad.reshape(length, kv_heads * head_size)
    query_w_grad = outer(normed_one, q_grad)
    key_w_grad = outer(normed_one, k_grad)
    value_w_grad = outer(normed_one, v_grad)
    one_partial = inner(q_grad, w_query) + inner(k_grad, w_key) + inner(v_grad, w_value)
    attn_part = jnp.sum(one_partial * tokens_wide * scale_one, axis=0)
    width = attn_part.shape[0]
    small = jnp.zeros((8, width), jnp.float32)
    small = small.at[0].set(ffn_grad).at[1].set(attn_part)
    small = small.at[2, :head_size].set(qgain_grad).at[2, head_size : 2 * head_size].set(kgain_grad)
    out_rows = out_w_grad.shape[0]
    ffn_w_grads, dp_sums, one_partial = lax.optimization_barrier(
        (
            ffn_w_grads,
            (query_w_grad, key_w_grad, value_w_grad, jnp.concatenate([out_w_grad, small])),
            one_partial,
        )
    )
    query_w_grad, key_w_grad, value_w_grad, out_pack = dp_sums
    q_cols = query_w_grad.shape[1]
    k_cols = key_w_grad.shape[1]
    width = out_pack.shape[1]
    flat = jnp.concatenate([query_w_grad, key_w_grad, value_w_grad], axis=1).reshape(-1, width)
    flat_rows = flat.shape[0]
    packed = jnp.concatenate([flat, out_pack], axis=0)
    padded_rows = -(-packed.shape[0] // 256) * 256
    packed = jnp.pad(packed, ((0, padded_rows - packed.shape[0]), (0, 0)))
    packed = ring_sum(packed, "dz", ("dc", "dx"))
    flat = packed[:flat_rows].reshape(query_w_grad.shape[0], -1)
    query_w_grad = flat[:, :q_cols]
    key_w_grad = flat[:, q_cols : q_cols + k_cols]
    value_w_grad = flat[:, q_cols + k_cols :]
    out_pack = packed[flat_rows : flat_rows + out_pack.shape[0]]
    down_grad, gate_w_grad, up_w_grad = ffn_w_grads
    normed_one_grad = split_tensor_sum(one_partial)
    input_grad = residual_grad + rms_back(normed_one_grad, tokens_wide, scale_one, attn_gain)
    out_w_grad = out_pack[:out_rows]
    ffn_grad = out_pack[out_rows]
    gains = small_tensor_sum(out_pack[out_rows + 1 : out_rows + 3])
    attn_grad = gains[0]
    qgain_grad = gains[1, :head_size]
    kgain_grad = gains[1, head_size : 2 * head_size]
    return (
        output,
        input_grad,
        attn_grad,
        query_w_grad,
        key_w_grad,
        value_w_grad,
        qgain_grad,
        kgain_grad,
        out_w_grad,
        ffn_grad,
        gate_w_grad,
        up_w_grad,
        down_grad,
    )


def solution(mesh):
    from jax.sharding import Mesh

    dp_size, tensor_size = mesh.devices.shape
    split = Mesh(
        mesh.devices.reshape(2, dp_size // 4, 2, tensor_size // 2, 2), DP + TENSOR
    )
    return jax.shard_map(
        per_device,
        mesh=split,
        in_specs=(
            P(DP, None),
            P(DP),
            P(),
            P(None, TENSOR),
            P(None, TENSOR),
            P(None, TENSOR),
            P(),
            P(),
            P(TENSOR, None),
            P(),
            P(None, TENSOR),
            P(None, TENSOR),
            P(TENSOR, None),
            P(DP, None),
        ),
        out_specs=(
            P(DP, None),
            P(DP, None),
            P(),
            P(None, TENSOR),
            P(None, TENSOR),
            P(None, TENSOR),
            P(),
            P(),
            P(TENSOR, None),
            P(),
            P(None, TENSOR),
            P(None, TENSOR),
            P(TENSOR, None),
        ),
        check_vma=False,
    )
```

```python
import math

import jax
import jax.numpy as jnp
from jax import lax
from jax.sharding import PartitionSpec as P

EPS = 1e-05
THETA = 1000000.0
TENSOR = ("ty", "tx")
DP = ("dx", "dz", "dc")


def outer(first_op, second_op):
    return lax.dot_general(
        first_op, second_op, (((0,), (0,)), ((), ())), preferred_element_type=jnp.float32
    )


def inner(first_op, second_op):
    return lax.dot_general(
        first_op, second_op, (((1,), (1,)), ((), ())), preferred_element_type=jnp.float32
    )


def rms_scale(values):
    return lax.rsqrt(jnp.mean(values * values, axis=-1, keepdims=True) + EPS)


def rms_back(upstream, values, inv_rms, gain_vec):
    normed = values * inv_rms
    weighted = upstream * gain_vec
    return inv_rms * (weighted - normed * jnp.mean(weighted * normed, axis=-1, keepdims=True))


def seq_layout(segment):
    length = segment.shape[0]
    ordinal = jnp.arange(length, dtype=jnp.int32)
    same_seq = segment[:, None] == segment[None, :]
    places = jnp.sum((same_seq & (ordinal[None, :] < ordinal[:, None])).astype(jnp.int32), axis=1)
    allowed = same_seq & (ordinal[None, :] <= ordinal[:, None])
    return (places, allowed)


def rope_tables(places, head_size):
    frequency = jnp.exp(
        jnp.arange(head_size // 2, dtype=jnp.float32) * (-2.0 * math.log(THETA) / head_size)
    )
    angles = places.astype(jnp.float32)[:, None] * frequency[None, :]
    angles = jnp.concatenate([angles, angles], axis=1)
    return (jnp.cos(angles), jnp.sin(angles))


def rotate(values, cosine, sine_table):
    half = values.shape[-1] // 2
    turned = jnp.concatenate([-values[..., half:], values[..., :half]], axis=-1)
    return values * cosine[:, None, :] + turned * sine_table[:, None, :]


def unrotate(incoming, cosine, sine_table):
    half = incoming.shape[-1] // 2
    scaled = incoming * sine_table[:, None, :]
    swapped = jnp.concatenate([scaled[..., half:], -scaled[..., :half]], axis=-1)
    return incoming * cosine[:, None, :] + swapped


def score_table(q_rot, k_rot, allowed, factor):
    raw = jnp.einsum("ikgd,jkd->kgij", q_rot, k_rot, preferred_element_type=jnp.float32) * factor
    return jnp.where(allowed[None, None], raw, -1e30)


def ring(size, shift):
    return [(i, (i + shift) % size) for i in range(size)]


def tensor_sum(values, extra=None):
    rows, cols = values.shape
    ny = lax.axis_size("ty")
    nx = lax.axis_size("tx")
    y = lax.axis_index("ty")
    h = lax.axis_index("tx")
    leaf = rows // (2 * ny * nx)
    parts = values.reshape(2, ny, nx, leaf, cols)
    pairs = ring(nx, 1)
    total = extra
    accs = []
    for way, shift in ((0, 1), (1, -1)):
        chunks = parts[way]
        acc = lax.dynamic_index_in_dim(chunks, (y - shift) % ny, 0, keepdims=False)
        passing = extra
        for step in range(1, ny):
            if way == 0 and extra is not None:
                acc, passing = lax.ppermute((acc, passing), "ty", ring(ny, shift))
                total = total + passing
            else:
                acc = lax.ppermute(acc, "ty", ring(ny, shift))
            acc = acc + lax.dynamic_index_in_dim(chunks, (y - shift * (1 + step)) % ny, 0, keepdims=False)
        accs.append(acc)
    acc = jnp.stack(accs)
    keep = lax.dynamic_index_in_dim(acc, h, 1, keepdims=False)
    send = lax.dynamic_index_in_dim(acc, (h + 1) % nx, 1, keepdims=False)
    if extra is not None:
        got, got_total = lax.ppermute((send, total), "tx", pairs)
        total = total + got_total
    else:
        got = lax.ppermute(send, "tx", pairs)
    mine = keep + got
    other = lax.ppermute(mine, "tx", pairs)
    both = jnp.where(h == 0, jnp.stack([mine, other], 1), jnp.stack([other, mine], 1))
    outs = []
    for way, shift in ((0, 1), (1, -1)):
        cur = both[way]
        gathered = jnp.zeros((ny,) + cur.shape, values.dtype)
        gathered = lax.dynamic_update_index_in_dim(gathered, cur, y, 0)
        for step in range(1, ny):
            cur = lax.ppermute(cur, "ty", ring(ny, shift))
            gathered = lax.dynamic_update_index_in_dim(gathered, cur, (y - shift * step) % ny, 0)
        outs.append(gathered)
    result = jnp.stack(outs).reshape(rows, cols)
    if extra is None:
        return result
    return result, total


def split_tensor_sum(values, pieces=2):
    blocks = jnp.split(values, pieces, axis=0)
    return jnp.concatenate([tensor_sum(block) for block in blocks], axis=0)


def ring_sum(values, ring_axis, pair_axes):
    rows, cols = values.shape
    size = lax.axis_size(ring_axis)
    here = lax.axis_index(ring_axis)
    parts = values.reshape(2, size, rows // (2 * size), cols)
    accs = []
    for way, shift in ((0, 1), (1, -1)):
        chunks = parts[way]
        acc = lax.dynamic_index_in_dim(chunks, (here - shift) % size, 0, keepdims=False)
        for step in range(1, size):
            acc = lax.ppermute(acc, ring_axis, ring(size, shift))
            acc = acc + lax.dynamic_index_in_dim(chunks, (here - shift * (1 + step)) % size, 0, keepdims=False)
        accs.append(acc)
    acc = jnp.stack(accs)
    sides = []
    for axis in pair_axes:
        side = lax.axis_index(axis)
        halves = acc.reshape(2, 2, acc.shape[1] // 2, cols)
        keep = lax.dynamic_index_in_dim(halves, side, 1, keepdims=False)
        send = lax.dynamic_index_in_dim(halves, 1 - side, 1, keepdims=False)
        acc = keep + lax.ppermute(send, axis, [(0, 1), (1, 0)])
        sides.append(side)
    for axis, side in zip(pair_axes[::-1], sides[::-1]):
        other = lax.ppermute(acc, axis, [(0, 1), (1, 0)])
        both = jnp.where(side == 0, jnp.stack([acc, other], 1), jnp.stack([other, acc], 1))
        acc = both.reshape(2, 2 * acc.shape[1], cols)
    outs = []
    for way, shift in ((0, 1), (1, -1)):
        cur = acc[way]
        gathered = jnp.zeros((size,) + cur.shape, values.dtype)
        gathered = lax.dynamic_update_index_in_dim(gathered, cur, here, 0)
        for step in range(1, size):
            cur = lax.ppermute(cur, ring_axis, ring(size, shift))
            gathered = lax.dynamic_update_index_in_dim(gathered, cur, (here - shift * step) % size, 0)
        outs.append(gathered)
    return jnp.stack(outs).reshape(rows, cols)


def small_tensor_sum(values):
    ny = lax.axis_size("ty")
    nx = lax.axis_size("tx")
    dist = 1
    while dist < ny:
        values = values + lax.ppermute(values, "ty", [(i, i ^ dist) for i in range(ny)])
        dist *= 2
    dist = 1
    while dist < nx:
        values = values + lax.ppermute(values, "tx", [(i, i ^ dist) for i in range(nx)])
        dist *= 2
    return values


def per_device(
    tokens,
    segment_ids,
    attn_gain,
    w_query,
    w_key,
    w_value,
    query_gain,
    key_gain,
    w_out,
    ffn_gain,
    w_gate,
    w_up,
    w_down,
    cotangent,
):
    length = tokens.shape[0]
    head_size = query_gain.shape[0]
    q_heads = w_query.shape[1] // head_size
    kv_heads = w_key.shape[1] // head_size
    groups = q_heads // kv_heads
    factor = 1.0 / math.sqrt(head_size)
    places, allowed = seq_layout(segment_ids)
    cosine, sine_table = rope_tables(places, head_size)
    tokens_wide = tokens.astype(jnp.float32)
    scale_one = rms_scale(tokens_wide)
    normed_one = (tokens_wide * scale_one * attn_gain).astype(jnp.bfloat16)
    q_raw = jnp.dot(normed_one, w_query, preferred_element_type=jnp.float32).reshape(
        length, q_heads, head_size
    )
    k_raw = jnp.dot(normed_one, w_key, preferred_element_type=jnp.float32).reshape(
        length, kv_heads, head_size
    )
    v_half = (
        jnp.dot(normed_one, w_value, preferred_element_type=jnp.float32)
        .astype(jnp.bfloat16)
        .reshape(length, kv_heads, head_size)
    )
    q_scale = rms_scale(q_raw)
    k_scale = rms_scale(k_raw)
    q_hat = q_raw * q_scale
    k_hat = k_raw * k_scale
    q_rot = (
        rotate(q_hat * query_gain, cosine, sine_table)
        .astype(jnp.bfloat16)
        .reshape(length, kv_heads, groups, head_size)
    )
    k_rot = rotate(k_hat * key_gain, cosine, sine_table).astype(jnp.bfloat16)
    scores = score_table(q_rot, k_rot, allowed, factor)
    row_peak = jnp.max(scores, axis=-1, keepdims=True)
    log_total = row_peak + jnp.log(jnp.sum(jnp.exp(scores - row_peak), axis=-1, keepdims=True))
    attn_probs = jnp.exp(scores - log_total).astype(jnp.bfloat16)
    attn_mixed = jnp.einsum(
        "kgij,jkd->ikgd", attn_probs, v_half, preferred_element_type=jnp.float32
    )
    attn_mixed = attn_mixed.reshape(length, q_heads * head_size).astype(jnp.bfloat16)
    attn_sum = split_tensor_sum(jnp.dot(attn_mixed, w_out, preferred_element_type=jnp.float32))
    residual = tokens_wide + attn_sum
    scale_two = rms_scale(residual)
    normed_two = (residual * scale_two * ffn_gain).astype(jnp.bfloat16)
    gate_proj = jnp.dot(normed_two, w_gate, preferred_element_type=jnp.float32)
    up_proj = jnp.dot(normed_two, w_up, preferred_element_type=jnp.float32)
    gate_sigmoid = jax.nn.sigmoid(gate_proj)
    hidden = (gate_proj * gate_sigmoid * up_proj).astype(jnp.bfloat16)
    mlp_sum = tensor_sum(jnp.dot(hidden, w_down, preferred_element_type=jnp.float32))
    output = (residual + mlp_sum).astype(jnp.bfloat16)
    down_grad = outer(hidden, cotangent)
    hidden_grad = inner(cotangent, w_down)
    gate_grad = (
        hidden_grad * up_proj * gate_sigmoid * (1.0 + gate_proj * (1.0 - gate_sigmoid))
    ).astype(jnp.bfloat16)
    up_grad = (hidden_grad * gate_proj * gate_sigmoid).astype(jnp.bfloat16)
    gate_w_grad = outer(normed_two, gate_grad)
    up_w_grad = outer(normed_two, up_grad)
    ffn_w_grads, two_partial = lax.optimization_barrier(
        ((down_grad, gate_w_grad, up_w_grad), inner(gate_grad, w_gate) + inner(up_grad, w_up))
    )
    ffn_w_grads = lax.psum(ffn_w_grads, DP)
    normed_two_grad = tensor_sum(two_partial)
    ffn_grad = jnp.sum(normed_two_grad * residual * scale_two, axis=0)
    residual_grad = cotangent.astype(jnp.float32) + rms_back(
        normed_two_grad, residual, scale_two, ffn_gain
    )
    residual_half = residual_grad.astype(jnp.bfloat16)
    out_w_grad = outer(attn_mixed, residual_half)
    mixed_grad = (
        inner(residual_half, w_out)
        .astype(jnp.bfloat16)
        .reshape(length, kv_heads, groups, head_size)
    )
    attn_full = jnp.exp(score_table(q_rot, k_rot, allowed, factor) - log_total)
    probs_half = attn_full.astype(jnp.bfloat16)
    value_grad = jnp.einsum(
        "kgij,ikgd->jkd", probs_half, mixed_grad, preferred_element_type=jnp.float32
    ).astype(jnp.bfloat16)
    prob_grad = jnp.einsum("ikgd,jkd->kgij", mixed_grad, v_half, preferred_element_type=jnp.float32)
    row_delta = jnp.sum(attn_full * prob_grad, axis=-1, keepdims=True)
    score_grad = (attn_full * (prob_grad - row_delta) * factor).astype(jnp.bfloat16)
    q_rot_grad = jnp.einsum(
        "kgij,jkd->ikgd", score_grad, k_rot, preferred_element_type=jnp.float32
    ).reshape(length, q_heads, head_size)
    k_rot_grad = jnp.einsum("kgij,ikgd->jkd", score_grad, q_rot, preferred_element_type=jnp.float32)
    q_norm_grad = unrotate(q_rot_grad, cosine, sine_table)
    k_norm_grad = unrotate(k_rot_grad, cosine, sine_table)
    qgain_grad = jnp.sum(q_norm_grad * q_hat, axis=(0, 1))
    kgain_grad = jnp.sum(k_norm_grad * k_hat, axis=(0, 1))
    q_grad = (
        rms_back(q_norm_grad, q_raw, q_scale, query_gain)
        .astype(jnp.bfloat16)
        .reshape(length, q_heads * head_size)
    )
    k_grad = (
        rms_back(k_norm_grad, k_raw, k_scale, key_gain)
        .astype(jnp.bfloat16)
        .reshape(length, kv_heads * head_size)
    )
    v_grad = value_grad.reshape(length, kv_heads * head_size)
    query_w_grad = outer(normed_one, q_grad)
    key_w_grad = outer(normed_one, k_grad)
    value_w_grad = outer(normed_one, v_grad)
    one_partial = inner(q_grad, w_query) + inner(k_grad, w_key) + inner(v_grad, w_value)
    attn_part = jnp.sum(one_partial * tokens_wide * scale_one, axis=0)
    width = attn_part.shape[0]
    small = jnp.zeros((8, width), jnp.float32)
    small = small.at[0].set(ffn_grad).at[1].set(attn_part)
    small = small.at[2, :head_size].set(qgain_grad).at[2, head_size : 2 * head_size].set(kgain_grad)
    out_rows = out_w_grad.shape[0]
    ffn_w_grads, dp_sums, one_partial = lax.optimization_barrier(
        (
            ffn_w_grads,
            (query_w_grad, key_w_grad, value_w_grad, jnp.concatenate([out_w_grad, small])),
            one_partial,
        )
    )
    query_w_grad, key_w_grad, value_w_grad, out_pack = dp_sums
    q_cols = query_w_grad.shape[1]
    k_cols = key_w_grad.shape[1]
    width = out_pack.shape[1]
    flat = jnp.concatenate([query_w_grad, key_w_grad, value_w_grad], axis=1).reshape(-1, width)
    flat_rows = flat.shape[0]
    packed = jnp.concatenate([flat, out_pack], axis=0)
    padded_rows = -(-packed.shape[0] // 256) * 256
    packed = jnp.pad(packed, ((0, padded_rows - packed.shape[0]), (0, 0)))
    packed = ring_sum(packed, "dz", ("dc", "dx"))
    flat = packed[:flat_rows].reshape(query_w_grad.shape[0], -1)
    query_w_grad = flat[:, :q_cols]
    key_w_grad = flat[:, q_cols : q_cols + k_cols]
    value_w_grad = flat[:, q_cols + k_cols :]
    out_pack = packed[flat_rows : flat_rows + out_pack.shape[0]]
    down_grad, gate_w_grad, up_w_grad = ffn_w_grads
    normed_one_grad = split_tensor_sum(one_partial)
    input_grad = residual_grad + rms_back(normed_one_grad, tokens_wide, scale_one, attn_gain)
    out_w_grad = out_pack[:out_rows]
    ffn_grad = out_pack[out_rows]
    gains = small_tensor_sum(out_pack[out_rows + 1 : out_rows + 3])
    attn_grad = gains[0]
    qgain_grad = gains[1, :head_size]
    kgain_grad = gains[1, head_size : 2 * head_size]
    return (
        output,
        input_grad,
        attn_grad,
        query_w_grad,
        key_w_grad,
        value_w_grad,
        qgain_grad,
        kgain_grad,
        out_w_grad,
        ffn_grad,
        gate_w_grad,
        up_w_grad,
        down_grad,
    )


def solution(mesh):
    from jax.sharding import Mesh

    dp_size, tensor_size = mesh.devices.shape
    split = Mesh(
        mesh.devices.reshape(2, dp_size // 4, 2, tensor_size // 2, 2), DP + TENSOR
    )
    return jax.shard_map(
        per_device,
        mesh=split,
        in_specs=(
            P(DP, None),
            P(DP),
            P(),
            P(None, TENSOR),
            P(None, TENSOR),
            P(None, TENSOR),
            P(),
            P(),
            P(TENSOR, None),
            P(),
            P(None, TENSOR),
            P(None, TENSOR),
            P(TENSOR, None),
            P(DP, None),
        ),
        out_specs=(
            P(DP, None),
            P(DP, None),
            P(),
            P(None, TENSOR),
            P(None, TENSOR),
            P(None, TENSOR),
            P(),
            P(),
            P(TENSOR, None),
            P(),
            P(None, TENSOR),
            P(None, TENSOR),
            P(TENSOR, None),
        ),
        check_vma=False,
    )
```
